128 devices in a mesh: row: 32 (over z, x, core), col: 4 (over y).
Axes of the slice: x: 4, y: 4, z: 4, core: 2. Of those that a mesh axis runs over, the one named last changes fastest.
Arguments:
- panel: float32 [256, 65536], P('col', 'row'), may hold values from -6 to 6
- cauchy: float32 [256, 256], replicated, may hold values from -1 to 1
- refl_v: float32 [2, 512, 256, 128], P(None, 'row'), may hold values from -1 to 1
- block_start: int32 [2], replicated, may hold values from 0 to 127
Outputs:
- eigvec_out: float32 [256, 65536], P('col', 'row')
The draws below stay inside these ranges and needn't reach their ends.
All inputs are finite; a program needn't handle non-finite values.
Results may differ from the reference program's by a relative error of at most 0.0003.
Values sent between devices are 32-bit elements; how exact they have to be, the bound alone decides.
A program may use at most 128 MiB of HBM per device.

```python
import math
import jax
import jax.numpy as jnp
from jax import lax

HALF_WIDTH = 128
P_SIZE = 256
PASS_TOTAL = 2
N = 65536
PIECES_PER_PASS = 512


def draw_cauchy(key, part):
    seeded_generators = jax.random.split(jax.random.fold_in(key, 23), 4)
    jitter = jax.random.uniform(seeded_generators[0], (P_SIZE,), jnp.float32, -0.3, 0.3)
    pole_set = jnp.arange(P_SIZE, dtype=jnp.float32) + jitter
    spacing = jnp.concatenate([pole_set[1:] - pole_set[:-1], jnp.ones((1,), jnp.float32)])
    fraction = jax.random.uniform(seeded_generators[1], (P_SIZE,), jnp.float32, 0.15, 0.85)
    root_set = pole_set + fraction * spacing
    magnitude = jnp.exp(jax.random.uniform(seeded_generators[2], (P_SIZE,), jnp.float32, math.log(0.3), math.log(3.0)))
    sign_set = jnp.where(jax.random.uniform(seeded_generators[3], (P_SIZE,)) < 0.5, -1.0, 1.0)
    weight = sign_set * magnitude
    entries = weight[:, None] / (pole_set[:, None] - root_set[None, :])
    return entries / jnp.sqrt(jnp.sum(entries * entries, axis=0, keepdims=True))


def draw_refl_v(key, part):
    seeded_generators = jax.random.split(jax.random.fold_in(key, 11), 7)
    gaussian = jax.random.normal(seeded_generators[0], (PASS_TOTAL, PIECES_PER_PASS + 1, HALF_WIDTH, HALF_WIDTH), jnp.float32)
    orthogonal, _ = jnp.linalg.qr(gaussian)
    fast_share = 0.5
    tilt = 0.002
    fast_mode = jax.random.uniform(seeded_generators[1], (PASS_TOTAL, 1, HALF_WIDTH)) < fast_share
    slow_loss = jax.random.uniform(seeded_generators[2], (PASS_TOTAL, 1, HALF_WIDTH), jnp.float32, 0.2, 0.5)
    gradual_preserve = 10.0 ** (-slow_loss / PIECES_PER_PASS)
    quick_location = jax.random.randint(seeded_generators[3], (PASS_TOTAL, 2), 0, PIECES_PER_PASS - 2)
    storage_locations = jnp.arange(PIECES_PER_PASS)
    quick_pairing = jnp.any(storage_locations[None, :, None] == quick_location[:, None, :], axis=2)
    quick_preserve = jax.random.uniform(seeded_generators[4], (PASS_TOTAL, PIECES_PER_PASS, HALF_WIDTH), jnp.float32, 0.7, 0.9)
    gradual_preserve = jnp.where(quick_pairing[:, :, None], gradual_preserve * quick_preserve, gradual_preserve)
    fast_keep = 1.0 - jnp.exp(jax.random.uniform(seeded_generators[5], (PASS_TOTAL, PIECES_PER_PASS, HALF_WIDTH), jnp.float32, math.log(0.02), math.log(0.1)))
    retained = jnp.where(fast_mode, fast_keep, gradual_preserve)
    mode_beta = (1.0 - jnp.sqrt(1.0 - retained * retained)) / retained
    upper_part = orthogonal[:, :PIECES_PER_PASS]
    lower_part = -orthogonal[:, 1:] * mode_beta[:, :, None, :]
    stacked = jnp.concatenate([upper_part, lower_part], axis=2)
    triangle_part = jax.random.uniform(seeded_generators[6], (PASS_TOTAL, PIECES_PER_PASS, HALF_WIDTH, HALF_WIDTH), jnp.float32, -tilt, tilt)
    mixing = jnp.triu(triangle_part, 1) + jnp.eye(HALF_WIDTH, dtype=jnp.float32)
    tilted = jnp.einsum('pgik,pgkj->pgij', stacked, mixing, precision=lax.Precision.HIGHEST)
    return jnp.clip(tilted, -1.0, 1.0)


def levels(own_key, extent, shards, smallest, largest):
    factor_of = 1.0
    for dim, parts in shards:
        steps = jax.random.uniform(jax.random.fold_in(jax.random.fold_in(own_key, 6), dim), (parts,), jnp.float32, smallest / len(shards), largest / len(shards))
        factor_of = factor_of * jnp.repeat(jnp.exp(steps), extent[dim] // parts).reshape((-1,) + (1,) * (len(extent) - 1 - dim))
    return factor_of


def scatter_about(own_key, dims, width, most, pieces=(), held_as=jnp.bfloat16):
    factor_of = levels(own_key, dims, pieces, -0.22, 0.18) if pieces else 1.0
    drawn = jax.random.normal(own_key, dims, jnp.float32) * width * factor_of
    return jnp.minimum(jnp.maximum(drawn, -most), most).astype(held_as)


def setup_inputs(seed: int = 0) -> dict:
    key_of = jax.random.split(jax.random.key(seed), 5)
    panel = scatter_about(key_of[0], (P_SIZE, N), 1.0, 6.0, ((0, 4), (1, 32)), jnp.float32)
    cauchy = draw_cauchy(jax.random.fold_in(key_of[4], 71), 0)
    refl_v = draw_refl_v(jax.random.fold_in(key_of[4], 71), 0)
    block_start = jax.random.randint(key_of[3], (PASS_TOTAL,), 0, HALF_WIDTH).astype(jnp.int32)
    return dict(panel=panel, cauchy=cauchy, refl_v=refl_v, block_start=block_start)


HIGHEST = lax.Precision.HIGHEST

def upper_inverse(gram_matrix):
    identity = jnp.eye(HALF_WIDTH, dtype=jnp.float32)
    halves = 0.5 * jnp.sum(gram_matrix * identity, axis=1)
    nilpotent = jnp.triu(gram_matrix, 1) / halves[:, None]
    power = nilpotent
    result = identity - nilpotent
    reach = 2
    while reach < HALF_WIDTH:
        power = jnp.dot(power.astype(jnp.float32), power.astype(jnp.float32), precision=HIGHEST, preferred_element_type=jnp.float32)
        result = jnp.dot(result.astype(jnp.float32), (identity + power).astype(jnp.float32), precision=HIGHEST, preferred_element_type=jnp.float32)
        reach = reach * 2
    return result / halves[None, :]

def reflector(vblock):
    gram_matrix = jnp.dot(vblock.T.astype(jnp.float32), vblock.astype(jnp.float32), precision=HIGHEST, preferred_element_type=jnp.float32)
    triangle = upper_inverse(gram_matrix)
    return jnp.dot(vblock.astype(jnp.float32), triangle.T.astype(jnp.float32), precision=HIGHEST, preferred_element_type=jnp.float32)

def apply_sweep(current, reflectors, anchor):
    anchor = anchor.astype(jnp.int32)
    segment = lax.dynamic_slice_in_dim(current, anchor, N - HALF_WIDTH, 1)
    segments = segment.reshape(P_SIZE, PIECES_PER_PASS - 1, HALF_WIDTH).transpose(1, 0, 2)

    def advance(moving, inputs):
        vblock, fresh_seg = inputs
        stacked = jnp.concatenate([moving, fresh_seg], axis=1)
        scaled_v = reflector(vblock)
        inner = jnp.dot(stacked.astype(jnp.float32), scaled_v.astype(jnp.float32), precision=HIGHEST, preferred_element_type=jnp.float32)
        mixed_rows = stacked - jnp.dot(inner.astype(jnp.float32), vblock.T.astype(jnp.float32), precision=HIGHEST, preferred_element_type=jnp.float32)
        return (mixed_rows[:, HALF_WIDTH:], mixed_rows[:, :HALF_WIDTH])
    last_carry, outputs = lax.scan(advance, segments[0], (reflectors[:PIECES_PER_PASS - 2], segments[1:]))
    finished = jnp.concatenate([outputs, last_carry[None]], axis=0)
    updated = finished.transpose(1, 0, 2).reshape(P_SIZE, N - HALF_WIDTH)
    return lax.dynamic_update_slice_in_dim(current, updated, anchor, 1)

def reference(panel, cauchy, refl_v, block_start):
    current = jnp.dot(cauchy.T.astype(jnp.float32), panel.astype(jnp.float32), precision=HIGHEST, preferred_element_type=jnp.float32)
    for sweep_turn in range(PASS_TOTAL):
        current = apply_sweep(current, refl_v[sweep_turn], block_start[sweep_turn])
    return current
```

```python
import functools
import jax
import jax.numpy as jnp
from jax import lax
from jax.experimental import pallas as pl
from jax.experimental.pallas import tpu as pltpu
from jax.sharding import PartitionSpec as P

F32 = jnp.float32
BF = jnp.bfloat16
S = 128
MESH = pl.DeviceIdType.MESH
VMEM = pl.BlockSpec(memory_space=pltpu.VMEM)
SMEM = pl.BlockSpec(memory_space=pltpu.SMEM)


def split(x):
    high = x.astype(BF)
    return high, (x - high.astype(F32)).astype(BF)


def dot(a, b):
    return jnp.dot(a, b, preferred_element_type=F32)


def wide(x):
    return jnp.concatenate(split(x), axis=1)


def square(x):
    row = wide(x)
    return jnp.concatenate([row, row], axis=0)


def fold(x):
    return x[:, :S] + x[:, S:]


def mul(a, b_high, b_low):
    high, low = split(a)
    return dot(high, b_high) + (dot(low, b_high) + dot(high, b_low))


def reflectors(blocks):
    row = lax.broadcasted_iota(jnp.int32, (S, S), 0)
    col = lax.broadcasted_iota(jnp.int32, (S, S), 1)
    eye = (row == col).astype(F32)
    turned = [split(v.T) for v in blocks]
    quads = [
        dot(jnp.concatenate(t, axis=0), wide(v)) for t, v in zip(turned, blocks)
    ]
    grams = [fold(q[:S]) + fold(q[S:]) for q in quads]
    scale = [2.0 / jnp.sum(g * eye, axis=0, keepdims=True) for g in grams]
    nil = [jnp.where(row > col, g * s, 0.0) for g, s in zip(grams, scale)]
    result = [eye - x for x in nil]
    power = [fold(dot(wide(x), square(x))) for x in nil]
    for _ in range(5):
        both = [
            fold(dot(wide(jnp.concatenate([p, r], axis=0)), square(p)))
            for p, r in zip(power, result)
        ]
        result = [r + b[S:] for r, b in zip(result, both)]
        power = [b[:S] for b in both]
    result = [r + fold(dot(wide(r), square(p))) for p, r in zip(power, result)]
    scaled = [
        wide(fold(dot(wide(v * s), square(r)))) for v, s, r in zip(blocks, scale, result)
    ]
    return [
        dot(w, jnp.concatenate([t[0], t[0]], axis=0))
        + dot(w, jnp.concatenate([t[1], t[1]], axis=0))
        for w, t in zip(scaled, turned)
    ]


def block_kernel(count, active_ref, v_ref, high_ref, low_ref):
    first = pl.program_id(0) * count
    row = lax.broadcasted_iota(jnp.int32, (2 * S, 2 * S), 0)
    col = lax.broadcasted_iota(jnp.int32, (2 * S, 2 * S), 1)
    eye = (row == col).astype(F32)
    moved = reflectors([v_ref[i] for i in range(count)])
    for i in range(count):
        high, low = split(eye - jnp.where(active_ref[first + i] > 0, moved[i], 0.0))
        high_ref[i] = high
        low_ref[i] = low


def block_matrices(active, v, count):
    total = v.shape[0]
    spec = pl.BlockSpec((count, 2 * S, 2 * S), lambda i: (i, 0, 0))
    shape = jax.ShapeDtypeStruct((total, 2 * S, 2 * S), BF)
    return pl.pallas_call(
        functools.partial(block_kernel, count),
        grid=(total // count,),
        in_specs=[SMEM, pl.BlockSpec((count, 2 * S, S), lambda i: (i, 0, 0))],
        out_specs=[spec, spec],
        out_shape=[shape, shape],
        compiler_params=pltpu.CompilerParams(vmem_limit_bytes=60 * 2**20),
        cost_estimate=pl.CostEstimate(
            flops=total * 1_000_000_000 // 2, bytes_accessed=total * 400_000, transcendentals=0
        ),
        name="blocks",
    )(active, v)


def window(left, right, by):
    lane = lax.broadcasted_iota(jnp.int32, left.shape, 1)
    turn = lax.rem(S - by, S)
    return jnp.where(
        lane < S - by, pltpu.roll(left, turn, 1), pltpu.roll(right, turn, 1)
    )


def sweep_kernel(
    steps, offset_ref, first_ref, cauchy_ref, p0, p1, p2, p3, own_high, own_low, far_high, far_low,
    data_ref, high_ref, low_ref, state_ref, home, mid, carry_one, carry_two,
):
    rows = p0.shape[0]
    pieces = p0.shape[1] // S
    o_one, o_two = offset_ref[0], offset_ref[1]
    is_first = first_ref[0] > 0
    row = lax.broadcasted_iota(jnp.int32, (S, S), 0)
    col = lax.broadcasted_iota(jnp.int32, (S, S), 1)
    eye = (row == col).astype(F32)
    zero_map = jnp.zeros((S, S), F32)

    mix_high, mix_low = split(cauchy_ref[...])
    mix = jnp.concatenate([mix_high, mix_low], axis=0)
    home[0] = jnp.zeros((rows, S), F32)

    def merge(j, _):
        at = pl.ds(pl.multiple_of(j * S, S), S)
        part = jnp.concatenate([p[:, at] for p in (p0, p1, p2, p3)], axis=0)
        high, low = split(part)
        both = dot(mix, jnp.concatenate([high, low], axis=1))
        home[j + 1] = fold(both[:rows]) + fold(both[rows:])
        return 0

    lax.fori_loop(0, pieces, merge, 0)

    def fresh_one(k):
        return window(home[k + 1], home[k + 2], o_one)

    start = jnp.where(is_first, fresh_one(-1), 0.0)
    carry_one[...] = jnp.concatenate([start, eye], axis=0)
    mid[0] = jnp.zeros((rows + S, S), F32)

    def step_one(k, high, low):
        fresh = jnp.concatenate([fresh_one(k + 1), zero_map], axis=0)
        out = mul(jnp.concatenate([carry_one[...], fresh], axis=1), high, low)
        mid[k + 2] = out[:, :S]
        carry_one[...] = out[:, S:]

    step_one(-1, far_high[0], far_low[0])

    def body_one(k, _):
        step_one(k, own_high[k], own_low[k])
        return 0

    lax.fori_loop(0, steps - 1, body_one, 0)
    state_ref[0] = carry_one[rows:]
    state_ref[3, :rows] = carry_one[:rows]
    step_one(steps - 1, own_high[steps - 1], own_low[steps - 1])
    step_one(steps, far_high[2], far_low[2])
    step_one(steps + 1, far_high[3], far_low[3])

    reach = S + o_two - o_one
    jump = reach // S
    by = lax.rem(reach, S)

    def fresh_two(k):
        return window(mid[k + 1 + jump], mid[k + 2 + jump], by)

    head = fresh_two(-1)
    start = jnp.where(is_first, head[:rows], 0.0)
    carry_two[...] = jnp.concatenate([start, zero_map, eye], axis=0)

    def step_two(k, high, low):
        fresh = jnp.concatenate([fresh_two(k + 1), zero_map], axis=0)
        out = mul(jnp.concatenate([carry_two[...], fresh], axis=1), high, low)
        data_ref[k + 1] = out[:rows, :S]
        high, low = split(out[rows:, :S])
        high_ref[k + 1] = high
        low_ref[k + 1] = low
        carry_two[...] = out[:, S:]

    step_two(-1, far_high[1], far_low[1])

    def body_two(k, _):
        step_two(k, own_high[steps + k], own_low[steps + k])
        return 0

    lax.fori_loop(0, steps - 1, body_two, 0)
    state_ref[1] = carry_two[rows : rows + S]
    state_ref[2] = carry_two[rows + S :]
    state_ref[3, rows:] = carry_two[:rows]
    step_two(steps - 1, own_high[2 * steps - 1], own_low[2 * steps - 1])


def sweeps(offsets, first, cauchy, pieces, own, far):
    rows, width = pieces[0].shape
    steps = own[0].shape[0] // 2
    return pl.pallas_call(
        functools.partial(sweep_kernel, steps),
        in_specs=[SMEM, SMEM] + [VMEM] * 9,
        out_specs=[VMEM] * 4,
        out_shape=[
            jax.ShapeDtypeStruct((steps + 1, rows, S), F32),
            jax.ShapeDtypeStruct((steps + 1, 2 * S, S), BF),
            jax.ShapeDtypeStruct((steps + 1, 2 * S, S), BF),
            jax.ShapeDtypeStruct((4, S, S), F32),
        ],
        scratch_shapes=[
            pltpu.VMEM((width // S + 1, rows, S), F32),
            pltpu.VMEM((steps + 5, rows + S, S), F32),
            pltpu.VMEM((rows + S, S), F32),
            pltpu.VMEM((rows + 2 * S, S), F32),
        ],
        compiler_params=pltpu.CompilerParams(vmem_limit_bytes=60 * 2**20),
        name="sweeps",
    )(offsets, first, cauchy, *pieces, *own, *far)


def scan_kernel(group, state_ref, carry_ref, near, total, far, send_sem, near_sem, far_sem):
    me = lax.axis_index("row")
    place = lax.rem(me, group)
    base = me - place
    outer = lax.axis_size("row") // group
    layer = me // group
    half = state_ref.shape[1] // 2
    barrier = pltpu.get_barrier_semaphore()
    for s in range(1, group):
        pl.semaphore_signal(
            barrier, inc=1, device_id={"row": base + lax.rem(place + s, group)}, device_id_type=MESH
        )
    for s in range(1, outer):
        pl.semaphore_signal(
            barrier,
            inc=1,
            device_id={"row": lax.rem(layer + s, outer) * group + place},
            device_id_type=MESH,
        )
    pl.semaphore_wait(barrier, group + outer - 2)

    copies = []
    for s in range(1, group):
        copies.append(
            pltpu.make_async_remote_copy(
                src_ref=state_ref,
                dst_ref=near.at[s],
                send_sem=send_sem.at[s - 1],
                recv_sem=near_sem.at[s],
                device_id={"row": base + lax.rem(place + s, group)},
                device_id_type=MESH,
            )
        )
        copies[-1].start()
    near[0] = state_ref[...]
    for copy in copies:
        copy.wait()

    def load(ref, at):
        first = jnp.concatenate([ref[at, 0], ref[at, 1]], axis=1)
        second = jnp.concatenate([jnp.zeros((S, S), F32), ref[at, 2]], axis=1)
        offset = jnp.concatenate([ref[at, 3, :half], ref[at, 3, half:]], axis=1)
        return jnp.concatenate([first, second], axis=0), offset

    def slot(j):
        return lax.rem(place - j + group, group)

    matrix, offset = load(near, slot(0))
    zero = jnp.zeros((half, 2 * S), F32)
    row = lax.broadcasted_iota(jnp.int32, (2 * S, 2 * S), 0)
    col = lax.broadcasted_iota(jnp.int32, (2 * S, 2 * S), 1)
    eye = (row == col).astype(F32)
    so_far = jnp.concatenate([matrix, offset], axis=0)
    mine = jnp.where(
        place > 0, so_far, jnp.concatenate([eye, zero], axis=0)
    )

    def join(j, both):
        so_far, mine = both
        matrix, offset = load(near, slot(j))
        longer = mul(so_far, *split(matrix))
        so_far = jnp.concatenate([longer[: 2 * S], longer[2 * S :] + offset], axis=0)
        return so_far, jnp.where(j < place, so_far, mine)

    so_far, mine = lax.fori_loop(1, group, join, (so_far, mine))
    total[0] = so_far[:S, :S]
    total[1] = so_far[:S, S:]
    total[2] = so_far[S : 2 * S, S:]
    total[3, :half] = so_far[2 * S :, :S]
    total[3, half:] = so_far[2 * S :, S:]

    copies = []
    for s in range(1, outer):
        copies.append(
            pltpu.make_async_remote_copy(
                src_ref=total,
                dst_ref=far.at[s],
                send_sem=send_sem.at[group - 2 + s],
                recv_sem=far_sem.at[s],
                device_id={"row": lax.rem(layer + s, outer) * group + place},
                device_id_type=MESH,
            )
        )
        copies[-1].start()
    far[0] = total[...]
    for copy in copies:
        copy.wait()

    carry = zero
    for z in range(outer - 1):
        matrix, offset = load(far, lax.rem(layer - z + outer, outer))
        longer = mul(carry, *split(matrix)) + offset
        carry = jnp.where(z < layer, longer, carry)
    carry_ref[...] = mul(carry, *split(mine[: 2 * S])) + mine[2 * S :]


def scan(state, half):
    group, outer = 8, lax.axis_size("row") // 8
    return pl.pallas_call(
        functools.partial(scan_kernel, group),
        in_specs=[VMEM],
        out_specs=VMEM,
        out_shape=jax.ShapeDtypeStruct((half, 2 * S), F32),
        scratch_shapes=[
            pltpu.VMEM((group,) + state.shape, F32),
            pltpu.VMEM(state.shape, F32),
            pltpu.VMEM((outer,) + state.shape, F32),
            pltpu.SemaphoreType.DMA((group + outer - 2,)),
            pltpu.SemaphoreType.DMA((group,)),
            pltpu.SemaphoreType.DMA((outer,)),
        ],
        compiler_params=pltpu.CompilerParams(
            collective_id=0, has_side_effects=True, vmem_limit_bytes=40 * 2**20
        ),
        name="scan",
    )(state)


def finish_kernel(offset_ref, carry_ref, data_ref, high_ref, low_ref, out_ref, aligned):
    count, rows, _ = data_ref.shape
    high, low = split(carry_ref[...])
    both = jnp.concatenate([high, low], axis=0)
    for j in range(count):
        near = dot(both, high_ref[j])
        aligned[j] = data_ref[j] + (near[:rows] + (near[rows:] + dot(high, low_ref[j])))
    reach = S - offset_ref[1]
    jump = reach // S
    by = lax.rem(reach, S)
    for j in range(count - 1):
        out_ref[:, j * S : (j + 1) * S] = window(aligned[j + jump], aligned[j + jump + 1], by)


def finish(offsets, carry, data, high, low):
    count, rows, _ = data.shape
    return pl.pallas_call(
        finish_kernel,
        in_specs=[SMEM] + [VMEM] * 4,
        out_specs=VMEM,
        out_shape=jax.ShapeDtypeStruct((rows, (count - 1) * S), F32),
        scratch_shapes=[pltpu.VMEM((count + 1, rows, S), F32)],
        name="finish",
    )(offsets, carry, data, high, low)


def shifted(array, axis, by, wrap):
    size = lax.axis_size(axis)
    pairs = [(i, (i + by) % size) for i in range(size) if wrap or 0 <= i + by < size]
    return lax.ppermute(array, axis, pairs)


def shards(panel, cauchy, refl_v, block_start):
    rows = panel.shape[0]
    steps = refl_v.shape[1]
    me, slabs = lax.axis_index("row"), lax.axis_size("row")
    col, cols = lax.axis_index("col"), lax.axis_size("col")

    before = shifted(refl_v[:, steps - 1], "row", 1, False)
    after = shifted(refl_v[0, :2], "row", -1, False)
    margin = shifted(panel[:, : 4 * S], "row", -1, False)
    panel = jnp.concatenate([panel, margin], axis=1)
    pieces = [panel] + [shifted(panel, "col", s, True) for s in range(1, cols)]
    order = [lax.rem(col - s + cols, cols) for s in range(cols)]
    mine = lax.dynamic_slice_in_dim(cauchy, col * rows, rows, 1).T
    mix = jnp.concatenate(
        [lax.dynamic_slice_in_dim(mine, at * rows, rows, 1) for at in order], axis=1
    )

    last = slabs * steps - 3
    slot = me * steps + lax.iota(jnp.int32, steps)
    own_on = jnp.tile((slot <= last).astype(jnp.int32), 2)
    far_at = me * steps + jnp.array([-1, -1, steps, steps + 1], jnp.int32)
    far_on = ((far_at >= 0) & (far_at <= last)).astype(jnp.int32)
    own = block_matrices(own_on, refl_v.reshape(2 * steps, 2 * S, S), 8)
    far = block_matrices(far_on, jnp.concatenate([before, after], axis=0), 4)
    first = (me == 0).astype(jnp.int32).reshape(1)
    data, high, low, state = sweeps(block_start, first, mix, pieces, own, far)
    carry = scan(state, rows)
    return finish(block_start, carry, data, high, low)


def solution(mesh):
    placed = (P("col", "row"), P(), P(None, "row", None, None), P())
    return jax.shard_map(
        shards, mesh=mesh, in_specs=placed, out_specs=P("col", "row"), check_vma=False
    )
```

```python
import functools
import jax
import jax.numpy as jnp
from jax import lax
from jax.experimental import pallas as pl
from jax.experimental.pallas import tpu as pltpu
from jax.sharding import PartitionSpec as P

F32 = jnp.float32
BF = jnp.bfloat16
S = 128
MESH = pl.DeviceIdType.MESH
VMEM = pl.BlockSpec(memory_space=pltpu.VMEM)
SMEM = pl.BlockSpec(memory_space=pltpu.SMEM)
ANY = pl.BlockSpec(memory_space=pl.ANY)


def split(x):
    high = x.astype(BF)
    return high, (x - high.astype(F32)).astype(BF)


def dot(a, b):
    return jnp.dot(a, b, preferred_element_type=F32)


def wide(x):
    return jnp.concatenate(split(x), axis=1)


def square(x):
    row = wide(x)
    return jnp.concatenate([row, row], axis=0)


def fold(x):
    return x[:, :S] + x[:, S:]


def mul(a, b_high, b_low):
    high, low = split(a)
    return dot(high, b_high) + (dot(low, b_high) + dot(high, b_low))


def lanes(rows, size):
    lane = lax.broadcasted_iota(jnp.int32, (rows, S), 1) // size
    return [(lane == b).astype(F32) for b in range(S // size)]


def spread(x, masks, at):
    high, low = split(x)
    zero = jnp.zeros(high.shape, BF)
    rows = []
    for b in range(len(masks)):
        if at[b] is None:
            rows.append(jnp.concatenate([zero, zero], axis=1))
        else:
            mask = masks[at[b]]
            rows.append(jnp.concatenate([high * mask, low * mask], axis=1))
    top = jnp.concatenate(rows, axis=0)
    return jnp.concatenate([top, top], axis=0)


def unit_inverses(nils):
    f4, f2 = lanes(32, 32), lanes(64, 64)
    b4, b2 = [m.astype(BF) for m in f4], [m.astype(BF) for m in f2]
    row = lax.broadcasted_iota(jnp.int32, (32, S), 0)
    lane = lax.broadcasted_iota(jnp.int32, (32, S), 1)
    eye = (row == lax.rem(lane, 32)).astype(F32)
    diag4, diag2 = [0, 1, 2, 3], [0, 1]

    def pick(n, size, masks, at):
        part = None
        for b, mask in zip(at, masks):
            piece = n[b * size : (b + 1) * size] * mask
            part = piece if part is None else part + piece
        return part

    small = [pick(n, 32, f4, diag4) for n in nils]
    result = [eye - c for c in small]
    power = [fold(dot(wide(c), spread(c, b4, diag4))) for c in small]
    for _ in range(3):
        both = [
            fold(dot(wide(jnp.concatenate([p, r], axis=0)), spread(p, b4, diag4)))
            for p, r in zip(power, result)
        ]
        result = [r + b[32:] for r, b in zip(result, both)]
        power = [b[:32] for b in both]
    result = [r + fold(dot(wide(r), spread(p, b4, diag4))) for p, r in zip(power, result)]

    under = [pick(n, 32, [f4[0], f4[2]], [1, 3]) for n in nils]
    inner = [fold(dot(wide(u), spread(r, b4, diag4))) for u, r in zip(under, result)]
    outer = [
        fold(dot(wide(r), spread(t, b4, [None, 0, None, 2]))) for r, t in zip(result, inner)
    ]
    result = [
        jnp.concatenate([r * (f4[0] + f4[2]), r * (f4[1] + f4[3]) - o], axis=0)
        for r, o in zip(result, outer)
    ]
    under = [n[64:] * f2[0] for n in nils]
    inner = [fold(dot(wide(u), spread(r, b2, diag2))) for u, r in zip(under, result)]
    outer = [fold(dot(wide(r), spread(t, b2, [None, 0]))) for r, t in zip(result, inner)]
    return [
        jnp.concatenate([r * f2[0], r * f2[1] - o], axis=0) for r, o in zip(result, outer)
    ]


def reflectors(blocks):
    row = lax.broadcasted_iota(jnp.int32, (S, S), 0)
    col = lax.broadcasted_iota(jnp.int32, (S, S), 1)
    eye = (row == col).astype(F32)
    turned = [split(v.T) for v in blocks]
    quads = [dot(t[0], wide(v)) for t, v in zip(turned, blocks)]
    grams = [fold(q) + q[:, S:].T for q in quads]
    scale = [2.0 / jnp.sum(g * eye, axis=0, keepdims=True) for g in grams]
    nils = [jnp.where(row > col, g * s, 0.0) for g, s in zip(grams, scale)]
    result = unit_inverses(nils)
    scaled = [
        wide(fold(dot(wide(v * s), square(r)))) for v, s, r in zip(blocks, scale, result)
    ]
    return [
        dot(w, jnp.concatenate([t[0], t[0]], axis=0))
        + dot(w, jnp.concatenate([t[1], t[1]], axis=0))
        for w, t in zip(scaled, turned)
    ]


def window(left, right, by):
    lane = lax.broadcasted_iota(jnp.int32, left.shape, 1)
    turn = lax.rem(S - by, S)
    return jnp.where(
        lane < S - by, pltpu.roll(left, turn, 1), pltpu.roll(right, turn, 1)
    )


def kernel(
    inner, offset_ref, panel_ref, cauchy_ref, v_ref, out_ref,
    v_all, k_high, k_low, panels, turned, home, mid_map, mid_data, z_high, z_low, aligned,
    map_one, map_two, data_one, data_two,
    pair_m, chip_m, chips_m, layer_m, layers_m, own_b, pair_b, chip_b, chips_b, layer_b, layers_b,
    own_m, load_sem, ring_send, ring_sem, halo_send, halo_sem, scan_send, scan_sem,
):
    me, slabs = lax.axis_index("row"), lax.axis_size("row")
    col, cols = lax.axis_index("col"), lax.axis_size("col")
    steps = v_ref.shape[1]
    rows = panel_ref.shape[0]
    half = rows // 2
    group = 2 * inner
    outer = slabs // group
    core = lax.rem(me, 2)
    chip = lax.rem(me // 2, inner)
    layer = me // group
    right, left = lax.rem(col + 1, cols), lax.rem(col + cols - 1, cols)
    after, before = lax.rem(me + 1, slabs), lax.rem(me + slabs - 1, slabs)
    partner = me + 1 - 2 * core
    near = [layer * group + lax.rem(chip + s, inner) * 2 + core for s in range(1, inner)]
    apart = [lax.rem(me + s * group, slabs) for s in range(1, outer)]

    loads = []
    for i in range(4):
        sweep, at = i // 2, (i % 2) * (steps // 2)
        loads.append(
            pltpu.make_async_copy(
                v_ref.at[sweep, pl.ds(at, steps // 2)],
                v_all.at[pl.ds(1 + sweep * (steps + 3) + at, steps // 2)],
                load_sem.at[i],
            )
        )
    loads.append(pltpu.make_async_copy(panel_ref, panels.at[col], load_sem.at[4]))
    for copy in loads:
        copy.start()

    barrier = pltpu.get_barrier_semaphore()
    for peer in (right, left):
        pl.semaphore_signal(barrier, inc=1, device_id={"col": peer}, device_id_type=MESH)
    for peer in [after, before, partner] + near + apart:
        pl.semaphore_signal(barrier, inc=1, device_id={"row": peer}, device_id_type=MESH)
    pl.semaphore_wait(barrier, 5 + len(near) + len(apart))

    def send(source, target, send_sem, recv_sem, device):
        return pltpu.make_async_remote_copy(
            src_ref=source, dst_ref=target, send_sem=send_sem, recv_sem=recv_sem,
            device_id=device, device_id_type=MESH,
        )

    halos = [
        send(v_ref.at[0, steps - 1], v_all.at[0], halo_send.at[0], halo_sem.at[0], {"row": after}),
        send(v_ref.at[1, steps - 1], v_all.at[steps + 3], halo_send.at[1], halo_sem.at[1], {"row": after}),
        send(v_ref.at[0, pl.ds(0, 2)], v_all.at[pl.ds(steps + 1, 2)], halo_send.at[2], halo_sem.at[2], {"row": before}),
    ]
    for copy in halos:
        copy.start()

    top, low_half = pl.ds(0, half), pl.ds(half, half)

    def ring(i, slot, part, peer, source=None):
        return send(
            panels.at[slot, part] if source is None else source,
            panels.at[slot, part], ring_send.at[i], ring_sem.at[i], {"col": peer},
        )

    first_ring = [
        ring(0, col, top, right, panel_ref.at[top]),
        ring(1, col, low_half, left, panel_ref.at[low_half]),
        ring(2, col, low_half, right, panel_ref.at[low_half]),
        ring(3, col, top, left, panel_ref.at[top]),
    ]
    for copy in first_ring:
        copy.start()
    second_ring = [ring(4, left, top, right), ring(5, right, low_half, left)]

    last = slabs * steps - 3
    row = lax.broadcasted_iota(jnp.int32, (2 * S, 2 * S), 0)
    colm = lax.broadcasted_iota(jnp.int32, (2 * S, 2 * S), 1)
    eye2 = (row == colm).astype(F32)

    def form(spots, slots):
        moved = reflectors([v_all[at] for at in spots])
        for at, slot, x in zip(spots, slots, moved):
            active = (slot >= 0) & (slot <= last)
            high, low = split(eye2 - jnp.where(active, x, 0.0))
            k_high[at] = high
            k_low[at] = low

    for copy in loads[:4]:
        copy.wait()

    def tick(t, _):
        at = 1 + 8 * t + 3 * (t // (steps // 8))
        k = lax.rem(t, steps // 8) * 8
        form([at + i for i in range(8)], [me * steps + k + i for i in range(8)])

        @pl.when(t == 2)
        def _():
            first_ring[0].wait_recv()
            second_ring[0].start()
            first_ring[1].wait_recv()
            second_ring[1].start()

        return 0

    lax.fori_loop(0, steps // 4, tick, 0)
    for copy in halos:
        copy.wait()
    form(
        [0, steps + 1, steps + 2, steps + 3],
        [me * steps - 1, me * steps + steps, me * steps + steps + 1, me * steps - 1],
    )

    o_one, o_two = offset_ref[0], offset_ref[1]
    reach = S + o_two - o_one
    jump = reach // S
    by = lax.rem(reach, S)
    eye = eye2[:S, :S]
    zero = jnp.zeros((S, S), F32)
    map_one[...] = eye
    map_two[...] = jnp.concatenate([zero, eye], axis=0)
    mid_map[0] = zero

    def map_step_one(k):
        high, low = k_high[k + 1, :S], k_low[k + 1, :S]
        out = mul(map_one[...], high, low)
        mid_map[k + 2] = out[:, :S]
        map_one[...] = out[:, S:]

    def map_step_two(k):
        fresh = window(mid_map[k + 2 + jump], mid_map[k + 3 + jump], by)
        x = jnp.concatenate([map_two[...], jnp.concatenate([fresh, zero], axis=0)], axis=1)
        out = mul(x, k_high[k + steps + 4], k_low[k + steps + 4])
        high, low = split(out[:, :S])
        z_high[k + 1] = high
        z_low[k + 1] = low
        map_two[...] = out[:, S:]

    def waves(one, two, save_one, save_two):
        for k in range(-1, 2):
            one(k)

        def both(k, _):
            one(k)
            two(k - 3)
            return 0

        lax.fori_loop(2, steps - 1, both, 0)
        save_one()
        lax.fori_loop(steps - 1, steps + 2, both, 0)
        save_two()
        two(steps - 1)

    def save_map_one():
        own_m[0] = map_one[...]

    def save_map_two():
        own_m[1] = map_two[:S]
        own_m[2] = map_two[S:]

    waves(map_step_one, map_step_two, save_map_one, save_map_two)

    def matrix(ref):
        high0, low0 = split(jnp.concatenate([ref[0], ref[1]], axis=1))
        high1, low1 = split(jnp.concatenate([zero, ref[2]], axis=1))
        return jnp.concatenate([high0, high1], axis=0), jnp.concatenate([low0, low1], axis=0)

    def whole(ref):
        return jnp.concatenate(
            [jnp.concatenate([ref[0], ref[1]], axis=1), jnp.concatenate([zero, ref[2]], axis=1)], axis=0
        )

    def keep(ref, x):
        ref[0] = x[:S, :S]
        ref[1] = x[:S, S:]
        ref[2] = x[S:, S:]

    pair = send(own_m, pair_m, scan_send.at[0], scan_sem.at[0], {"row": partner})
    pair.start()

    turned[...] = cauchy_ref[...].T
    loads[4].wait()
    for copy in first_ring[2:]:
        copy.wait_recv()
    for copy in second_ring:
        copy.wait_recv()
    mix_high, mix_low = split(turned[pl.ds(pl.multiple_of(col * rows, rows), rows)])
    mix = jnp.concatenate([mix_high, mix_low], axis=0)
    home[0] = jnp.zeros((rows, S), F32)

    def merge(j, _):
        at = pl.ds(pl.multiple_of(j * S, S), S)
        part = jnp.concatenate([panels[c, :, at] for c in range(cols)], axis=0)
        both = dot(mix, wide(part))
        home[j + 1] = fold(both[:rows]) + fold(both[rows:])
        return 0

    lax.fori_loop(0, 4, merge, 0)
    margin = send(
        home.at[pl.ds(1, 4)], home.at[pl.ds(steps + 1, 4)], halo_send.at[3], halo_sem.at[3], {"row": before}
    )
    margin.start()
    lax.fori_loop(4, steps, merge, 0)

    pair.wait()
    on_first = core == 0
    first_m = jnp.where(on_first, whole(own_m), whole(pair_m))
    second_m = jnp.where(on_first, whole(pair_m), whole(own_m))
    keep(chip_m, mul(first_m, *split(second_m)))
    chip_sends = []
    for s in range(1, inner):
        chip_sends.append(
            send(chip_m, chips_m.at[chip], scan_send.at[s], scan_sem.at[s], {"row": near[s - 1]})
        )
        chip_sends[-1].start()
    chips_m[chip] = chip_m[...]
    margin.wait()

    def fresh_one(k):
        return window(home[k + 1], home[k + 2], o_one)

    is_first = me == 0
    data_one[...] = jnp.where(is_first, fresh_one(-1), 0.0)
    mid_data[0] = jnp.zeros((rows, S), F32)

    def data_step_one(k):
        x = jnp.concatenate([data_one[...], fresh_one(k + 1)], axis=1)
        out = mul(x, k_high[k + 1], k_low[k + 1])
        mid_data[k + 2] = out[:, :S]
        data_one[...] = out[:, S:]

    def fresh_two(k):
        return window(mid_data[k + 1 + jump], mid_data[k + 2 + jump], by)

    def data_step_two(k):
        carried = data_two[...]
        if not isinstance(k, int):
            carried = jnp.where(is_first & (k == -1), fresh_two(-1), carried)
        x = jnp.concatenate([carried, fresh_two(k + 1)], axis=1)
        out = mul(x, k_high[k + steps + 4], k_low[k + steps + 4])
        aligned[k + 1] = out[:, :S]
        data_two[...] = out[:, S:]

    data_two[...] = jnp.zeros((rows, S), F32)

    def save_data_one():
        own_b[:, :S] = data_one[...]

    def save_data_two():
        own_b[:, S:] = data_two[...]

    waves(data_step_one, data_step_two, save_data_one, save_data_two)

    pair = send(own_b, pair_b, scan_send.at[inner], scan_sem.at[inner], {"row": partner})
    pair.start()

    for copy in chip_sends:
        copy.wait()
    total = whole(chips_m.at[0])
    lead = eye2
    for j in range(1, inner):
        lead = jnp.where(chip == j, total, lead)
        total = mul(total, *matrix(chips_m.at[j]))
    keep(layer_m, total)
    at = inner + 1
    layer_sends = []
    for s in range(1, outer):
        layer_sends.append(
            send(layer_m, layers_m.at[layer], scan_send.at[at], scan_sem.at[at], {"row": apart[s - 1]})
        )
        layer_sends[-1].start()
        at += 1
    layers_m[layer] = layer_m[...]

    pair.wait()
    first_b = jnp.where(on_first, own_b[...], pair_b[...])
    second_b = jnp.where(on_first, pair_b[...], own_b[...])
    chip_b[...] = mul(first_b, *split(second_m)) + second_b
    chip_sends = []
    for s in range(1, inner):
        chip_sends.append(
            send(chip_b, chips_b.at[chip], scan_send.at[at], scan_sem.at[at], {"row": near[s - 1]})
        )
        chip_sends[-1].start()
        at += 1
    chips_b[chip] = chip_b[...]
    lead_m = jnp.where(on_first, lead, mul(lead, *split(first_m)))
    for copy in chip_sends:
        copy.wait()
    total_b = chips_b[0]
    lead_b = jnp.zeros((rows, 2 * S), F32)
    for j in range(1, inner):
        lead_b = jnp.where(chip == j, total_b, lead_b)
        total_b = mul(total_b, *matrix(chips_m.at[j])) + chips_b[j]
    layer_b[...] = total_b
    last_sends = []
    for s in range(1, outer):
        last_sends.append(
            send(layer_b, layers_b.at[layer], scan_send.at[at], scan_sem.at[at], {"row": apart[s - 1]})
        )
        last_sends[-1].start()
        at += 1
    layers_b[layer] = layer_b[...]
    lead_b = jnp.where(on_first, lead_b, mul(lead_b, *split(first_m)) + first_b)
    for copy in layer_sends:
        copy.wait()
    for copy in last_sends:
        copy.wait()
    carry = jnp.zeros((rows, 2 * S), F32)
    for z in range(outer - 1):
        longer = mul(carry, *matrix(layers_m.at[z])) + layers_b[z]
        carry = jnp.where(z < layer, longer, carry)
    carry = mul(carry, *split(lead_m)) + lead_b

    high, low = split(carry)
    both = jnp.concatenate([high, low], axis=0)
    for j in range(steps + 1):
        part = dot(both, z_high[j])
        aligned[j] = aligned[j] + (part[:rows] + (part[rows:] + dot(high, z_low[j])))
    reach_out = S - o_two
    jump_out = reach_out // S
    by_out = lax.rem(reach_out, S)
    for j in range(steps):
        out_ref[:, j * S : (j + 1) * S] = window(
            aligned[j + jump_out], aligned[j + jump_out + 1], by_out
        )
    for copy in first_ring + second_ring:
        copy.wait_send()


def shards(panel, cauchy, refl_v, block_start):
    rows, width = panel.shape
    steps = refl_v.shape[1]
    cols, slabs = lax.axis_size("col"), lax.axis_size("row")
    inner = 4
    outer = slabs // (2 * inner)
    count = 2 * steps + 4
    scan_copies = 2 + 2 * (inner - 1) + 2 * (outer - 1)

    def f(*shape):
        return pltpu.VMEM(shape, F32)

    def b(*shape):
        return pltpu.VMEM(shape, BF)

    dma = pltpu.SemaphoreType.DMA
    return pl.pallas_call(
        functools.partial(kernel, inner),
        in_specs=[SMEM, ANY, VMEM, ANY],
        out_specs=VMEM,
        out_shape=jax.ShapeDtypeStruct((rows, width), F32),
        scratch_shapes=[
            f(count, 2 * S, S), b(count, 2 * S, 2 * S), b(count, 2 * S, 2 * S),
            f(cols, rows, width), f(2 * S, 2 * S), f(steps + 5, rows, S),
            f(steps + 5, S, S), f(steps + 5, rows, S),
            b(steps + 1, 2 * S, S), b(steps + 1, 2 * S, S), f(steps + 2, rows, S),
            f(S, S), f(2 * S, S), f(rows, S), f(rows, S),
            f(3, S, S), f(3, S, S), f(inner, 3, S, S), f(3, S, S), f(outer, 3, S, S),
            f(rows, 2 * S), f(rows, 2 * S), f(rows, 2 * S), f(inner, rows, 2 * S),
            f(rows, 2 * S), f(outer, rows, 2 * S), f(3, S, S),
            dma((5,)), dma((6,)), dma((6,)), dma((4,)), dma((4,)),
            dma((scan_copies,)), dma((scan_copies,)),
        ],
        compiler_params=pltpu.CompilerParams(
            collective_id=0, has_side_effects=True, vmem_limit_bytes=60 * 2**20
        ),
        name="back_transform",
    )(block_start, panel, cauchy, refl_v)


def solution(mesh):
    placed = (P("col", "row"), P(), P(None, "row", None, None), P())
    return jax.shard_map(
        shards, mesh=mesh, in_specs=placed, out_specs=P("col", "row"), check_vma=False
    )
```

```python
import functools
import jax
import jax.numpy as jnp
from jax import lax
from jax.experimental import pallas as pl
from jax.experimental.pallas import tpu as pltpu
from jax.sharding import PartitionSpec as P

F32 = jnp.float32
BF = jnp.bfloat16
S = 128
MESH = pl.DeviceIdType.MESH
VMEM = pl.BlockSpec(memory_space=pltpu.VMEM)
SMEM = pl.BlockSpec(memory_space=pltpu.SMEM)
ANY = pl.BlockSpec(memory_space=pl.ANY)


def split(x):
    high = x.astype(BF)
    return high, (x - high.astype(F32)).astype(BF)


def dot(a, b):
    return jnp.dot(a, b, preferred_element_type=F32)


def dot_t(a, b):
    return lax.dot_general(a, b, (((1,), (1,)), ((), ())), preferred_element_type=F32)


def wide(x):
    return jnp.concatenate(split(x), axis=1)


def square(x):
    row = wide(x)
    return jnp.concatenate([row, row], axis=0)


def fold(x):
    return x[:, :S] + x[:, S:]


def mul(a, b_high, b_low):
    high, low = split(a)
    return dot(
        jnp.concatenate([high, low, high], axis=1), jnp.concatenate([b_high, b_high, b_low], axis=0)
    )


def lanes(rows, size):
    lane = lax.broadcasted_iota(jnp.int32, (rows, S), 1) // size
    return [(lane == b).astype(F32) for b in range(S // size)]


def spread(x, masks, at):
    high, low = split(x)
    zero = jnp.zeros(high.shape, BF)
    rows = []
    for b in range(len(masks)):
        if at[b] is None:
            rows.append(jnp.concatenate([zero, zero], axis=1))
        else:
            mask = masks[at[b]]
            rows.append(jnp.concatenate([high * mask, low * mask], axis=1))
    top = jnp.concatenate(rows, axis=0)
    return jnp.concatenate([top, top], axis=0)


def unit_inverses(nils):
    f4, f2 = lanes(32, 32), lanes(64, 64)
    b4, b2 = [m.astype(BF) for m in f4], [m.astype(BF) for m in f2]
    row = lax.broadcasted_iota(jnp.int32, (32, S), 0)
    lane = lax.broadcasted_iota(jnp.int32, (32, S), 1)
    eye = (row == lax.rem(lane, 32)).astype(F32)
    diag4, diag2 = [0, 1, 2, 3], [0, 1]

    def pick(n, size, masks, at):
        part = None
        for b, mask in zip(at, masks):
            piece = n[b * size : (b + 1) * size] * mask
            part = piece if part is None else part + piece
        return part

    small = [pick(n, 32, f4, diag4) for n in nils]
    result = [eye - c for c in small]
    power = [fold(dot(wide(c), spread(c, b4, diag4))) for c in small]
    yield
    for _ in range(3):
        both = [
            fold(dot(wide(jnp.concatenate([p, r], axis=0)), spread(p, b4, diag4)))
            for p, r in zip(power, result)
        ]
        result = [r + b[32:] for r, b in zip(result, both)]
        power = [b[:32] for b in both]
        yield
    result = [r + fold(dot(wide(r), spread(p, b4, diag4))) for p, r in zip(power, result)]
    yield

    under = [pick(n, 32, [f4[0], f4[2]], [1, 3]) for n in nils]
    inner = [fold(dot(wide(u), spread(r, b4, diag4))) for u, r in zip(under, result)]
    yield
    outer = [
        fold(dot(wide(r), spread(t, b4, [None, 0, None, 2]))) for r, t in zip(result, inner)
    ]
    result = [
        jnp.concatenate([r * (f4[0] + f4[2]), r * (f4[1] + f4[3]) - o], axis=0)
        for r, o in zip(result, outer)
    ]
    yield
    under = [n[64:] * f2[0] for n in nils]
    inner = [fold(dot(wide(u), spread(r, b2, diag2))) for u, r in zip(under, result)]
    yield
    outer = [fold(dot(wide(r), spread(t, b2, [None, 0]))) for r, t in zip(result, inner)]
    return [
        jnp.concatenate([r * f2[0], r * f2[1] - o], axis=0) for r, o in zip(result, outer)
    ]


def prepare(blocks, active):
    row = lax.broadcasted_iota(jnp.int32, (S, S), 0)
    col = lax.broadcasted_iota(jnp.int32, (S, S), 1)
    eye = (row == col).astype(F32)
    quads = [dot(v.T.astype(BF), wide(v)) for v in blocks]
    yield
    grams = [fold(q) + q[:, S:].T for q in quads]
    scale = [
        jnp.where(on, -2.0 / jnp.sum(g * eye, axis=0, keepdims=True), 0.0)
        for g, on in zip(grams, active)
    ]
    nils = [jnp.where(row > col, g * -s, 0.0) for g, s in zip(grams, scale)]
    yield
    result = yield from unit_inverses(nils)
    return scale, result


def less(v, scale, result):
    high, low = split(fold(dot(wide(v * scale), square(result))))
    v_high, v_low = split(v)
    both = jnp.concatenate([high, low], axis=1)
    return dot_t(both, jnp.concatenate([v_high, v_high], axis=1)) + dot_t(high, v_low)


def window(left, right, by):
    lane = lax.broadcasted_iota(jnp.int32, left.shape, 1)
    turn = lax.rem(S - by, S)
    return jnp.where(
        lane < S - by, pltpu.roll(left, turn, 1), pltpu.roll(right, turn, 1)
    )


def kernel(
    inner, offset_ref, panel_ref, cauchy_ref, v_ref, out_ref,
    v_all, k_high, k_low, panels, turned, home, mid_map, mid_data, z_high, z_low, aligned,
    map_one, map_two, data_one, data_two,
    pair_m, chip_m, chips_m, layer_m, layers_m, own_b, pair_b, chip_b, chips_b, layer_b, layers_b,
    own_m, ready_s, ready_r, load_sem, ring_send, ring_sem, halo_send, halo_sem, scan_send, scan_sem,
):
    me, slabs = lax.axis_index("row"), lax.axis_size("row")
    col, cols = lax.axis_index("col"), lax.axis_size("col")
    steps = v_ref.shape[1]
    rows = panel_ref.shape[0]
    half = rows // 2
    group = 2 * inner
    outer = slabs // group
    core = lax.rem(me, 2)
    chip = lax.rem(me // 2, inner)
    layer = me // group
    right, left = lax.rem(col + 1, cols), lax.rem(col + cols - 1, cols)
    after, before = lax.rem(me + 1, slabs), lax.rem(me + slabs - 1, slabs)
    partner = me + 1 - 2 * core
    near = [layer * group + lax.rem(chip + s, inner) * 2 + core for s in range(1, inner)]
    apart = [lax.rem(me + s * group, slabs) for s in range(1, outer)]

    loads = []
    for i in range(4):
        sweep, at = i // 2, (i % 2) * (steps // 2)
        loads.append(
            pltpu.make_async_copy(
                v_ref.at[sweep, pl.ds(at, steps // 2)],
                v_all.at[pl.ds(1 + sweep * (steps + 3) + at, steps // 2)],
                load_sem.at[i],
            )
        )
    loads.append(pltpu.make_async_copy(panel_ref, panels.at[col], load_sem.at[4]))
    loads[0].start()

    barrier = pltpu.get_barrier_semaphore()
    for peer in (right, left):
        pl.semaphore_signal(barrier, inc=1, device_id={"col": peer}, device_id_type=MESH)
    for peer in [after, before, partner] + near + apart:
        pl.semaphore_signal(barrier, inc=1, device_id={"row": peer}, device_id_type=MESH)

    def send(source, target, send_sem, recv_sem, device):
        return pltpu.make_async_remote_copy(
            src_ref=source, dst_ref=target, send_sem=send_sem, recv_sem=recv_sem,
            device_id=device, device_id_type=MESH,
        )

    halos = [
        send(v_ref.at[0, steps - 1], v_all.at[0], halo_send.at[0], halo_sem.at[0], {"row": after}),
        send(v_ref.at[1, steps - 1], v_all.at[steps + 3], halo_send.at[1], halo_sem.at[1], {"row": after}),
        send(v_ref.at[0, pl.ds(0, 2)], v_all.at[pl.ds(steps + 1, 2)], halo_send.at[2], halo_sem.at[2], {"row": before}),
    ]

    class Ring:
        def __init__(self, source, slots, place, size, axis, peer, parts, send_sem, recv_sem, base):
            ahead, behind = lax.rem(place + 1, size), lax.rem(place + size - 1, size)
            up, down = {axis: peer(ahead)}, {axis: peer(behind)}
            one, two = parts
            sems = iter(range(base, base + 6))

            def copy(slot, part, device, own):
                i = next(sems)
                target = slots.at[(slot, *part)]
                return send(source.at[part] if own else target, target, send_sem.at[i], recv_sem.at[i], device)

            self.first = [
                copy(place, one, up, True), copy(place, two, down, True),
                copy(place, two, up, True), copy(place, one, down, True),
            ]
            self.second = [copy(behind, one, up, False), copy(ahead, two, down, False)]

        def start(self):
            for copy in self.first:
                copy.start()

        def forward(self):
            for arrived, onward in zip(self.first, self.second):
                arrived.wait_recv()
                onward.start()

        def arrive(self):
            for copy in self.first[2:] + self.second:
                copy.wait_recv()

        def finish(self):
            for copy in self.first + self.second:
                copy.wait_send()

    class SplitRing(Ring):
        def __init__(self, source, slots, place, size, axis, peer, send_sem, recv_sem, base):
            at, quarter = core * (S // 2), S // 4
            parts = [(slice(None), pl.ds(pl.multiple_of(at + i * quarter, quarter), quarter)) for i in range(2)]
            super().__init__(source, slots, place, size, axis, peer, parts, send_sem, recv_sem, base)
            rows_here = pl.ds(pl.multiple_of(at, S // 2), S // 2)
            self.swaps = []
            for i, shift in enumerate((size - 1, 1, 2)):
                ref = slots.at[lax.rem(place + shift, size), :, rows_here]
                self.swaps.append(
                    send(ref, ref, send_sem.at[base + 6 + i], recv_sem.at[base + 6 + i], {"row": partner})
                )

        def swap_near(self):
            for copy, swap in zip(self.first[2:], self.swaps):
                copy.wait_recv()
                swap.start()

        def swap_far(self):
            for copy in self.second:
                copy.wait_recv()
            self.swaps[2].start()

        def arrive(self):
            for swap in self.swaps:
                swap.wait_recv()

        def finish(self):
            for copy in self.first + self.second + self.swaps:
                copy.wait_send()

    class Direct:
        def __init__(self, source, slots, place, size, axis, peer, send_sem, recv_sem, base):
            mine = pl.ds(pl.multiple_of(core * half, half), half)
            to = [{axis: peer(lax.rem(place + shift, size))} for shift in (2, 1, size - 1)]
            refs = [(source.at[mine], slots.at[place, mine])] + [(source, slots.at[place])] * 2
            self.copies = [
                send(*ref, send_sem.at[base + i], recv_sem.at[base + i], device)
                for i, (ref, device) in enumerate(zip(refs, to))
            ]
            ref = slots.at[lax.rem(place + 2, size), mine]
            self.swap = send(ref, ref, send_sem.at[base + 3], recv_sem.at[base + 3], {"row": partner})

        def start(self):
            for copy in self.copies:
                copy.start()

        def relay(self):
            self.copies[0].wait_recv()
            self.swap.start()

        def arrive(self):
            for copy in [*self.copies[1:], self.swap]:
                copy.wait_recv()

        def finish(self):
            for copy in [*self.copies, self.swap]:
                copy.wait_send()

    flat = [(pl.ds(i * half, half),) for i in range(2)]
    width = panel_ref.shape[1] // 2
    panel_rings = []
    for i in range(2):
        parts = [(*rows_of, pl.ds(i * width, width)) for rows_of in flat]
        panel_rings.append(
            Ring(panel_ref, panels, col, cols, "col", lambda c: c, parts, ring_send, ring_sem, 6 * i)
        )
    in_layer = dict(place=chip, size=inner, axis="row", peer=lambda x: layer * group + 2 * x + core)
    over_layers = dict(place=layer, size=outer, axis="row", peer=lambda z: z * group + 2 * chip + core)

    scan_sems = dict(send_sem=scan_send, recv_sem=scan_sem)
    chip_ring_m = SplitRing(chip_m, chips_m, base=2, **in_layer, **scan_sems)
    layer_ring_m = SplitRing(layer_m, layers_m, base=11, **over_layers, **scan_sems)
    chip_ring_b = Direct(chip_b, chips_b, base=20, **in_layer, **scan_sems)
    layer_ring_b = Direct(layer_b, layers_b, base=24, **over_layers, **scan_sems)

    last = slabs * steps - 3
    row = lax.broadcasted_iota(jnp.int32, (2 * S, 2 * S), 0)
    colm = lax.broadcasted_iota(jnp.int32, (2 * S, 2 * S), 1)
    eye2 = (row == colm).astype(F32)

    def is_on(slot):
        return (slot >= 0) & (slot <= last)

    def begin(batch, filler):
        stages = prepare([v_all[at] for at, _ in batch], [is_on(slot) for _, slot in batch])
        share = -(-len(filler) // 9)
        filler = list(filler)
        while True:
            try:
                next(stages)
            except StopIteration as done:
                scale, result = done.value
                break
            for piece in filler[:share]:
                piece()
            filler = filler[share:]
        for piece in filler:
            piece()
        for i in range(len(batch)):
            ready_s[i] = jnp.broadcast_to(scale[i], (8, S))
            ready_r[i] = result[i]

    def end(i, at):
        x = less(v_all[at], ready_s[i, :1], ready_r[i])
        for r in range(2):
            for c in range(2):
                here = pl.ds(r * S, S), pl.ds(c * S, S)
                part = x[r * S : (r + 1) * S, c * S : (c + 1) * S]
                high, low = split(eye2[:S, :S] + part if r == c else part)
                k_high[(at, *here)] = high
                k_low[(at, *here)] = low

    def ends(batch):
        return [functools.partial(end, i, at) for i, (at, _) in enumerate(batch)]

    first_slot = me * steps

    def batch_of(t):
        at, slot = 1 + 8 * t + 3 * (t // (steps // 8)), first_slot + lax.rem(t, steps // 8) * 8
        return [(at + i, slot + i) for i in range(8)]

    seam = [(0, first_slot - 1), (steps + 3, first_slot - 1)]
    seam += [(steps + 1, first_slot + steps), (steps + 2, first_slot + steps + 1)]

    o_one, o_two = offset_ref[0], offset_ref[1]
    reach = S + o_two - o_one
    jump = reach // S
    by = lax.rem(reach, S)
    eye = eye2[:S, :S]
    zero = jnp.zeros((S, S), F32)
    map_one[...] = eye
    map_two[...] = jnp.concatenate([zero, eye], axis=0)
    mid_map[0] = zero

    def map_step_one(k):
        out = mul(map_one[...], k_high[k + 1, :S], k_low[k + 1, :S])
        mid_map[k + 2] = out[:, :S]
        map_one[...] = out[:, S:]

    def map_step_two(k):
        fresh = window(mid_map[k + 2 + jump], mid_map[k + 3 + jump], by)
        at = k + steps + 4
        x = jnp.concatenate([map_two[...], jnp.concatenate([fresh, zero], axis=0)], axis=1)
        out = mul(x, k_high[at], k_low[at])
        z_high[k + 1], z_low[k + 1] = split(out[:, :S])
        map_two[...] = out[:, S:]

    def wave(k, one, two, save_one, save_two):
        if k < steps + 2:
            one(k)
        if k > 1:
            two(k - 3)
        if k == steps - 2:
            save_one()
        if k == steps + 1:
            save_two()

    def save_map_one():
        own_m[0] = map_one[...]

    def save_map_two():
        own_m[1] = map_two[:S]
        own_m[2] = map_two[S:]

    def map_waves(ks):
        return [functools.partial(wave, k, map_step_one, map_step_two, save_map_one, save_map_two) for k in ks]

    def mixed(some, others):
        out = []
        while some or others:
            out += some[:1] + others[:1]
            some, others = some[1:], others[1:]
        return out

    def enter():
        pl.semaphore_wait(barrier, 5 + len(near) + len(apart))
        for copy in halos:
            copy.start()
        panel_rings[0].start()

    loads[0].wait()
    for copy in loads[1:]:
        copy.start()
    begin(batch_of(0), [])
    enter()
    for copy in loads[1:4]:
        copy.wait()

    def tick(t, _):
        @pl.when(t == 3)
        def _():
            panel_rings[0].forward()
            panel_rings[1].start()

        begin(batch_of(t), ends(batch_of(t - 1)))
        return 0

    lax.fori_loop(1, steps // 4, tick, 0)
    for copy in halos:
        copy.wait()
    begin(seam, ends(batch_of(steps // 4 - 1)))
    turned[...] = cauchy_ref[...].T
    mix_high, mix_low = split(turned[pl.ds(pl.multiple_of(col * rows, rows), rows)])
    mix = jnp.concatenate([mix_high, mix_low], axis=0)
    home[0] = jnp.zeros((rows, S), F32)

    def merge(j, _):
        at = pl.ds(pl.multiple_of(j * S, S), S)
        part = jnp.concatenate([panels[c, :, at] for c in range(cols)], axis=0)
        both = dot(mix, wide(part))
        home[j + 1] = fold(both[:rows]) + fold(both[rows:])
        return 0

    margin = send(
        home.at[pl.ds(1, 4)], home.at[pl.ds(steps + 1, 4)], halo_send.at[3], halo_sem.at[3], {"row": before}
    )

    def merge_first():
        loads[4].wait()
        panel_rings[0].arrive()
        lax.fori_loop(0, steps // 2, merge, 0, unroll=4)

        @pl.when(me > 0)
        def _():
            margin.start()

        @pl.when(me == slabs - 1)
        def _():
            home[pl.ds(steps + 1, 4)] = jnp.zeros((4, rows, S), F32)


    for piece in ends(seam):
        piece()
    merge_first()
    for piece in map_waves(range(-1, 9)):
        piece()
    panel_rings[1].forward()
    for piece in map_waves(range(9, steps + 3)):
        piece()

    def matrix(ref):
        high0, low0 = split(jnp.concatenate([ref[0], ref[1]], axis=1))
        high1, low1 = split(jnp.concatenate([zero, ref[2]], axis=1))
        return jnp.concatenate([high0, high1], axis=0), jnp.concatenate([low0, low1], axis=0)

    def whole(ref):
        return jnp.concatenate(
            [jnp.concatenate([ref[0], ref[1]], axis=1), jnp.concatenate([zero, ref[2]], axis=1)], axis=0
        )

    def keep(ref, x):
        ref[0] = x[:S, :S]
        ref[1] = x[:S, S:]
        ref[2] = x[S:, S:]

    pair = send(own_m, pair_m, scan_send.at[0], scan_sem.at[0], {"row": partner})
    pair.start()

    pair.wait()
    on_first = core == 0
    first_m = jnp.where(on_first, whole(own_m), whole(pair_m))
    second_m = jnp.where(on_first, whole(pair_m), whole(own_m))
    keep(chip_m, mul(first_m, *split(second_m)))
    chip_ring_m.start()
    chips_m[chip] = chip_m[...]

    def fresh_one(k):
        return window(home[k + 1], home[k + 2], o_one)

    is_first = me == 0
    data_one[...] = jnp.where(is_first, fresh_one(-1), 0.0)
    mid_data[0] = jnp.zeros((rows, S), F32)

    def data_step_one(k):
        x = jnp.concatenate([data_one[...], fresh_one(k + 1)], axis=1)
        out = mul(x, k_high[k + 1], k_low[k + 1])
        mid_data[k + 2] = out[:, :S]
        data_one[...] = out[:, S:]

    def fresh_two(k):
        return window(mid_data[k + 1 + jump], mid_data[k + 2 + jump], by)

    def data_step_two(k):
        carried = data_two[...] if k >= 0 else jnp.where(is_first, fresh_two(-1), 0.0)
        x = jnp.concatenate([carried, fresh_two(k + 1)], axis=1)
        out = mul(x, k_high[k + steps + 4], k_low[k + steps + 4])
        aligned[k + 1] = out[:, :S]
        data_two[...] = out[:, S:]


    def save_data_one():
        own_b[:, :S] = data_one[...]

    def save_data_two():
        own_b[:, S:] = data_two[...]

    def merge_second():
        panel_rings[1].arrive()
        lax.fori_loop(steps // 2, steps, merge, 0, unroll=4)

    def take_margin():
        @pl.when(me < slabs - 1)
        def _():
            margin.wait_recv()

    also = {
        4: merge_second, 7: chip_ring_m.forward, 11: chip_ring_m.swap_near, steps - 2: take_margin,
        steps + 1: chip_ring_m.swap_far,
    }
    for k in range(-1, steps + 3):
        if k in also:
            also[k]()
        wave(k, data_step_one, data_step_two, save_data_one, save_data_two)

    pair = send(own_b, pair_b, scan_send.at[1], scan_sem.at[1], {"row": partner})
    pair.start()

    chip_ring_m.arrive()
    total = whole(chips_m.at[0])
    lead = eye2
    for j in range(1, inner):
        lead = jnp.where(chip == j, total, lead)
        total = mul(total, *matrix(chips_m.at[j]))
    keep(layer_m, total)
    layer_ring_m.start()
    layers_m[layer] = layer_m[...]

    pair.wait()
    first_b = jnp.where(on_first, own_b[...], pair_b[...])
    second_b = jnp.where(on_first, pair_b[...], own_b[...])
    chip_b[...] = mul(first_b, *split(second_m)) + second_b
    chip_ring_b.start()
    chips_b[chip] = chip_b[...]
    lead_m = jnp.where(on_first, lead, mul(lead, *split(first_m)))
    chip_ring_b.relay()
    layer_ring_m.forward()
    layer_ring_m.swap_near()
    chip_ring_b.arrive()
    total_b = chips_b[0]
    lead_b = jnp.zeros((rows, 2 * S), F32)
    for j in range(1, inner):
        lead_b = jnp.where(chip == j, total_b, lead_b)
        total_b = mul(total_b, *matrix(chips_m.at[j])) + chips_b[j]
    layer_b[...] = total_b
    layer_ring_b.start()
    layers_b[layer] = layer_b[...]
    lead_b = jnp.where(on_first, lead_b, mul(lead_b, *split(first_m)) + first_b)
    layer_ring_m.swap_far()
    layer_ring_b.relay()
    layer_ring_m.arrive()
    layer_ring_b.arrive()
    carry = jnp.zeros((rows, 2 * S), F32)
    for z in range(outer - 1):
        longer = mul(carry, *matrix(layers_m.at[z])) + layers_b[z]
        carry = jnp.where(z < layer, longer, carry)
    carry = mul(carry, *split(lead_m)) + lead_b

    high, low = split(carry)
    both = jnp.concatenate([high, low], axis=0)
    for j in range(steps + 1):
        part = dot(both, z_high[j])
        aligned[j] = aligned[j] + (part[:rows] + (part[rows:] + dot(high, z_low[j])))
    reach_out = S - o_two
    jump_out = reach_out // S
    by_out = lax.rem(reach_out, S)
    for j in range(steps):
        out_ref[:, j * S : (j + 1) * S] = window(
            aligned[j + jump_out], aligned[j + jump_out + 1], by_out
        )
    for ring in (*panel_rings, chip_ring_m, chip_ring_b, layer_ring_m, layer_ring_b):
        ring.finish()

    @pl.when(me > 0)
    def _():
        margin.wait_send()


def shards(panel, cauchy, refl_v, block_start):
    rows, width = panel.shape
    steps = refl_v.shape[1]
    cols, slabs = lax.axis_size("col"), lax.axis_size("row")
    inner = 4
    outer = slabs // (2 * inner)
    count = 2 * steps + 4
    scan_copies = 2 + 2 * 9 + 2 * 4

    def f(*shape):
        return pltpu.VMEM(shape, F32)

    def b(*shape):
        return pltpu.VMEM(shape, BF)

    dma = pltpu.SemaphoreType.DMA
    return pl.pallas_call(
        functools.partial(kernel, inner),
        in_specs=[SMEM, ANY, VMEM, ANY],
        out_specs=VMEM,
        out_shape=jax.ShapeDtypeStruct((rows, width), F32),
        scratch_shapes=[
            f(count, 2 * S, S), b(count, 2 * S, 2 * S), b(count, 2 * S, 2 * S),
            f(cols, rows, width), f(2 * S, 2 * S), f(steps + 5, rows, S),
            f(steps + 5, S, S), f(steps + 5, rows, S),
            b(steps + 1, 2 * S, S), b(steps + 1, 2 * S, S), f(steps + 2, rows, S),
            f(S, S), f(2 * S, S), f(rows, S), f(rows, S),
            f(3, S, S), f(3, S, S), f(inner, 3, S, S), f(3, S, S), f(outer, 3, S, S),
            f(rows, 2 * S), f(rows, 2 * S), f(rows, 2 * S), f(inner, rows, 2 * S),
            f(rows, 2 * S), f(outer, rows, 2 * S), f(3, S, S),
            f(8, 8, S), f(8, S, S),
            dma((5,)), dma((12,)), dma((12,)), dma((4,)), dma((4,)),
            dma((scan_copies,)), dma((scan_copies,)),
        ],
        compiler_params=pltpu.CompilerParams(
            collective_id=0, has_side_effects=True, vmem_limit_bytes=60 * 2**20
        ),
        name="back_transform",
    )(block_start, panel, cauchy, refl_v)


def solution(mesh):
    placed = (P("col", "row"), P(), P(None, "row", None, None), P())
    return jax.shard_map(
        shards, mesh=mesh, in_specs=placed, out_specs=P("col", "row"), check_vma=False
    )
```

```python
import functools
import jax
import jax.numpy as jnp
from jax import lax
from jax.experimental import pallas as pl
from jax.experimental.pallas import tpu as pltpu
from jax.sharding import PartitionSpec as P

F32 = jnp.float32
BF = jnp.bfloat16
S = 128
MESH = pl.DeviceIdType.MESH
VMEM = pl.BlockSpec(memory_space=pltpu.VMEM)
SMEM = pl.BlockSpec(memory_space=pltpu.SMEM)
HBM = pl.BlockSpec(memory_space=pltpu.HBM)


def split(x):
    high = x.astype(BF)
    return high, (x - high.astype(F32)).astype(BF)


def dot(a, b):
    return jnp.dot(a, b, preferred_element_type=F32)


def dot_t(a, b):
    return lax.dot_general(a, b, (((1,), (1,)), ((), ())), preferred_element_type=F32)


def wide(x):
    return jnp.concatenate(split(x), axis=1)


def square(x):
    row = wide(x)
    return jnp.concatenate([row, row], axis=0)


def fold(x):
    return x[:, :S] + x[:, S:]


def mul(a, b_high, b_low):
    high, low = split(a)
    return dot(
        jnp.concatenate([high, low, high], axis=1), jnp.concatenate([b_high, b_high, b_low], axis=0)
    )


def lanes(rows, size):
    lane = lax.broadcasted_iota(jnp.int32, (rows, S), 1) // size
    return [(lane == b).astype(F32) for b in range(S // size)]


def spread(x, masks, at):
    high, low = split(x)
    zero = jnp.zeros(high.shape, BF)
    rows = []
    for b in range(len(masks)):
        if at[b] is None:
            rows.append(jnp.concatenate([zero, zero], axis=1))
        else:
            mask = masks[at[b]]
            rows.append(jnp.concatenate([high * mask, low * mask], axis=1))
    top = jnp.concatenate(rows, axis=0)
    return jnp.concatenate([top, top], axis=0)


def unit_inverses(nils):
    f4, f2 = lanes(32, 32), lanes(64, 64)
    b4, b2 = [m.astype(BF) for m in f4], [m.astype(BF) for m in f2]
    row = lax.broadcasted_iota(jnp.int32, (32, S), 0)
    lane = lax.broadcasted_iota(jnp.int32, (32, S), 1)
    eye = (row == lax.rem(lane, 32)).astype(F32)
    diag4, diag2 = [0, 1, 2, 3], [0, 1]

    def pick(n, size, masks, at):
        part = None
        for b, mask in zip(at, masks):
            piece = n[b * size : (b + 1) * size] * mask
            part = piece if part is None else part + piece
        return part

    small = [pick(n, 32, f4, diag4) for n in nils]
    result = [eye - c for c in small]
    power = [fold(dot(wide(c), spread(c, b4, diag4))) for c in small]
    yield
    for _ in range(3):
        both = [
            fold(dot(wide(jnp.concatenate([p, r], axis=0)), spread(p, b4, diag4)))
            for p, r in zip(power, result)
        ]
        result = [r + b[32:] for r, b in zip(result, both)]
        power = [b[:32] for b in both]
        yield
    result = [r + fold(dot(wide(r), spread(p, b4, diag4))) for p, r in zip(power, result)]
    yield

    under = [pick(n, 32, [f4[0], f4[2]], [1, 3]) for n in nils]
    inner = [fold(dot(wide(u), spread(r, b4, diag4))) for u, r in zip(under, result)]
    yield
    outer = [
        fold(dot(wide(r), spread(t, b4, [None, 0, None, 2]))) for r, t in zip(result, inner)
    ]
    result = [
        jnp.concatenate([r * (f4[0] + f4[2]), r * (f4[1] + f4[3]) - o], axis=0)
        for r, o in zip(result, outer)
    ]
    yield
    under = [n[64:] * f2[0] for n in nils]
    inner = [fold(dot(wide(u), spread(r, b2, diag2))) for u, r in zip(under, result)]
    yield
    outer = [fold(dot(wide(r), spread(t, b2, [None, 0]))) for r, t in zip(result, inner)]
    return [
        jnp.concatenate([r * f2[0], r * f2[1] - o], axis=0) for r, o in zip(result, outer)
    ]


def prepare(blocks, active):
    row = lax.broadcasted_iota(jnp.int32, (S, S), 0)
    col = lax.broadcasted_iota(jnp.int32, (S, S), 1)
    eye = (row == col).astype(F32)
    quads = [dot(v.T.astype(BF), wide(v)) for v in blocks]
    yield
    grams = [fold(q) + q[:, S:].T for q in quads]
    scale = [
        jnp.where(on, -2.0 / jnp.sum(g * eye, axis=0, keepdims=True), 0.0)
        for g, on in zip(grams, active)
    ]
    nils = [jnp.where(row > col, g * -s, 0.0) for g, s in zip(grams, scale)]
    yield
    result = yield from unit_inverses(nils)
    return scale, result


def less(v, scale, result):
    high, low = split(fold(dot(wide(v * scale), square(result))))
    v_high, v_low = split(v)
    both = jnp.concatenate([high, low], axis=1)
    return dot_t(both, jnp.concatenate([v_high, v_high], axis=1)) + dot_t(high, v_low)


def window(left, right, by):
    lane = lax.broadcasted_iota(jnp.int32, left.shape, 1)
    turn = lax.rem(S - by, S)
    return jnp.where(
        lane < S - by, pltpu.roll(left, turn, 1), pltpu.roll(right, turn, 1)
    )


def kernel(
    inner, offset_ref, panel_ref, cauchy_ref, v_ref, out_ref,
    v_all, k_high, k_low, panels, mixing, turned, home, mid_map, mid_data, z_all, z_high, z_low, aligned, y_home,
    map_one, map_two, data_one, data_two,
    pair_m, chip_m, chips_m, layer_m, layers_m, own_b, pair_b, chip_b, chips_b, layer_b, layers_b,
    own_m, ready_s, ready_r, load_sem, ring_send, ring_sem, halo_send, halo_sem, scan_send, scan_sem,
):
    me, slabs = lax.axis_index("row"), lax.axis_size("row")
    col, cols = lax.axis_index("col"), lax.axis_size("col")
    steps = v_ref.shape[1]
    rows = panel_ref.shape[0]
    half = rows // 2
    group = 2 * inner
    outer = slabs // group
    core = lax.rem(me, 2)
    chip = lax.rem(me // 2, inner)
    layer = me // group
    right, left = lax.rem(col + 1, cols), lax.rem(col + cols - 1, cols)
    after, before = lax.rem(me + 1, slabs), lax.rem(me + slabs - 1, slabs)
    partner = me + 1 - 2 * core
    near = [layer * group + lax.rem(chip + s, inner) * 2 + core for s in range(1, inner)]
    apart = [lax.rem(me + s * group, slabs) for s in range(1, outer)]

    loads = []
    for i in range(4):
        sweep, at = i // 2, (i % 2) * (steps // 2)
        loads.append(
            pltpu.make_async_copy(
                v_ref.at[sweep, pl.ds(at, steps // 2)],
                v_all.at[pl.ds(1 + sweep * (steps + 3) + at, steps // 2)],
                load_sem.at[i],
            )
        )
    loads.append(pltpu.make_async_copy(panel_ref, panels.at[col], load_sem.at[4]))
    loads.append(pltpu.make_async_copy(cauchy_ref, mixing, load_sem.at[5]))
    loads[0].start()

    barrier = pltpu.get_barrier_semaphore()
    for peer in (right, left):
        pl.semaphore_signal(barrier, inc=1, device_id={"col": peer}, device_id_type=MESH)
    for peer in [after, before, partner] + near + apart:
        pl.semaphore_signal(barrier, inc=1, device_id={"row": peer}, device_id_type=MESH)

    def send(source, target, send_sem, recv_sem, device):
        return pltpu.make_async_remote_copy(
            src_ref=source, dst_ref=target, send_sem=send_sem, recv_sem=recv_sem,
            device_id=device, device_id_type=MESH,
        )

    halos = [
        send(v_ref.at[0, steps - 1], v_all.at[0], halo_send.at[0], halo_sem.at[0], {"row": after}),
        send(v_ref.at[1, steps - 1], v_all.at[steps + 3], halo_send.at[1], halo_sem.at[1], {"row": after}),
        send(v_ref.at[0, pl.ds(0, 2)], v_all.at[pl.ds(steps + 1, 2)], halo_send.at[2], halo_sem.at[2], {"row": before}),
    ]

    class Ring:
        def __init__(self, source, slots, place, size, axis, peer, parts, send_sem, recv_sem, base):
            ahead, behind = lax.rem(place + 1, size), lax.rem(place + size - 1, size)
            up, down = {axis: peer(ahead)}, {axis: peer(behind)}
            one, two = parts
            sems = iter(range(base, base + 6))

            def copy(slot, part, device, own):
                i = next(sems)
                target = slots.at[(slot, *part)]
                return send(source.at[part] if own else target, target, send_sem.at[i], recv_sem.at[i], device)

            self.first = [
                copy(place, one, up, True), copy(place, two, down, True),
                copy(place, two, up, True), copy(place, one, down, True),
            ]
            self.second = [copy(behind, one, up, False), copy(ahead, two, down, False)]

        def start(self):
            for copy in self.first:
                copy.start()

        def forward(self):
            for arrived, onward in zip(self.first, self.second):
                arrived.wait_recv()
                onward.start()

        def arrive(self):
            for copy in self.first[2:] + self.second:
                copy.wait_recv()

        def finish(self):
            for copy in self.first + self.second:
                copy.wait_send()

    class SplitRing(Ring):
        def __init__(self, source, slots, place, size, axis, peer, send_sem, recv_sem, base):
            at, quarter = core * (S // 2), S // 4
            parts = [(slice(None), pl.ds(pl.multiple_of(at + i * quarter, quarter), quarter)) for i in range(2)]
            super().__init__(source, slots, place, size, axis, peer, parts, send_sem, recv_sem, base)
            rows_here = pl.ds(pl.multiple_of(at, S // 2), S // 2)
            self.swaps = []
            for i, shift in enumerate((size - 1, 1, 2)):
                ref = slots.at[lax.rem(place + shift, size), :, rows_here]
                self.swaps.append(
                    send(ref, ref, send_sem.at[base + 6 + i], recv_sem.at[base + 6 + i], {"row": partner})
                )

        def swap_near(self):
            for copy, swap in zip(self.first[2:], self.swaps):
                copy.wait_recv()
                swap.start()

        def swap_far(self):
            for copy in self.second:
                copy.wait_recv()
            self.swaps[2].start()

        def arrive(self):
            for swap in self.swaps:
                swap.wait_recv()

        def finish(self):
            for copy in self.first + self.second + self.swaps:
                copy.wait_send()

    class Direct:
        def __init__(self, source, slots, place, size, axis, peer, send_sem, recv_sem, base):
            mine = pl.ds(pl.multiple_of(core * half, half), half)
            to = [{axis: peer(lax.rem(place + shift, size))} for shift in (2, 1, size - 1)]
            refs = [(source.at[mine], slots.at[place, mine])] + [(source, slots.at[place])] * 2
            self.copies = [
                send(*ref, send_sem.at[base + i], recv_sem.at[base + i], device)
                for i, (ref, device) in enumerate(zip(refs, to))
            ]
            ref = slots.at[lax.rem(place + 2, size), mine]
            self.swap = send(ref, ref, send_sem.at[base + 3], recv_sem.at[base + 3], {"row": partner})

        def start(self):
            for copy in self.copies:
                copy.start()

        def relay(self):
            self.copies[0].wait_recv()
            self.swap.start()

        def arrive(self):
            for copy in [*self.copies[1:], self.swap]:
                copy.wait_recv()

        def finish(self):
            for copy in [*self.copies, self.swap]:
                copy.wait_send()

    flat = [(pl.ds(i * half, half),) for i in range(2)]
    width = panel_ref.shape[1] // 2
    panel_rings = []
    for i in range(2):
        parts = [(*rows_of, pl.ds(i * width, width)) for rows_of in flat]
        panel_rings.append(
            Ring(panel_ref, panels, col, cols, "col", lambda c: c, parts, ring_send, ring_sem, 6 * i)
        )
    in_layer = dict(place=chip, size=inner, axis="row", peer=lambda x: layer * group + 2 * x + core)
    over_layers = dict(place=layer, size=outer, axis="row", peer=lambda z: z * group + 2 * chip + core)

    scan_sems = dict(send_sem=scan_send, recv_sem=scan_sem)
    chip_ring_m = SplitRing(chip_m, chips_m, base=2, **in_layer, **scan_sems)
    layer_ring_m = SplitRing(layer_m, layers_m, base=11, **over_layers, **scan_sems)
    chip_ring_b = Direct(chip_b, chips_b, base=20, **in_layer, **scan_sems)
    layer_ring_b = Direct(layer_b, layers_b, base=24, **over_layers, **scan_sems)

    last = slabs * steps - 3
    row = lax.broadcasted_iota(jnp.int32, (2 * S, 2 * S), 0)
    colm = lax.broadcasted_iota(jnp.int32, (2 * S, 2 * S), 1)
    eye2 = (row == colm).astype(F32)

    def is_on(slot):
        return (slot >= 0) & (slot <= last)

    def begin(batch, filler):
        stages = prepare([v_all[at] for at, _ in batch], [is_on(slot) for _, slot in batch])
        share = -(-len(filler) // 9)
        filler = list(filler)
        while True:
            try:
                next(stages)
            except StopIteration as done:
                scale, result = done.value
                break
            for piece in filler[:share]:
                piece()
            filler = filler[share:]
        for piece in filler:
            piece()
        for i in range(len(batch)):
            ready_s[i] = jnp.broadcast_to(scale[i], (8, S))
            ready_r[i] = result[i]

    def end(i, at):
        x = less(v_all[at], ready_s[i, :1], ready_r[i])
        for r in range(2):
            for c in range(2):
                here = pl.ds(r * S, S), pl.ds(c * S, S)
                part = x[r * S : (r + 1) * S, c * S : (c + 1) * S]
                high, low = split(eye2[:S, :S] + part if r == c else part)
                k_high[(at, *here)] = high
                k_low[(at, *here)] = low

    def ends(batch):
        return [functools.partial(end, i, at) for i, (at, _) in enumerate(batch)]

    first_slot = me * steps

    def batch_of(t):
        at, slot = 1 + 8 * t + 3 * (t // (steps // 8)), first_slot + lax.rem(t, steps // 8) * 8
        return [(at + i, slot + i) for i in range(8)]

    seam = [(0, first_slot - 1), (steps + 3, first_slot - 1)]
    seam += [(steps + 1, first_slot + steps), (steps + 2, first_slot + steps + 1)]

    o_one, o_two = offset_ref[0], offset_ref[1]
    reach = S + o_two - o_one
    jump = reach // S
    by = lax.rem(reach, S)
    eye = eye2[:S, :S]
    zero = jnp.zeros((S, S), F32)
    map_one[...] = eye
    map_two[...] = jnp.concatenate([zero, eye], axis=0)
    mid_map[0] = zero

    def map_step_one(k):
        out = mul(map_one[...], k_high[k + 1, :S], k_low[k + 1, :S])
        mid_map[k + 2] = out[:, :S]
        map_one[...] = out[:, S:]

    def map_step_two(k):
        fresh = window(mid_map[k + 2 + jump], mid_map[k + 3 + jump], by)
        at = k + steps + 4
        x = jnp.concatenate([map_two[...], jnp.concatenate([fresh, zero], axis=0)], axis=1)
        out = mul(x, k_high[at], k_low[at])
        z_all[k + 1] = out[:, :S]
        map_two[...] = out[:, S:]

    def wave(k, one, two, save_one, save_two):
        if k < steps + 2:
            one(k)
        if k > 1:
            two(k - 3)
        if k == steps - 2:
            save_one()
        if k == steps + 1:
            save_two()

    def save_map_one():
        own_m[0] = map_one[...]

    def save_map_two():
        own_m[1] = map_two[:S]
        own_m[2] = map_two[S:]

    def map_waves(ks):
        return [functools.partial(wave, k, map_step_one, map_step_two, save_map_one, save_map_two) for k in ks]

    def mixed(some, others):
        out = []
        while some or others:
            out += some[:1] + others[:1]
            some, others = some[1:], others[1:]
        return out

    def enter():
        pl.semaphore_wait(barrier, 5 + len(near) + len(apart))
        for copy in halos:
            copy.start()
        panel_rings[0].start()

    loads[0].wait()
    for copy in loads[1:]:
        copy.start()
    begin(batch_of(0), [])
    enter()
    for copy in loads[1:4]:
        copy.wait()

    def tick(t, _):
        @pl.when(t == 3)
        def _():
            panel_rings[0].forward()
            panel_rings[1].start()

        begin(batch_of(t), ends(batch_of(t - 1)))
        return 0

    lax.fori_loop(1, steps // 4, tick, 0)
    for copy in halos:
        copy.wait()
    begin(seam, ends(batch_of(steps // 4 - 1)))
    loads[5].wait()
    turned[...] = mixing[...].T
    mix_high, mix_low = split(turned[pl.ds(pl.multiple_of(col * rows, rows), rows)])
    mix = jnp.concatenate([mix_high, mix_low], axis=0)
    home[0] = jnp.zeros((rows, S), F32)

    def merge(j, _):
        at = pl.ds(pl.multiple_of(j * S, S), S)
        part = jnp.concatenate([panels[c, :, at] for c in range(cols)], axis=0)
        both = dot(mix, wide(part))
        home[j + 1] = fold(both[:rows]) + fold(both[rows:])
        return 0

    margin = send(
        home.at[pl.ds(1, 4)], home.at[pl.ds(steps + 1, 4)], halo_send.at[3], halo_sem.at[3], {"row": before}
    )

    def merge_first():
        loads[4].wait()
        panel_rings[0].arrive()
        lax.fori_loop(0, steps // 2, merge, 0, unroll=4)

        @pl.when(me > 0)
        def _():
            margin.start()

        @pl.when(me == slabs - 1)
        def _():
            home[pl.ds(steps + 1, 4)] = jnp.zeros((4, rows, S), F32)


    for piece in ends(seam):
        piece()
    merge_first()
    for piece in map_waves(range(-1, 9)):
        piece()
    panel_rings[1].forward()
    for piece in map_waves(range(9, steps + 3)):
        piece()

    def matrix(ref):
        high0, low0 = split(jnp.concatenate([ref[0], ref[1]], axis=1))
        high1, low1 = split(jnp.concatenate([zero, ref[2]], axis=1))
        return jnp.concatenate([high0, high1], axis=0), jnp.concatenate([low0, low1], axis=0)

    def whole(ref):
        return jnp.concatenate(
            [jnp.concatenate([ref[0], ref[1]], axis=1), jnp.concatenate([zero, ref[2]], axis=1)], axis=0
        )

    def keep(ref, x):
        ref[0] = x[:S, :S]
        ref[1] = x[:S, S:]
        ref[2] = x[S:, S:]

    pair = send(own_m, pair_m, scan_send.at[0], scan_sem.at[0], {"row": partner})
    pair.start()

    on_first = core == 0

    def pair_maps():
        pair.wait()
        first = jnp.where(on_first, whole(own_m), whole(pair_m))
        second = jnp.where(on_first, whole(pair_m), whole(own_m))
        keep(chip_m, mul(first, *split(second)))
        chip_ring_m.start()
        chips_m[chip] = chip_m[...]

    def fresh_one(k):
        return window(home[k + 1], home[k + 2], o_one)

    is_first = me == 0
    data_one[...] = jnp.where(is_first, fresh_one(-1), 0.0)
    mid_data[0] = jnp.zeros((rows, S), F32)

    def data_step_one(k):
        x = jnp.concatenate([data_one[...], fresh_one(k + 1)], axis=1)
        out = mul(x, k_high[k + 1], k_low[k + 1])
        mid_data[k + 2] = out[:, :S]
        data_one[...] = out[:, S:]

    def fresh_two(k):
        return window(mid_data[k + 1 + jump], mid_data[k + 2 + jump], by)

    def data_step_two(k):
        carried = data_two[...] if k >= 0 else jnp.where(is_first, fresh_two(-1), 0.0)
        x = jnp.concatenate([carried, fresh_two(k + 1)], axis=1)
        out = mul(x, k_high[k + steps + 4], k_low[k + steps + 4])
        aligned[k + 1] = out[:, :S]
        data_two[...] = out[:, S:]


    def save_data_one():
        own_b[:, :S] = data_one[...]

    def save_data_two():
        own_b[:, S:] = data_two[...]

    def merge_second():
        panel_rings[1].arrive()
        lax.fori_loop(steps // 2, steps, merge, 0, unroll=4)

    def take_margin():
        @pl.when(me < slabs - 1)
        def _():
            margin.wait_recv()

    also = {
        3: pair_maps, 5: merge_second, 12: chip_ring_m.forward, steps - 2: take_margin,
        steps: chip_ring_m.swap_near,
    }
    for k in range(-1, steps + 3):
        if k in also:
            also[k]()
        wave(k, data_step_one, data_step_two, save_data_one, save_data_two)

    pair_two = send(own_b, pair_b, scan_send.at[1], scan_sem.at[1], {"row": partner})
    pair_two.start()

    chip_ring_m.swap_far()
    pair_two.wait()
    first_m = jnp.where(on_first, whole(own_m), whole(pair_m))
    second_m = jnp.where(on_first, whole(pair_m), whole(own_m))
    first_b = jnp.where(on_first, own_b[...], pair_b[...])
    second_b = jnp.where(on_first, pair_b[...], own_b[...])
    chip_b[...] = mul(first_b, *split(second_m)) + second_b
    chip_ring_b.start()
    chips_b[chip] = chip_b[...]
    chip_ring_m.arrive()
    total = whole(chips_m.at[0])
    lead = eye2
    for j in range(1, inner):
        lead = jnp.where(chip == j, total, lead)
        total = mul(total, *matrix(chips_m.at[j]))
    keep(layer_m, total)
    layer_ring_m.start()
    layers_m[layer] = layer_m[...]
    lead_m = jnp.where(on_first, lead, mul(lead, *split(first_m)))
    chip_ring_b.relay()
    layer_ring_m.forward()
    reach_out = S - o_two
    jump_out = reach_out // S
    by_out = lax.rem(reach_out, S)

    for j in range(steps):
        y_home[:, j * S : (j + 1) * S] = window(aligned[j + jump_out], aligned[j + jump_out + 1], by_out)
        z_high[j], z_low[j] = split(window(z_all[j + jump_out], z_all[j + jump_out + 1], by_out))
    chip_ring_b.arrive()
    total_b = chips_b[0]
    lead_b = jnp.zeros((rows, 2 * S), F32)
    for j in range(1, inner):
        lead_b = jnp.where(chip == j, total_b, lead_b)
        total_b = mul(total_b, *matrix(chips_m.at[j])) + chips_b[j]
    layer_b[...] = total_b
    layer_ring_b.start()
    layers_b[layer] = layer_b[...]
    lead_b = jnp.where(on_first, lead_b, mul(lead_b, *split(first_m)) + first_b)
    layer_ring_m.swap_near()
    layer_ring_m.swap_far()
    layer_ring_b.relay()
    layer_ring_m.arrive()
    layer_ring_b.arrive()
    carry = jnp.where(layer > 0, layers_b[0], 0.0)
    for z in range(1, outer - 1):
        longer = mul(carry, *matrix(layers_m.at[z])) + layers_b[z]
        carry = jnp.where(z < layer, longer, carry)
    carry = mul(carry, *split(lead_m)) + lead_b
    for j in range(steps):
        here = slice(j * S, (j + 1) * S)
        out_ref[:, here] = y_home[:, here] + mul(carry, z_high[j], z_low[j])
    for ring in (*panel_rings, chip_ring_m, chip_ring_b, layer_ring_m, layer_ring_b):
        ring.finish()

    @pl.when(me > 0)
    def _():
        margin.wait_send()


def shards(panel, cauchy, refl_v, block_start):
    rows, width = panel.shape
    steps = refl_v.shape[1]
    cols, slabs = lax.axis_size("col"), lax.axis_size("row")
    inner = 4
    outer = slabs // (2 * inner)
    count = 2 * steps + 4
    scan_copies = 2 + 2 * 9 + 2 * 4

    def f(*shape):
        return pltpu.VMEM(shape, F32)

    def b(*shape):
        return pltpu.VMEM(shape, BF)

    dma = pltpu.SemaphoreType.DMA
    return pl.pallas_call(
        functools.partial(kernel, inner),
        in_specs=[SMEM, HBM, HBM, HBM],
        out_specs=VMEM,
        out_shape=pltpu.VMEM((rows, width), F32),
        scratch_shapes=[
            f(count, 2 * S, S), b(count, 2 * S, 2 * S), b(count, 2 * S, 2 * S),
            f(cols, rows, width), f(2 * S, 2 * S), f(2 * S, 2 * S), f(steps + 5, rows, S),
            f(steps + 5, S, S), f(steps + 5, rows, S),
            f(steps + 2, 2 * S, S), b(steps, 2 * S, S), b(steps, 2 * S, S), f(steps + 2, rows, S), f(rows, width),
            f(S, S), f(2 * S, S), f(rows, S), f(rows, S),
            f(3, S, S), f(3, S, S), f(inner, 3, S, S), f(3, S, S), f(outer, 3, S, S),
            f(rows, 2 * S), f(rows, 2 * S), f(rows, 2 * S), f(inner, rows, 2 * S),
            f(rows, 2 * S), f(outer, rows, 2 * S), f(3, S, S),
            f(8, 8, S), f(8, S, S),
            dma((6,)), dma((12,)), dma((12,)), dma((4,)), dma((4,)),
            dma((scan_copies,)), dma((scan_copies,)),
        ],
        compiler_params=pltpu.CompilerParams(
            collective_id=0, has_side_effects=True, vmem_limit_bytes=60 * 2**20
        ),
        name="back_transform",
    )(block_start, panel, cauchy, refl_v)

def solution(mesh):
    placed = (P("col", "row"), P(), P(None, "row", None, None), P())
    return jax.shard_map(
        shards, mesh=mesh, in_specs=placed, out_specs=P("col", "row"), check_vma=False
    )
```

```python
import functools
import jax
import jax.numpy as jnp
from jax import lax
from jax.experimental import pallas as pl
from jax.experimental.pallas import tpu as pltpu
from jax.sharding import PartitionSpec as P

F32 = jnp.float32
BF = jnp.bfloat16
S = 128
MESH = pl.DeviceIdType.MESH
VMEM = pl.BlockSpec(memory_space=pltpu.VMEM)
SMEM = pl.BlockSpec(memory_space=pltpu.SMEM)
HBM = pl.BlockSpec(memory_space=pltpu.HBM)


def split(x):
    high = x.astype(BF)
    return high, (x - high.astype(F32)).astype(BF)


def dot(a, b):
    return jnp.dot(a, b, preferred_element_type=F32)


def dot_t(a, b):
    return lax.dot_general(a, b, (((1,), (1,)), ((), ())), preferred_element_type=F32)


def wide(x):
    return jnp.concatenate(split(x), axis=1)


def square(x):
    row = wide(x)
    return jnp.concatenate([row, row], axis=0)


def fold(x):
    return x[:, :S] + x[:, S:]


def mul(a, b_high, b_low):
    high, low = split(a)
    return dot(
        jnp.concatenate([high, low, high], axis=1), jnp.concatenate([b_high, b_high, b_low], axis=0)
    )


def lanes(rows, size):
    lane = lax.broadcasted_iota(jnp.int32, (rows, S), 1) // size
    return [(lane == b).astype(F32) for b in range(S // size)]


def spread(x, masks, at):
    high, low = split(x)
    zero = jnp.zeros(high.shape, BF)
    rows = []
    for b in range(len(masks)):
        if at[b] is None:
            rows.append(jnp.concatenate([zero, zero], axis=1))
        else:
            mask = masks[at[b]]
            rows.append(jnp.concatenate([high * mask, low * mask], axis=1))
    top = jnp.concatenate(rows, axis=0)
    return jnp.concatenate([top, top], axis=0)


def unit_inverses(nils):
    f4, f2 = lanes(32, 32), lanes(64, 64)
    b4, b2 = [m.astype(BF) for m in f4], [m.astype(BF) for m in f2]
    row = lax.broadcasted_iota(jnp.int32, (32, S), 0)
    lane = lax.broadcasted_iota(jnp.int32, (32, S), 1)
    eye = (row == lax.rem(lane, 32)).astype(F32)
    diag4, diag2 = [0, 1, 2, 3], [0, 1]

    def pick(n, size, masks, at):
        part = None
        for b, mask in zip(at, masks):
            piece = n[b * size : (b + 1) * size] * mask
            part = piece if part is None else part + piece
        return part

    small = [pick(n, 32, f4, diag4) for n in nils]
    result = [eye - c for c in small]
    power = [fold(dot(wide(c), spread(c, b4, diag4))) for c in small]
    yield
    for _ in range(3):
        both = [
            fold(dot(wide(jnp.concatenate([p, r], axis=0)), spread(p, b4, diag4)))
            for p, r in zip(power, result)
        ]
        result = [r + b[32:] for r, b in zip(result, both)]
        power = [b[:32] for b in both]
        yield
    result = [r + fold(dot(wide(r), spread(p, b4, diag4))) for p, r in zip(power, result)]
    yield

    under = [pick(n, 32, [f4[0], f4[2]], [1, 3]) for n in nils]
    inner = [fold(dot(wide(u), spread(r, b4, diag4))) for u, r in zip(under, result)]
    yield
    outer = [
        fold(dot(wide(r), spread(t, b4, [None, 0, None, 2]))) for r, t in zip(result, inner)
    ]
    result = [
        jnp.concatenate([r * (f4[0] + f4[2]), r * (f4[1] + f4[3]) - o], axis=0)
        for r, o in zip(result, outer)
    ]
    yield
    under = [n[64:] * f2[0] for n in nils]
    inner = [fold(dot(wide(u), spread(r, b2, diag2))) for u, r in zip(under, result)]
    yield
    outer = [fold(dot(wide(r), spread(t, b2, [None, 0]))) for r, t in zip(result, inner)]
    return [
        jnp.concatenate([r * f2[0], r * f2[1] - o], axis=0) for r, o in zip(result, outer)
    ]


def prepare(blocks, active):
    row = lax.broadcasted_iota(jnp.int32, (S, S), 0)
    col = lax.broadcasted_iota(jnp.int32, (S, S), 1)
    eye = (row == col).astype(F32)
    quads = [dot(v.T.astype(BF), wide(v)) for v in blocks]
    yield
    grams = [fold(q) + q[:, S:].T for q in quads]
    scale = [
        jnp.where(on, -2.0 / jnp.sum(g * eye, axis=0, keepdims=True), 0.0)
        for g, on in zip(grams, active)
    ]
    nils = [jnp.where(row > col, g * -s, 0.0) for g, s in zip(grams, scale)]
    yield
    result = yield from unit_inverses(nils)
    return scale, result


def less(v, scale, result):
    high, low = split(fold(dot(wide(v * scale), square(result))))
    v_high, v_low = split(v)
    both = jnp.concatenate([high, low], axis=1)
    return dot_t(both, jnp.concatenate([v_high, v_high], axis=1)) + dot_t(high, v_low)


def window(left, right, by):
    lane = lax.broadcasted_iota(jnp.int32, left.shape, 1)
    turn = lax.rem(S - by, S)
    return jnp.where(
        lane < S - by, pltpu.roll(left, turn, 1), pltpu.roll(right, turn, 1)
    )


def kernel(
    inner, offset_ref, panel_ref, cauchy_ref, v_ref, out_ref,
    v_all, k_high, k_low, panels, mixing, turned, home, mid_map, mid_data, z_all, z_high, z_low, aligned, y_home,
    map_one, map_two, data_one, data_two,
    pair_m, chip_m, chips_m, layer_m, layers_m, own_b, pair_b, chip_b, chips_b, layer_b, layers_b,
    own_m, ready_s, ready_r, load_sem, ring_send, ring_sem, halo_send, halo_sem, scan_send, scan_sem,
):
    me, slabs = lax.axis_index("row"), lax.axis_size("row")
    col, cols = lax.axis_index("col"), lax.axis_size("col")
    steps = v_ref.shape[1]
    rows = panel_ref.shape[0]
    half = rows // 2
    group = 2 * inner
    outer = slabs // group
    core = lax.rem(me, 2)
    chip = lax.rem(me // 2, inner)
    layer = me // group
    right, left = lax.rem(col + 1, cols), lax.rem(col + cols - 1, cols)
    after, before = lax.rem(me + 1, slabs), lax.rem(me + slabs - 1, slabs)
    partner = me + 1 - 2 * core
    near = [layer * group + lax.rem(chip + s, inner) * 2 + core for s in range(1, inner)]
    apart = [lax.rem(me + s * group, slabs) for s in range(1, outer)]

    loads = []
    for i in range(4):
        sweep, at = i // 2, (i % 2) * (steps // 2)
        loads.append(
            pltpu.make_async_copy(
                v_ref.at[sweep, pl.ds(at, steps // 2)],
                v_all.at[pl.ds(1 + sweep * (steps + 3) + at, steps // 2)],
                load_sem.at[i],
            )
        )
    loads.append(pltpu.make_async_copy(panel_ref, panels.at[col], load_sem.at[4]))
    loads.append(pltpu.make_async_copy(cauchy_ref, mixing, load_sem.at[5]))
    loads[0].start()

    barrier = pltpu.get_barrier_semaphore()
    for peer in (right, left):
        pl.semaphore_signal(barrier, inc=1, device_id={"col": peer}, device_id_type=MESH)
    sides = [near[0], near[-1]]
    greeted = [after, before, partner] + near + apart + [peer + 1 - 2 * core for peer in sides]
    for peer in greeted:
        pl.semaphore_signal(barrier, inc=1, device_id={"row": peer}, device_id_type=MESH)

    def send(source, target, send_sem, recv_sem, device):
        return pltpu.make_async_remote_copy(
            src_ref=source, dst_ref=target, send_sem=send_sem, recv_sem=recv_sem,
            device_id=device, device_id_type=MESH,
        )

    halos = [
        send(v_ref.at[0, steps - 1], v_all.at[0], halo_send.at[0], halo_sem.at[0], {"row": after}),
        send(v_ref.at[1, steps - 1], v_all.at[steps + 3], halo_send.at[1], halo_sem.at[1], {"row": after}),
        send(v_ref.at[0, pl.ds(0, 2)], v_all.at[pl.ds(steps + 1, 2)], halo_send.at[2], halo_sem.at[2], {"row": before}),
    ]

    class Ring:
        def __init__(self, source, slots, place, size, axis, peer, parts, send_sem, recv_sem, base):
            ahead, behind = lax.rem(place + 1, size), lax.rem(place + size - 1, size)
            up, down = {axis: peer(ahead)}, {axis: peer(behind)}
            one, two = parts
            sems = iter(range(base, base + 6))

            def copy(slot, part, device, own):
                i = next(sems)
                target = slots.at[(slot, *part)]
                return send(source.at[part] if own else target, target, send_sem.at[i], recv_sem.at[i], device)

            self.first = [
                copy(place, one, up, True), copy(place, two, down, True),
                copy(place, two, up, True), copy(place, one, down, True),
            ]
            self.second = [copy(behind, one, up, False), copy(ahead, two, down, False)]

        def start(self):
            for copy in self.first:
                copy.start()

        def forward(self):
            for arrived, onward in zip(self.first, self.second):
                arrived.wait_recv()
                onward.start()

        def arrive(self):
            for copy in self.first[2:] + self.second:
                copy.wait_recv()

        def finish(self):
            for copy in self.first + self.second:
                copy.wait_send()

    class SplitRing(Ring):
        def __init__(self, source, slots, place, size, axis, peer, send_sem, recv_sem, base, cross):
            at, quarter = core * (S // 2), S // 4
            parts = [(slice(None), pl.ds(pl.multiple_of(at + i * quarter, quarter), quarter)) for i in range(2)]
            super().__init__(source, slots, place, size, axis, peer, parts, send_sem, recv_sem, base)
            rows_here = pl.ds(pl.multiple_of(at, S // 2), S // 2)
            across = 1 - 2 * core
            self.swaps, self.crossed = [], []
            for i, shift in enumerate((size - 1, 1)):
                ref = slots.at[lax.rem(place + shift, size), :, rows_here]
                self.swaps.append(
                    send(ref, ref, send_sem.at[base + 6 + i], recv_sem.at[base + 6 + i], {"row": partner})
                )
                if cross:
                    ref = slots.at[(lax.rem(place + shift, size), *parts[i])]
                    other = peer(lax.rem(place + size - shift, size)) + across
                    self.crossed.append(
                        send(ref, ref, send_sem.at[base + 8 + i], recv_sem.at[base + 8 + i], {axis: other})
                    )
            if not cross:
                ref = slots.at[lax.rem(place + 2, size), :, rows_here]
                self.far = send(ref, ref, send_sem.at[base + 8], recv_sem.at[base + 8], {"row": partner})
                self.swaps.append(self.far)

        def forward(self):
            for i in range(2):
                self.first[i].wait_recv()
                self.second[i].start()
                if self.crossed:
                    self.crossed[i].start()

        def swap_near(self):
            for copy, swap in zip(self.first[2:], self.swaps):
                copy.wait_recv()
                swap.start()

        def swap_far(self):
            for copy in self.second:
                copy.wait_recv()
            self.far.start()

        def arrive(self):
            for copy in self.swaps + (self.second + self.crossed if self.crossed else []):
                copy.wait_recv()

        def finish(self):
            for copy in self.first + self.second + self.swaps + self.crossed:
                copy.wait_send()

    class Direct:
        def __init__(self, source, slots, place, size, axis, peer, send_sem, recv_sem, base):
            mine = pl.ds(pl.multiple_of(core * half, half), half)
            to = [{axis: peer(lax.rem(place + shift, size))} for shift in (2, 1, size - 1)]
            refs = [(source.at[mine], slots.at[place, mine])] + [(source, slots.at[place])] * 2
            self.copies = [
                send(*ref, send_sem.at[base + i], recv_sem.at[base + i], device)
                for i, (ref, device) in enumerate(zip(refs, to))
            ]
            ref = slots.at[lax.rem(place + 2, size), mine]
            self.swap = send(ref, ref, send_sem.at[base + 3], recv_sem.at[base + 3], {"row": partner})

        def start(self):
            for copy in self.copies:
                copy.start()

        def relay(self):
            self.copies[0].wait_recv()
            self.swap.start()

        def arrive(self):
            for copy in [*self.copies[1:], self.swap]:
                copy.wait_recv()

        def finish(self):
            for copy in [*self.copies, self.swap]:
                copy.wait_send()

    flat = [(pl.ds(i * half, half),) for i in range(2)]
    width = panel_ref.shape[1] // 2
    panel_rings = []
    for i in range(2):
        parts = [(*rows_of, pl.ds(i * width, width)) for rows_of in flat]
        panel_rings.append(
            Ring(panel_ref, panels, col, cols, "col", lambda c: c, parts, ring_send, ring_sem, 6 * i)
        )
    in_layer = dict(place=chip, size=inner, axis="row", peer=lambda x: layer * group + 2 * x + core)
    over_layers = dict(place=layer, size=outer, axis="row", peer=lambda z: z * group + 2 * chip + core)

    scan_sems = dict(send_sem=scan_send, recv_sem=scan_sem)
    chip_ring_m = SplitRing(chip_m, chips_m, base=2, cross=True, **in_layer, **scan_sems)
    layer_ring_m = SplitRing(layer_m, layers_m, base=12, cross=False, **over_layers, **scan_sems)
    chip_ring_b = Direct(chip_b, chips_b, base=22, **in_layer, **scan_sems)
    layer_ring_b = Direct(layer_b, layers_b, base=26, **over_layers, **scan_sems)

    last = slabs * steps - 3
    row = lax.broadcasted_iota(jnp.int32, (2 * S, 2 * S), 0)
    colm = lax.broadcasted_iota(jnp.int32, (2 * S, 2 * S), 1)
    eye2 = (row == colm).astype(F32)

    def is_on(slot):
        return (slot >= 0) & (slot <= last)

    def begin(batch, filler):
        stages = prepare([v_all[at] for at, _ in batch], [is_on(slot) for _, slot in batch])
        share = -(-len(filler) // 9)
        filler = list(filler)
        while True:
            try:
                next(stages)
            except StopIteration as done:
                scale, result = done.value
                break
            for piece in filler[:share]:
                piece()
            filler = filler[share:]
        for piece in filler:
            piece()
        for i in range(len(batch)):
            ready_s[i] = jnp.broadcast_to(scale[i], (8, S))
            ready_r[i] = result[i]

    def end(i, at):
        x = less(v_all[at], ready_s[i, :1], ready_r[i])
        for r in range(2):
            for c in range(2):
                here = pl.ds(r * S, S), pl.ds(c * S, S)
                part = x[r * S : (r + 1) * S, c * S : (c + 1) * S]
                high, low = split(eye2[:S, :S] + part if r == c else part)
                k_high[(at, *here)] = high
                k_low[(at, *here)] = low

    def ends(batch):
        return [functools.partial(end, i, at) for i, (at, _) in enumerate(batch)]

    first_slot = me * steps

    def batch_of(t):
        at, slot = 1 + 8 * t + 3 * (t // (steps // 8)), first_slot + lax.rem(t, steps // 8) * 8
        return [(at + i, slot + i) for i in range(8)]

    seam = [(0, first_slot - 1), (steps + 3, first_slot - 1)]
    seam += [(steps + 1, first_slot + steps), (steps + 2, first_slot + steps + 1)]

    o_one, o_two = offset_ref[0], offset_ref[1]
    reach = S + o_two - o_one
    jump = reach // S
    by = lax.rem(reach, S)
    eye = eye2[:S, :S]
    zero = jnp.zeros((S, S), F32)
    map_one[...] = eye
    map_two[...] = jnp.concatenate([zero, eye], axis=0)
    mid_map[0] = zero

    def map_step_one(k):
        out = mul(map_one[...], k_high[k + 1, :S], k_low[k + 1, :S])
        mid_map[k + 2] = out[:, :S]
        map_one[...] = out[:, S:]

    def map_step_two(k):
        fresh = window(mid_map[k + 2 + jump], mid_map[k + 3 + jump], by)
        at = k + steps + 4
        x = jnp.concatenate([map_two[...], jnp.concatenate([fresh, zero], axis=0)], axis=1)
        out = mul(x, k_high[at], k_low[at])
        z_all[k + 1] = out[:, :S]
        map_two[...] = out[:, S:]

    def wave(k, one, two, save_one, save_two):
        if k < steps + 2:
            one(k)
        if k > 1:
            two(k - 3)
        if k == steps - 2:
            save_one()
        if k == steps + 1:
            save_two()

    def save_map_one():
        own_m[0] = map_one[...]

    def save_map_two():
        own_m[1] = map_two[:S]
        own_m[2] = map_two[S:]

    def map_waves(ks):
        return [functools.partial(wave, k, map_step_one, map_step_two, save_map_one, save_map_two) for k in ks]

    def mixed(some, others):
        out = []
        while some or others:
            out += some[:1] + others[:1]
            some, others = some[1:], others[1:]
        return out

    def enter():
        pl.semaphore_wait(barrier, 2 + len(greeted))
        for copy in halos:
            copy.start()
        panel_rings[0].start()

    loads[0].wait()
    for copy in loads[1:]:
        copy.start()
    begin(batch_of(0), [])
    enter()
    for copy in loads[1:4]:
        copy.wait()

    def tick(t, _):
        @pl.when(t == 3)
        def _():
            panel_rings[0].forward()
            panel_rings[1].start()

        begin(batch_of(t), ends(batch_of(t - 1)))
        return 0

    lax.fori_loop(1, steps // 4, tick, 0)
    for copy in halos:
        copy.wait()
    begin(seam, ends(batch_of(steps // 4 - 1)))
    loads[5].wait()
    turned[...] = mixing[...].T
    mix_high, mix_low = split(turned[pl.ds(pl.multiple_of(col * rows, rows), rows)])
    mix = jnp.concatenate([mix_high, mix_low], axis=0)
    home[0] = jnp.zeros((rows, S), F32)

    def merge(j, _):
        at = pl.ds(pl.multiple_of(j * S, S), S)
        part = jnp.concatenate([panels[c, :, at] for c in range(cols)], axis=0)
        both = dot(mix, wide(part))
        home[j + 1] = fold(both[:rows]) + fold(both[rows:])
        return 0

    margin = send(
        home.at[pl.ds(1, 4)], home.at[pl.ds(steps + 1, 4)], halo_send.at[3], halo_sem.at[3], {"row": before}
    )

    def merge_first():
        loads[4].wait()
        panel_rings[0].arrive()
        lax.fori_loop(0, steps // 2, merge, 0, unroll=4)

        @pl.when(me == slabs - 1)
        def _():
            home[pl.ds(steps + 1, 4)] = jnp.zeros((4, rows, S), F32)


    for piece in ends(seam) + map_waves(range(-1, 9)):
        piece()
    panel_rings[1].forward()
    for piece in map_waves(range(9, steps + 2)):
        piece()
    pair = send(own_m, pair_m, scan_send.at[0], scan_sem.at[0], {"row": partner})
    pair.start()
    map_waves([steps + 2])[0]()
    merge_first()

    def matrix(ref):
        high0, low0 = split(jnp.concatenate([ref[0], ref[1]], axis=1))
        high1, low1 = split(jnp.concatenate([zero, ref[2]], axis=1))
        return jnp.concatenate([high0, high1], axis=0), jnp.concatenate([low0, low1], axis=0)

    def whole(ref):
        return jnp.concatenate(
            [jnp.concatenate([ref[0], ref[1]], axis=1), jnp.concatenate([zero, ref[2]], axis=1)], axis=0
        )

    def keep(ref, x):
        ref[0] = x[:S, :S]
        ref[1] = x[:S, S:]
        ref[2] = x[S:, S:]

    on_first = core == 0

    def pair_maps():
        pair.wait()
        first = jnp.where(on_first, whole(own_m), whole(pair_m))
        second = jnp.where(on_first, whole(pair_m), whole(own_m))
        keep(chip_m, mul(first, *split(second)))
        chip_ring_m.start()

        @pl.when(me > 0)
        def _():
            margin.start()

        chips_m[chip] = chip_m[...]

    def fresh_one(k):
        return window(home[k + 1], home[k + 2], o_one)

    is_first = me == 0
    data_one[...] = jnp.where(is_first, fresh_one(-1), 0.0)
    mid_data[0] = jnp.zeros((rows, S), F32)

    def data_step_one(k):
        x = jnp.concatenate([data_one[...], fresh_one(k + 1)], axis=1)
        out = mul(x, k_high[k + 1], k_low[k + 1])
        mid_data[k + 2] = out[:, :S]
        data_one[...] = out[:, S:]

    def fresh_two(k):
        return window(mid_data[k + 1 + jump], mid_data[k + 2 + jump], by)

    def data_step_two(k):
        carried = data_two[...] if k >= 0 else jnp.where(is_first, fresh_two(-1), 0.0)
        x = jnp.concatenate([carried, fresh_two(k + 1)], axis=1)
        out = mul(x, k_high[k + steps + 4], k_low[k + steps + 4])
        aligned[k + 1] = out[:, :S]
        data_two[...] = out[:, S:]


    def save_data_one():
        own_b[:, :S] = data_one[...]

    def save_data_two():
        own_b[:, S:] = data_two[...]

    def merge_second():
        panel_rings[1].arrive()
        lax.fori_loop(steps // 2, steps, merge, 0, unroll=4)

    def take_margin():
        @pl.when(me < slabs - 1)
        def _():
            margin.wait_recv()

    pair_two = send(own_b, pair_b, scan_send.at[1], scan_sem.at[1], {"row": partner})
    also = {
        0: pair_maps, 5: merge_second, 12: chip_ring_m.forward, steps - 2: take_margin,
        steps: chip_ring_m.swap_near,
    }
    for k in range(-1, steps + 3):
        if k in also:
            also[k]()
        wave(k, data_step_one, data_step_two, save_data_one, save_data_two)
        if k == steps + 1:
            pair_two.start()


    pair_two.wait()
    first_m = jnp.where(on_first, whole(own_m), whole(pair_m))
    second_m = jnp.where(on_first, whole(pair_m), whole(own_m))
    first_b = jnp.where(on_first, own_b[...], pair_b[...])
    second_b = jnp.where(on_first, pair_b[...], own_b[...])
    chip_b[...] = mul(first_b, *split(second_m)) + second_b
    chip_ring_b.start()
    chips_b[chip] = chip_b[...]
    chip_ring_m.arrive()
    pieces = [whole(chips_m.at[j]) for j in range(inner)]
    halves = [split(x) for x in pieces]
    early = mul(pieces[0], *halves[1])
    late = mul(pieces[2], *halves[3])
    late_parts = split(late)
    keep(layer_m, mul(early, *late_parts))
    layer_ring_m.start()
    layers_m[layer] = layer_m[...]
    lead = jnp.where(chip == 0, eye2, jnp.where(chip == 1, pieces[0], early))
    lead = jnp.where(chip == 3, mul(early, *halves[2]), lead)
    lead_m = jnp.where(on_first, lead, mul(lead, *split(first_m)))
    chip_ring_b.relay()
    layer_ring_m.forward()
    chip_ring_b.arrive()
    early_b = mul(chips_b[0], *halves[1]) + chips_b[1]
    layer_b[...] = mul(early_b, *late_parts) + (mul(chips_b[2], *halves[3]) + chips_b[3])
    layer_ring_b.start()
    layers_b[layer] = layer_b[...]
    lead_b = jnp.where(chip == 0, 0.0, jnp.where(chip == 1, chips_b[0], early_b))
    lead_b = jnp.where(chip == 3, mul(early_b, *halves[2]) + chips_b[2], lead_b)
    lead_b = jnp.where(on_first, lead_b, mul(lead_b, *split(first_m)) + first_b)
    reach_out = S - o_two
    jump_out = reach_out // S
    by_out = lax.rem(reach_out, S)

    for j in range(steps):
        y_home[:, j * S : (j + 1) * S] = window(aligned[j + jump_out], aligned[j + jump_out + 1], by_out)
        z_high[j], z_low[j] = split(window(z_all[j + jump_out], z_all[j + jump_out + 1], by_out))
    layer_ring_m.swap_near()
    layer_ring_m.swap_far()
    layer_ring_b.relay()
    layer_ring_m.arrive()
    layer_ring_b.arrive()
    carry = jnp.where(layer > 0, layers_b[0], 0.0)
    for z in range(1, outer - 1):
        longer = mul(carry, *matrix(layers_m.at[z])) + layers_b[z]
        carry = jnp.where(z < layer, longer, carry)
    carry = mul(carry, *split(lead_m)) + lead_b
    for j in range(steps):
        here = slice(j * S, (j + 1) * S)
        out_ref[:, here] = y_home[:, here] + mul(carry, z_high[j], z_low[j])
    for ring in (*panel_rings, chip_ring_m, chip_ring_b, layer_ring_m, layer_ring_b):
        ring.finish()

    @pl.when(me > 0)
    def _():
        margin.wait_send()


def shards(panel, cauchy, refl_v, block_start):
    rows, width = panel.shape
    steps = refl_v.shape[1]
    cols, slabs = lax.axis_size("col"), lax.axis_size("row")
    inner = 4
    outer = slabs // (2 * inner)
    count = 2 * steps + 4
    scan_copies = 2 + 2 * 10 + 2 * 4

    def f(*shape):
        return pltpu.VMEM(shape, F32)

    def b(*shape):
        return pltpu.VMEM(shape, BF)

    dma = pltpu.SemaphoreType.DMA
    return pl.pallas_call(
        functools.partial(kernel, inner),
        in_specs=[SMEM, HBM, HBM, HBM],
        out_specs=VMEM,
        out_shape=pltpu.VMEM((rows, width), F32),
        scratch_shapes=[
            f(count, 2 * S, S), b(count, 2 * S, 2 * S), b(count, 2 * S, 2 * S),
            f(cols, rows, width), f(2 * S, 2 * S), f(2 * S, 2 * S), f(steps + 5, rows, S),
            f(steps + 5, S, S), f(steps + 5, rows, S),
            f(steps + 2, 2 * S, S), b(steps, 2 * S, S), b(steps, 2 * S, S), f(steps + 2, rows, S), f(rows, width),
            f(S, S), f(2 * S, S), f(rows, S), f(rows, S),
            f(3, S, S), f(3, S, S), f(inner, 3, S, S), f(3, S, S), f(outer, 3, S, S),
            f(rows, 2 * S), f(rows, 2 * S), f(rows, 2 * S), f(inner, rows, 2 * S),
            f(rows, 2 * S), f(outer, rows, 2 * S), f(3, S, S),
            f(8, 8, S), f(8, S, S),
            dma((6,)), dma((12,)), dma((12,)), dma((4,)), dma((4,)),
            dma((scan_copies,)), dma((scan_copies,)),
        ],
        compiler_params=pltpu.CompilerParams(
            collective_id=0, has_side_effects=True, vmem_limit_bytes=60 * 2**20
        ),
        name="back_transform",
    )(block_start, panel, cauchy, refl_v)

def solution(mesh):
    placed = (P("col", "row"), P(), P(None, "row", None, None), P())
    return jax.shard_map(
        shards, mesh=mesh, in_specs=placed, out_specs=P("col", "row"), check_vma=False
    )
```

```python
import functools
import jax
import jax.numpy as jnp
from jax import lax
from jax.experimental import pallas as pl
from jax.experimental.pallas import tpu as pltpu
from jax.sharding import PartitionSpec as P

F32 = jnp.float32
BF = jnp.bfloat16
S = 128
MESH = pl.DeviceIdType.MESH
VMEM = pl.BlockSpec(memory_space=pltpu.VMEM)
SMEM = pl.BlockSpec(memory_space=pltpu.SMEM)
HBM = pl.BlockSpec(memory_space=pltpu.HBM)


def split(x):
    high = x.astype(BF)
    return high, (x - high.astype(F32)).astype(BF)


def dot(a, b):
    return jnp.dot(a, b, preferred_element_type=F32)


def dot_t(a, b):
    return lax.dot_general(a, b, (((1,), (1,)), ((), ())), preferred_element_type=F32)


def wide(x):
    return jnp.concatenate(split(x), axis=1)


def square(x):
    row = wide(x)
    return jnp.concatenate([row, row], axis=0)


def fold(x):
    return x[:, :S] + x[:, S:]


def mul(a, b_high, b_low):
    high, low = split(a)
    return dot(
        jnp.concatenate([high, low, high], axis=1), jnp.concatenate([b_high, b_high, b_low], axis=0)
    )


def lanes(rows, size):
    lane = lax.broadcasted_iota(jnp.int32, (rows, S), 1) // size
    return [(lane == b).astype(F32) for b in range(S // size)]


def spread(x, masks, at):
    high, low = split(x)
    zero = jnp.zeros(high.shape, BF)
    rows = []
    for b in range(len(masks)):
        if at[b] is None:
            rows.append(jnp.concatenate([zero, zero], axis=1))
        else:
            mask = masks[at[b]]
            rows.append(jnp.concatenate([high * mask, low * mask], axis=1))
    top = jnp.concatenate(rows, axis=0)
    return jnp.concatenate([top, top], axis=0)


def unit_inverses(nils):
    f4, f2 = lanes(32, 32), lanes(64, 64)
    b4, b2 = [m.astype(BF) for m in f4], [m.astype(BF) for m in f2]
    row = lax.broadcasted_iota(jnp.int32, (32, S), 0)
    lane = lax.broadcasted_iota(jnp.int32, (32, S), 1)
    eye = (row == lax.rem(lane, 32)).astype(F32)
    diag4, diag2 = [0, 1, 2, 3], [0, 1]

    def pick(n, size, masks, at):
        part = None
        for b, mask in zip(at, masks):
            piece = n[b * size : (b + 1) * size] * mask
            part = piece if part is None else part + piece
        return part

    small = [pick(n, 32, f4, diag4) for n in nils]
    result = [eye - c for c in small]
    power = [fold(dot(wide(c), spread(c, b4, diag4))) for c in small]
    yield
    for _ in range(3):
        both = [
            fold(dot(wide(jnp.concatenate([p, r], axis=0)), spread(p, b4, diag4)))
            for p, r in zip(power, result)
        ]
        result = [r + b[32:] for r, b in zip(result, both)]
        power = [b[:32] for b in both]
        yield
    result = [r + fold(dot(wide(r), spread(p, b4, diag4))) for p, r in zip(power, result)]
    yield

    under = [pick(n, 32, [f4[0], f4[2]], [1, 3]) for n in nils]
    inner = [fold(dot(wide(u), spread(r, b4, diag4))) for u, r in zip(under, result)]
    yield
    outer = [
        fold(dot(wide(r), spread(t, b4, [None, 0, None, 2]))) for r, t in zip(result, inner)
    ]
    result = [
        jnp.concatenate([r * (f4[0] + f4[2]), r * (f4[1] + f4[3]) - o], axis=0)
        for r, o in zip(result, outer)
    ]
    yield
    under = [n[64:] * f2[0] for n in nils]
    inner = [fold(dot(wide(u), spread(r, b2, diag2))) for u, r in zip(under, result)]
    yield
    outer = [fold(dot(wide(r), spread(t, b2, [None, 0]))) for r, t in zip(result, inner)]
    return [
        jnp.concatenate([r * f2[0], r * f2[1] - o], axis=0) for r, o in zip(result, outer)
    ]


def prepare(blocks, active):
    row = lax.broadcasted_iota(jnp.int32, (S, S), 0)
    col = lax.broadcasted_iota(jnp.int32, (S, S), 1)
    pairs = [wide(v) for v in blocks]
    quads = [dot(v.T.astype(BF), p) for v, p in zip(blocks, pairs)]
    yield
    grams = [fold(q) + q[:, S:].T for q in quads]
    scale = [
        jnp.where(on, -2.0 / jnp.sum(v * v, axis=0, keepdims=True), 0.0)
        for v, on in zip(blocks, active)
    ]
    nils = [jnp.where(row > col, g * -s, 0.0) for g, s in zip(grams, scale)]
    yield
    result = yield from unit_inverses(nils)
    result = [jnp.broadcast_to(s, (S, S)).T * r for s, r in zip(scale, result)]
    return pairs, result


def less(v_pair, result):
    high, low = split(fold(dot(v_pair, square(result))))
    v_high, v_low = v_pair[:, :S], v_pair[:, S:]
    both = jnp.concatenate([high, low], axis=1)
    return dot_t(both, jnp.concatenate([v_high, v_high], axis=1)) + dot_t(high, v_low)


def window(left, right, by):
    lane = lax.broadcasted_iota(jnp.int32, left.shape, 1)
    turn = lax.rem(S - by, S)
    return jnp.where(
        lane < S - by, pltpu.roll(left, turn, 1), pltpu.roll(right, turn, 1)
    )


def kernel(
    inner, offset_ref, panel_ref, cauchy_ref, v_ref, out_ref,
    v_all, k_high, k_low, panels, mixing, turned, home, mid_map, mid_data, z_all, z_high, z_low, aligned, y_home,
    map_one, map_two, data_one, data_two,
    pair_m, chip_m, chips_m, layer_m, layers_m, own_b, pair_b, chip_b, chips_b, layer_b, layers_b,
    own_m, ready_v, ready_r, load_sem, ring_send, ring_sem, halo_send, halo_sem, scan_send, scan_sem,
):
    me, slabs = lax.axis_index("row"), lax.axis_size("row")
    col, cols = lax.axis_index("col"), lax.axis_size("col")
    steps = v_ref.shape[1]
    rows = panel_ref.shape[0]
    half = rows // 2
    group = 2 * inner
    outer = slabs // group
    core = lax.rem(me, 2)
    chip = lax.rem(me // 2, inner)
    layer = me // group
    right, left = lax.rem(col + 1, cols), lax.rem(col + cols - 1, cols)
    after, before = lax.rem(me + 1, slabs), lax.rem(me + slabs - 1, slabs)
    partner = me + 1 - 2 * core
    near = [layer * group + lax.rem(chip + s, inner) * 2 + core for s in range(1, inner)]
    apart = [lax.rem(me + s * group, slabs) for s in range(1, outer)]

    loads = []
    for i in range(4):
        sweep, at = i // 2, (i % 2) * (steps // 2)
        loads.append(
            pltpu.make_async_copy(
                v_ref.at[sweep, pl.ds(at, steps // 2)],
                v_all.at[pl.ds(1 + sweep * (steps + 3) + at, steps // 2)],
                load_sem.at[i],
            )
        )
    loads.append(pltpu.make_async_copy(panel_ref, panels.at[col], load_sem.at[4]))
    loads.append(pltpu.make_async_copy(cauchy_ref, mixing, load_sem.at[5]))
    head_loads = []
    for i in range(4):
        head_loads.append(
            pltpu.make_async_copy(v_ref.at[0, pl.ds(2 * i, 2)], v_all.at[pl.ds(1 + 2 * i, 2)], load_sem.at[6 + i])
        )
        head_loads[-1].start()

    barrier = pltpu.get_barrier_semaphore()
    for peer in (right, left):
        pl.semaphore_signal(barrier, inc=1, device_id={"col": peer}, device_id_type=MESH)
    sides = [near[0], near[-1]]
    greeted = [after, before, partner] + near + apart + [peer + 1 - 2 * core for peer in sides]
    for peer in greeted:
        pl.semaphore_signal(barrier, inc=1, device_id={"row": peer}, device_id_type=MESH)

    def send(source, target, send_sem, recv_sem, device):
        return pltpu.make_async_remote_copy(
            src_ref=source, dst_ref=target, send_sem=send_sem, recv_sem=recv_sem,
            device_id=device, device_id_type=MESH,
        )

    halos = [
        send(v_ref.at[0, steps - 1], v_all.at[0], halo_send.at[0], halo_sem.at[0], {"row": after}),
        send(v_ref.at[1, steps - 1], v_all.at[steps + 3], halo_send.at[1], halo_sem.at[1], {"row": after}),
        send(v_ref.at[0, pl.ds(0, 2)], v_all.at[pl.ds(steps + 1, 2)], halo_send.at[2], halo_sem.at[2], {"row": before}),
    ]

    class Ring:
        def __init__(self, source, slots, place, size, axis, peer, parts, send_sem, recv_sem, base):
            ahead, behind = lax.rem(place + 1, size), lax.rem(place + size - 1, size)
            up, down = {axis: peer(ahead)}, {axis: peer(behind)}
            one, two = parts
            sems = iter(range(base, base + 6))

            def copy(slot, part, device, own):
                i = next(sems)
                target = slots.at[(slot, *part)]
                return send(source.at[part] if own else target, target, send_sem.at[i], recv_sem.at[i], device)

            self.first = [
                copy(place, one, up, True), copy(place, two, down, True),
                copy(place, two, up, True), copy(place, one, down, True),
            ]
            self.second = [copy(behind, one, up, False), copy(ahead, two, down, False)]

        def start(self):
            for copy in self.first:
                copy.start()

        def forward(self):
            for arrived, onward in zip(self.first, self.second):
                arrived.wait_recv()
                onward.start()

        def arrive(self):
            for copy in self.first[2:] + self.second:
                copy.wait_recv()

        def finish(self):
            for copy in self.first + self.second:
                copy.wait_send()

    class SplitRing(Ring):
        def __init__(self, source, slots, place, size, axis, peer, send_sem, recv_sem, base, cross):
            at, quarter = core * (S // 2), S // 4
            parts = [(slice(None), pl.ds(pl.multiple_of(at + i * quarter, quarter), quarter)) for i in range(2)]
            super().__init__(source, slots, place, size, axis, peer, parts, send_sem, recv_sem, base)
            rows_here = pl.ds(pl.multiple_of(at, S // 2), S // 2)
            across = 1 - 2 * core
            self.swaps, self.crossed = [], []
            for i, shift in enumerate((size - 1, 1)):
                ref = slots.at[lax.rem(place + shift, size), :, rows_here]
                self.swaps.append(
                    send(ref, ref, send_sem.at[base + 6 + i], recv_sem.at[base + 6 + i], {"row": partner})
                )
                if cross:
                    ref = slots.at[(lax.rem(place + shift, size), *parts[i])]
                    other = peer(lax.rem(place + size - shift, size)) + across
                    self.crossed.append(
                        send(ref, ref, send_sem.at[base + 8 + i], recv_sem.at[base + 8 + i], {axis: other})
                    )
            if not cross:
                ref = slots.at[lax.rem(place + 2, size), :, rows_here]
                self.far = send(ref, ref, send_sem.at[base + 8], recv_sem.at[base + 8], {"row": partner})
                self.swaps.append(self.far)

        def forward(self):
            for i in range(2):
                self.first[i].wait_recv()
                self.second[i].start()
                if self.crossed:
                    self.crossed[i].start()

        def swap_near(self):
            for copy, swap in zip(self.first[2:], self.swaps):
                copy.wait_recv()
                swap.start()

        def swap_far(self):
            for copy in self.second:
                copy.wait_recv()
            self.far.start()

        def arrive(self):
            for copy in self.swaps + (self.second + self.crossed if self.crossed else []):
                copy.wait_recv()

        def finish(self):
            for copy in self.first + self.second + self.swaps + self.crossed:
                copy.wait_send()

    class Direct:
        def __init__(self, source, slots, place, size, axis, peer, send_sem, recv_sem, base):
            mine = pl.ds(pl.multiple_of(core * half, half), half)
            to = [{axis: peer(lax.rem(place + shift, size))} for shift in (2, 1, size - 1)]
            refs = [(source.at[mine], slots.at[place, mine])] + [(source, slots.at[place])] * 2
            self.copies = [
                send(*ref, send_sem.at[base + i], recv_sem.at[base + i], device)
                for i, (ref, device) in enumerate(zip(refs, to))
            ]
            ref = slots.at[lax.rem(place + 2, size), mine]
            self.swap = send(ref, ref, send_sem.at[base + 3], recv_sem.at[base + 3], {"row": partner})

        def start(self):
            for copy in self.copies:
                copy.start()

        def relay(self):
            self.copies[0].wait_recv()
            self.swap.start()

        def arrive(self):
            for copy in [*self.copies[1:], self.swap]:
                copy.wait_recv()

        def finish(self):
            for copy in [*self.copies, self.swap]:
                copy.wait_send()

    flat = [(pl.ds(i * half, half),) for i in range(2)]
    width = panel_ref.shape[1] // 2
    panel_rings = []
    for i in range(2):
        parts = [(*rows_of, pl.ds(i * width, width)) for rows_of in flat]
        panel_rings.append(
            Ring(panel_ref, panels, col, cols, "col", lambda c: c, parts, ring_send, ring_sem, 6 * i)
        )
    in_layer = dict(place=chip, size=inner, axis="row", peer=lambda x: layer * group + 2 * x + core)
    over_layers = dict(place=layer, size=outer, axis="row", peer=lambda z: z * group + 2 * chip + core)

    scan_sems = dict(send_sem=scan_send, recv_sem=scan_sem)
    chip_ring_m = SplitRing(chip_m, chips_m, base=2, cross=True, **in_layer, **scan_sems)
    layer_ring_m = SplitRing(layer_m, layers_m, base=12, cross=False, **over_layers, **scan_sems)
    chip_ring_b = Direct(chip_b, chips_b, base=22, **in_layer, **scan_sems)
    layer_ring_b = Direct(layer_b, layers_b, base=26, **over_layers, **scan_sems)

    last = slabs * steps - 3
    row = lax.broadcasted_iota(jnp.int32, (2 * S, 2 * S), 0)
    colm = lax.broadcasted_iota(jnp.int32, (2 * S, 2 * S), 1)
    eye2 = (row == colm).astype(F32)

    def is_on(slot):
        return (slot >= 0) & (slot <= last)

    def begin(batch, filler):
        stages = prepare([v_all[at] for at, _ in batch], [is_on(slot) for _, slot in batch])
        share = -(-len(filler) // 9)
        filler = list(filler)
        while True:
            try:
                next(stages)
            except StopIteration as done:
                pairs, result = done.value
                break
            for piece in filler[:share]:
                piece()
            filler = filler[share:]
        for piece in filler:
            piece()
        for i in range(len(batch)):
            ready_v[i] = pairs[i]
            ready_r[i] = result[i]

    def end(i, at):
        x = less(ready_v[i], ready_r[i])
        for r in range(2):
            for c in range(2):
                here = pl.ds(r * S, S), pl.ds(c * S, S)
                part = x[r * S : (r + 1) * S, c * S : (c + 1) * S]
                high, low = split(eye2[:S, :S] + part if r == c else part)
                k_high[(at, *here)] = high
                k_low[(at, *here)] = low

    def ends(batch):
        return [functools.partial(end, i, at) for i, (at, _) in enumerate(batch)]

    first_slot = me * steps

    def batch_of(t):
        at, slot = 1 + 8 * t + 3 * (t // (steps // 8)), first_slot + lax.rem(t, steps // 8) * 8
        return [(at + i, slot + i) for i in range(8)]

    seam = [(0, first_slot - 1), (steps + 3, first_slot - 1)]
    seam += [(steps + 1, first_slot + steps), (steps + 2, first_slot + steps + 1)]

    o_one, o_two = offset_ref[0], offset_ref[1]
    reach = S + o_two - o_one
    jump = reach // S
    by = lax.rem(reach, S)
    eye = eye2[:S, :S]
    zero = jnp.zeros((S, S), F32)
    map_one[...] = eye
    map_two[...] = jnp.concatenate([zero, eye], axis=0)
    mid_map[0] = zero

    def map_step_one(k):
        out = mul(map_one[...], k_high[k + 1, :S], k_low[k + 1, :S])
        mid_map[k + 2] = out[:, :S]
        map_one[...] = out[:, S:]

    def map_step_two(k):
        fresh = window(mid_map[k + 2 + jump], mid_map[k + 3 + jump], by)
        at = k + steps + 4
        x = jnp.concatenate([map_two[...], jnp.concatenate([fresh, zero], axis=0)], axis=1)
        out = mul(x, k_high[at], k_low[at])
        z_all[k + 1] = out[:, :S]
        map_two[...] = out[:, S:]

    def wave(k, one, two, save_one, save_two):
        if k < steps + 2:
            one(k)
        if k > 1:
            two(k - 3)
        if k == steps - 2:
            save_one()
        if k == steps + 1:
            save_two()

    def save_map_one():
        own_m[0] = map_one[...]

    def save_map_two():
        own_m[1] = map_two[:S]
        own_m[2] = map_two[S:]

    def map_waves(ks):
        return [functools.partial(wave, k, map_step_one, map_step_two, save_map_one, save_map_two) for k in ks]

    def mixed(some, others):
        out = []
        while some or others:
            out += some[:1] + others[:1]
            some, others = some[1:], others[1:]
        return out

    def enter():
        pl.semaphore_wait(barrier, 2 + len(greeted))
        for copy in halos:
            copy.start()
        panel_rings[0].start()

    for copy in head_loads:
        copy.wait()
    for copy in loads[1:]:
        copy.start()
    begin(batch_of(0), [])
    enter()
    for copy in loads[1:4]:
        copy.wait()

    def tick(t, _):
        @pl.when(t == 3)
        def _():
            panel_rings[0].forward()
            panel_rings[1].start()

        begin(batch_of(t), ends(batch_of(t - 1)))
        return 0

    lax.fori_loop(1, steps // 4, tick, 0)
    for copy in halos:
        copy.wait()
    begin(seam, ends(batch_of(steps // 4 - 1)))
    loads[5].wait()
    turned[...] = mixing[...].T
    mix_high, mix_low = split(turned[pl.ds(pl.multiple_of(col * rows, rows), rows)])
    mix = jnp.concatenate([mix_high, mix_low], axis=0)
    home[0] = jnp.zeros((rows, S), F32)

    def merge(j, _):
        at = pl.ds(pl.multiple_of(j * S, S), S)
        part = jnp.concatenate([panels[c, :, at] for c in range(cols)], axis=0)
        both = dot(mix, wide(part))
        home[j + 1] = fold(both[:rows]) + fold(both[rows:])
        return 0

    margin = send(
        home.at[pl.ds(1, 4)], home.at[pl.ds(steps + 1, 4)], halo_send.at[3], halo_sem.at[3], {"row": before}
    )

    def merge_first():
        loads[4].wait()
        panel_rings[0].arrive()
        lax.fori_loop(0, steps // 2, merge, 0, unroll=4)

        @pl.when(me == slabs - 1)
        def _():
            home[pl.ds(steps + 1, 4)] = jnp.zeros((4, rows, S), F32)


    for piece in ends(seam) + map_waves(range(-1, 9)):
        piece()
    panel_rings[1].forward()
    for piece in map_waves(range(9, steps + 2)):
        piece()
    pair = send(own_m, pair_m, scan_send.at[0], scan_sem.at[0], {"row": partner})
    pair.start()
    map_waves([steps + 2])[0]()
    merge_first()

    def matrix(ref):
        high0, low0 = split(jnp.concatenate([ref[0], ref[1]], axis=1))
        high1, low1 = split(jnp.concatenate([zero, ref[2]], axis=1))
        return jnp.concatenate([high0, high1], axis=0), jnp.concatenate([low0, low1], axis=0)

    def whole(ref):
        return jnp.concatenate(
            [jnp.concatenate([ref[0], ref[1]], axis=1), jnp.concatenate([zero, ref[2]], axis=1)], axis=0
        )

    def keep(ref, x):
        ref[0] = x[:S, :S]
        ref[1] = x[:S, S:]
        ref[2] = x[S:, S:]

    on_first = core == 0

    def pair_maps():
        pair.wait()
        first = jnp.where(on_first, whole(own_m), whole(pair_m))
        second = jnp.where(on_first, whole(pair_m), whole(own_m))
        keep(chip_m, mul(first, *split(second)))
        chip_ring_m.start()

        @pl.when(me > 0)
        def _():
            margin.start()

        chips_m[chip] = chip_m[...]

    def fresh_one(k):
        return window(home[k + 1], home[k + 2], o_one)

    is_first = me == 0
    data_one[...] = jnp.where(is_first, fresh_one(-1), 0.0)
    mid_data[0] = jnp.zeros((rows, S), F32)

    def data_step_one(k):
        x = jnp.concatenate([data_one[...], fresh_one(k + 1)], axis=1)
        out = mul(x, k_high[k + 1], k_low[k + 1])
        mid_data[k + 2] = out[:, :S]
        data_one[...] = out[:, S:]

    def fresh_two(k):
        return window(mid_data[k + 1 + jump], mid_data[k + 2 + jump], by)

    def data_step_two(k):
        carried = data_two[...] if k >= 0 else jnp.where(is_first, fresh_two(-1), 0.0)
        x = jnp.concatenate([carried, fresh_two(k + 1)], axis=1)
        out = mul(x, k_high[k + steps + 4], k_low[k + steps + 4])
        aligned[k + 1] = out[:, :S]
        data_two[...] = out[:, S:]


    def save_data_one():
        own_b[:, :S] = data_one[...]

    def save_data_two():
        own_b[:, S:] = data_two[...]

    def merge_second():
        panel_rings[1].arrive()
        lax.fori_loop(steps // 2, steps, merge, 0, unroll=True)

    def take_margin():
        @pl.when(me < slabs - 1)
        def _():
            margin.wait_recv()

    pair_two = send(own_b, pair_b, scan_send.at[1], scan_sem.at[1], {"row": partner})
    also = {
        0: pair_maps, 5: merge_second, 12: chip_ring_m.forward, steps - 2: take_margin,
        steps: chip_ring_m.swap_near,
    }
    for k in range(-1, steps + 3):
        if k in also:
            also[k]()
        wave(k, data_step_one, data_step_two, save_data_one, save_data_two)
        if k == steps + 1:
            pair_two.start()


    pair_two.wait()
    first_m = jnp.where(on_first, whole(own_m), whole(pair_m))
    second_m = jnp.where(on_first, whole(pair_m), whole(own_m))
    first_b = jnp.where(on_first, own_b[...], pair_b[...])
    second_b = jnp.where(on_first, pair_b[...], own_b[...])
    chip_b[...] = mul(first_b, *split(second_m)) + second_b
    chip_ring_b.start()
    chips_b[chip] = chip_b[...]
    chip_ring_m.arrive()
    pieces = [whole(chips_m.at[j]) for j in range(inner)]
    halves = [split(x) for x in pieces]
    early = mul(pieces[0], *halves[1])
    late = mul(pieces[2], *halves[3])
    late_parts = split(late)
    keep(layer_m, mul(early, *late_parts))
    layer_ring_m.start()
    layers_m[layer] = layer_m[...]
    lead = jnp.where(chip == 0, eye2, jnp.where(chip == 1, pieces[0], early))
    lead = jnp.where(chip == 3, mul(early, *halves[2]), lead)
    lead_m = jnp.where(on_first, lead, mul(lead, *split(first_m)))
    chip_ring_b.relay()
    layer_ring_m.forward()
    chip_ring_b.arrive()
    early_b = mul(chips_b[0], *halves[1]) + chips_b[1]
    layer_b[...] = mul(early_b, *late_parts) + (mul(chips_b[2], *halves[3]) + chips_b[3])
    layer_ring_b.start()
    layers_b[layer] = layer_b[...]
    lead_b = jnp.where(chip == 0, 0.0, jnp.where(chip == 1, chips_b[0], early_b))
    lead_b = jnp.where(chip == 3, mul(early_b, *halves[2]) + chips_b[2], lead_b)
    lead_b = jnp.where(on_first, lead_b, mul(lead_b, *split(first_m)) + first_b)
    reach_out = S - o_two
    jump_out = reach_out // S
    by_out = lax.rem(reach_out, S)

    for j in range(steps):
        y_home[:, j * S : (j + 1) * S] = window(aligned[j + jump_out], aligned[j + jump_out + 1], by_out)
        z_high[j], z_low[j] = split(window(z_all[j + jump_out], z_all[j + jump_out + 1], by_out))
    layer_ring_m.swap_near()
    layer_ring_m.swap_far()
    layer_ring_b.relay()
    layer_ring_m.arrive()
    layer_ring_b.arrive()
    carry = jnp.where(layer > 0, layers_b[0], 0.0)
    for z in range(1, outer - 1):
        longer = mul(carry, *matrix(layers_m.at[z])) + layers_b[z]
        carry = jnp.where(z < layer, longer, carry)
    carry = mul(carry, *split(lead_m)) + lead_b
    for j in range(steps):
        here = slice(j * S, (j + 1) * S)
        out_ref[:, here] = y_home[:, here] + mul(carry, z_high[j], z_low[j])
    for ring in (*panel_rings, chip_ring_m, chip_ring_b, layer_ring_m, layer_ring_b):
        ring.finish()

    @pl.when(me > 0)
    def _():
        margin.wait_send()


def shards(panel, cauchy, refl_v, block_start):
    rows, width = panel.shape
    steps = refl_v.shape[1]
    cols, slabs = lax.axis_size("col"), lax.axis_size("row")
    inner = 4
    outer = slabs // (2 * inner)
    count = 2 * steps + 4
    scan_copies = 2 + 2 * 10 + 2 * 4

    def f(*shape):
        return pltpu.VMEM(shape, F32)

    def b(*shape):
        return pltpu.VMEM(shape, BF)

    dma = pltpu.SemaphoreType.DMA
    return pl.pallas_call(
        functools.partial(kernel, inner),
        in_specs=[SMEM, HBM, HBM, HBM],
        out_specs=VMEM,
        out_shape=pltpu.VMEM((rows, width), F32),
        scratch_shapes=[
            f(count, 2 * S, S), b(count, 2 * S, 2 * S), b(count, 2 * S, 2 * S),
            f(cols, rows, width), f(2 * S, 2 * S), f(2 * S, 2 * S), f(steps + 5, rows, S),
            f(steps + 5, S, S), f(steps + 5, rows, S),
            f(steps + 2, 2 * S, S), b(steps, 2 * S, S), b(steps, 2 * S, S), f(steps + 2, rows, S), f(rows, width),
            f(S, S), f(2 * S, S), f(rows, S), f(rows, S),
            f(3, S, S), f(3, S, S), f(inner, 3, S, S), f(3, S, S), f(outer, 3, S, S),
            f(rows, 2 * S), f(rows, 2 * S), f(rows, 2 * S), f(inner, rows, 2 * S),
            f(rows, 2 * S), f(outer, rows, 2 * S), f(3, S, S),
            b(8, 2 * S, 2 * S), f(8, S, S),
            dma((10,)), dma((12,)), dma((12,)), dma((4,)), dma((4,)),
            dma((scan_copies,)), dma((scan_copies,)),
        ],
        compiler_params=pltpu.CompilerParams(
            collective_id=0, has_side_effects=True, vmem_limit_bytes=60 * 2**20
        ),
        name="back_transform",
    )(block_start, panel, cauchy, refl_v)

def solution(mesh):
    placed = (P("col", "row"), P(), P(None, "row", None, None), P())
    return jax.shard_map(
        shards, mesh=mesh, in_specs=placed, out_specs=P("col", "row"), check_vma=False
    )
```

```python
import functools
import jax
import jax.numpy as jnp
from jax import lax
from jax.experimental import pallas as pl
from jax.experimental.pallas import tpu as pltpu
from jax.sharding import PartitionSpec as P

F32 = jnp.float32
BF = jnp.bfloat16
S = 128
MESH = pl.DeviceIdType.MESH
VMEM = pl.BlockSpec(memory_space=pltpu.VMEM)
SMEM = pl.BlockSpec(memory_space=pltpu.SMEM)
HBM = pl.BlockSpec(memory_space=pltpu.HBM)


def split(x):
    high = x.astype(BF)
    return high, (x - high.astype(F32)).astype(BF)


def dot(a, b):
    return jnp.dot(a, b, preferred_element_type=F32)


def dot_t(a, b):
    return lax.dot_general(a, b, (((1,), (1,)), ((), ())), preferred_element_type=F32)


def wide(x):
    return jnp.concatenate(split(x), axis=1)


def square(x):
    row = wide(x)
    return jnp.concatenate([row, row], axis=0)


def fold(x):
    return x[:, :S] + x[:, S:]


def mul(a, b_high, b_low):
    high, low = split(a)
    return dot(
        jnp.concatenate([high, low, high], axis=1), jnp.concatenate([b_high, b_high, b_low], axis=0)
    )


def lanes(rows, size):
    lane = lax.broadcasted_iota(jnp.int32, (rows, S), 1) // size
    return [(lane == b).astype(F32) for b in range(S // size)]


def spread(x, masks, at):
    high, low = split(x)
    zero = jnp.zeros(high.shape, BF)
    rows = []
    for b in range(len(masks)):
        if at[b] is None:
            rows.append(jnp.concatenate([zero, zero], axis=1))
        else:
            mask = masks[at[b]]
            rows.append(jnp.concatenate([high * mask, low * mask], axis=1))
    top = jnp.concatenate(rows, axis=0)
    return jnp.concatenate([top, top], axis=0)


def unit_inverses(nils):
    f4, f2 = lanes(32, 32), lanes(64, 64)
    b4, b2 = [m.astype(BF) for m in f4], [m.astype(BF) for m in f2]
    row = lax.broadcasted_iota(jnp.int32, (32, S), 0)
    lane = lax.broadcasted_iota(jnp.int32, (32, S), 1)
    eye = (row == lax.rem(lane, 32)).astype(F32)
    diag4, diag2 = [0, 1, 2, 3], [0, 1]

    def pick(n, size, masks, at):
        part = None
        for b, mask in zip(at, masks):
            piece = n[b * size : (b + 1) * size] * mask
            part = piece if part is None else part + piece
        return part

    small = [pick(n, 32, f4, diag4) for n in nils]
    result = [eye - c for c in small]
    power = [fold(dot(wide(c), spread(c, b4, diag4))) for c in small]
    yield
    for _ in range(3):
        both = [
            fold(dot(wide(jnp.concatenate([p, r], axis=0)), spread(p, b4, diag4)))
            for p, r in zip(power, result)
        ]
        result = [r + b[32:] for r, b in zip(result, both)]
        power = [b[:32] for b in both]
        yield
    result = [r + fold(dot(wide(r), spread(p, b4, diag4))) for p, r in zip(power, result)]
    yield

    under = [pick(n, 32, [f4[0], f4[2]], [1, 3]) for n in nils]
    inner = [fold(dot(wide(u), spread(r, b4, diag4))) for u, r in zip(under, result)]
    yield
    outer = [
        fold(dot(wide(r), spread(t, b4, [None, 0, None, 2]))) for r, t in zip(result, inner)
    ]
    result = [
        jnp.concatenate([r * (f4[0] + f4[2]), r * (f4[1] + f4[3]) - o], axis=0)
        for r, o in zip(result, outer)
    ]
    yield
    under = [n[64:] * f2[0] for n in nils]
    inner = [fold(dot(wide(u), spread(r, b2, diag2))) for u, r in zip(under, result)]
    yield
    outer = [fold(dot(wide(r), spread(t, b2, [None, 0]))) for r, t in zip(result, inner)]
    return [
        jnp.concatenate([r * f2[0], r * f2[1] - o], axis=0) for r, o in zip(result, outer)
    ]


def prepare(blocks, active):
    row = lax.broadcasted_iota(jnp.int32, (S, S), 0)
    col = lax.broadcasted_iota(jnp.int32, (S, S), 1)
    pairs = [wide(v) for v in blocks]
    quads = [dot(v.T.astype(BF), p) for v, p in zip(blocks, pairs)]
    yield
    grams = [fold(q) + q[:, S:].T for q in quads]
    scale = [
        jnp.where(on, -2.0 / jnp.sum(v * v, axis=0, keepdims=True), 0.0)
        for v, on in zip(blocks, active)
    ]
    nils = [jnp.where(row > col, g * -s, 0.0) for g, s in zip(grams, scale)]
    yield
    result = yield from unit_inverses(nils)
    result = [jnp.broadcast_to(s, (S, S)).T * r for s, r in zip(scale, result)]
    return pairs, result


def less(v_pair, result):
    high, low = split(fold(dot(v_pair, square(result))))
    v_high, v_low = v_pair[:, :S], v_pair[:, S:]
    both = jnp.concatenate([high, low], axis=1)
    return dot_t(both, jnp.concatenate([v_high, v_high], axis=1)) + dot_t(high, v_low)


def window(left, right, by):
    lane = lax.broadcasted_iota(jnp.int32, left.shape, 1)
    turn = lax.rem(S - by, S)
    return jnp.where(
        lane < S - by, pltpu.roll(left, turn, 1), pltpu.roll(right, turn, 1)
    )


def kernel(
    inner, offset_ref, panel_ref, cauchy_ref, v_ref, out_ref,
    v_all, k_high, k_low, panels, mixing, turned, home, mid_map, mid_data, z_all, z_high, z_low, aligned, y_home,
    map_one, map_two, data_one, data_two,
    pair_m, chip_m, chips_m, layer_m, layers_m, own_b, pair_b, chip_b, chips_b, layer_b, layers_b,
    own_m, ready_v, ready_r, load_sem, ring_send, ring_sem, halo_send, halo_sem, scan_send, scan_sem,
):
    me, slabs = lax.axis_index("row"), lax.axis_size("row")
    col, cols = lax.axis_index("col"), lax.axis_size("col")
    steps = v_ref.shape[1]
    rows = panel_ref.shape[0]
    half = rows // 2
    group = 2 * inner
    outer = slabs // group
    core = lax.rem(me, 2)
    chip = lax.rem(me // 2, inner)
    layer = me // group
    right, left = lax.rem(col + 1, cols), lax.rem(col + cols - 1, cols)
    after, before = lax.rem(me + 1, slabs), lax.rem(me + slabs - 1, slabs)
    partner = me + 1 - 2 * core
    near = [layer * group + lax.rem(chip + s, inner) * 2 + core for s in range(1, inner)]
    apart = [lax.rem(me + s * group, slabs) for s in range(1, outer)]

    loads = []
    for i in range(4):
        sweep, at = i // 2, (i % 2) * (steps // 2)
        loads.append(
            pltpu.make_async_copy(
                v_ref.at[sweep, pl.ds(at, steps // 2)],
                v_all.at[pl.ds(1 + sweep * (steps + 3) + at, steps // 2)],
                load_sem.at[i],
            )
        )
    loads.append(pltpu.make_async_copy(panel_ref, panels.at[col], load_sem.at[4]))
    loads.append(pltpu.make_async_copy(cauchy_ref, mixing, load_sem.at[5]))
    head_loads = []
    for i in range(4):
        head_loads.append(
            pltpu.make_async_copy(v_ref.at[0, pl.ds(2 * i, 2)], v_all.at[pl.ds(1 + 2 * i, 2)], load_sem.at[6 + i])
        )
        head_loads[-1].start()

    barrier = pltpu.get_barrier_semaphore()
    for peer in (right, left):
        pl.semaphore_signal(barrier, inc=1, device_id={"col": peer}, device_id_type=MESH)
    sides = [near[0], near[-1]]
    greeted = [after, before, partner] + near + apart + [peer + 1 - 2 * core for peer in sides]
    for peer in greeted:
        pl.semaphore_signal(barrier, inc=1, device_id={"row": peer}, device_id_type=MESH)

    def send(source, target, send_sem, recv_sem, device):
        return pltpu.make_async_remote_copy(
            src_ref=source, dst_ref=target, send_sem=send_sem, recv_sem=recv_sem,
            device_id=device, device_id_type=MESH,
        )

    halos = [
        send(v_ref.at[0, steps - 1], v_all.at[0], halo_send.at[0], halo_sem.at[0], {"row": after}),
        send(v_ref.at[1, steps - 1], v_all.at[steps + 3], halo_send.at[1], halo_sem.at[1], {"row": after}),
        send(v_ref.at[0, pl.ds(0, 2)], v_all.at[pl.ds(steps + 1, 2)], halo_send.at[2], halo_sem.at[2], {"row": before}),
    ]

    class Ring:
        def __init__(self, source, slots, place, size, axis, peer, parts, send_sem, recv_sem, base):
            ahead, behind = lax.rem(place + 1, size), lax.rem(place + size - 1, size)
            up, down = {axis: peer(ahead)}, {axis: peer(behind)}
            one, two = parts
            sems = iter(range(base, base + 6))

            def copy(slot, part, device, own):
                i = next(sems)
                target = slots.at[(slot, *part)]
                return send(source.at[part] if own else target, target, send_sem.at[i], recv_sem.at[i], device)

            self.first = [
                copy(place, one, up, True), copy(place, two, down, True),
                copy(place, two, up, True), copy(place, one, down, True),
            ]
            self.second = [copy(behind, one, up, False), copy(ahead, two, down, False)]

        def start(self):
            for copy in self.first:
                copy.start()

        def forward(self):
            for arrived, onward in zip(self.first, self.second):
                arrived.wait_recv()
                onward.start()

        def arrive(self):
            for copy in self.first[2:] + self.second:
                copy.wait_recv()

        def finish(self):
            for copy in self.first + self.second:
                copy.wait_send()

    class SplitRing(Ring):
        def __init__(self, source, slots, place, size, axis, peer, send_sem, recv_sem, base, cross):
            at, quarter = core * (S // 2), S // 4
            parts = [(slice(None), pl.ds(pl.multiple_of(at + i * quarter, quarter), quarter)) for i in range(2)]
            super().__init__(source, slots, place, size, axis, peer, parts, send_sem, recv_sem, base)
            rows_here = pl.ds(pl.multiple_of(at, S // 2), S // 2)
            across = 1 - 2 * core
            self.swaps, self.crossed = [], []
            for i, shift in enumerate((size - 1, 1)):
                ref = slots.at[lax.rem(place + shift, size), :, rows_here]
                self.swaps.append(
                    send(ref, ref, send_sem.at[base + 6 + i], recv_sem.at[base + 6 + i], {"row": partner})
                )
                if cross:
                    ref = slots.at[(lax.rem(place + shift, size), *parts[i])]
                    other = peer(lax.rem(place + size - shift, size)) + across
                    self.crossed.append(
                        send(ref, ref, send_sem.at[base + 8 + i], recv_sem.at[base + 8 + i], {axis: other})
                    )
            if not cross:
                ref = slots.at[lax.rem(place + 2, size), :, rows_here]
                self.far = send(ref, ref, send_sem.at[base + 8], recv_sem.at[base + 8], {"row": partner})
                self.swaps.append(self.far)

        def forward(self):
            for i in range(2):
                self.first[i].wait_recv()
                self.second[i].start()
                if self.crossed:
                    self.crossed[i].start()

        def swap_near(self):
            for copy, swap in zip(self.first[2:], self.swaps):
                copy.wait_recv()
                swap.start()

        def swap_far(self):
            for copy in self.second:
                copy.wait_recv()
            self.far.start()

        def arrive(self):
            for copy in self.swaps + (self.second + self.crossed if self.crossed else []):
                copy.wait_recv()

        def finish(self):
            for copy in self.first + self.second + self.swaps + self.crossed:
                copy.wait_send()

    def only(on, act):
        if on is None:
            act()
        elif on is not False:
            pl.when(on)(act)

    z1, z2 = layer == 1, layer == 2
    upper, top_layer, bottom = layer > 1, layer == outer - 1, layer == 0

    class LayerMaps(SplitRing):
        def start(self):
            self.first, self.sent = self.first[:3], [z1 | z2, z1, z1 | z2]
            for copy, on in zip(self.first, self.sent):
                only(on, copy.start)

        def forward(self):
            for i, (came, here) in enumerate([(upper, z2), (bottom, bottom)]):
                only(came, self.first[i].wait_recv)
                only(here, self.second[i].start)

        def swap_near(self):
            only(upper, self.first[2].wait_recv)
            only(upper, self.swaps[0].start)

        def swap_far(self):
            for copy in self.second:
                only(top_layer, copy.wait_recv)
            only(top_layer, self.far.start)

        def arrive(self):
            only(upper, self.swaps[0].wait_recv)
            only(top_layer, self.far.wait_recv)

        def finish(self):
            for copy, on in zip(self.first, self.sent):
                only(on, copy.wait_send)
            only(z2, self.second[0].wait_send)
            only(bottom, self.second[1].wait_send)
            only(upper, self.swaps[0].wait_send)
            only(top_layer, self.far.wait_send)

    class Direct:
        def __init__(self, source, slots, place, size, axis, peer, send_sem, recv_sem, base, later):
            self.sends = [place < size - 2, place < size - 1, place == 0] if later else [None] * 3
            self.comes = [place > 1, place > 0, place == size - 1] if later else [None] * 3
            mine = pl.ds(pl.multiple_of(core * half, half), half)
            to = [{axis: peer(lax.rem(place + shift, size))} for shift in (2, 1, size - 1)]
            refs = [(source.at[mine], slots.at[place, mine])] + [(source, slots.at[place])] * 2
            self.copies = [
                send(*ref, send_sem.at[base + i], recv_sem.at[base + i], device)
                for i, (ref, device) in enumerate(zip(refs, to))
            ]
            ref = slots.at[lax.rem(place + 2, size), mine]
            self.swap = send(ref, ref, send_sem.at[base + 3], recv_sem.at[base + 3], {"row": partner})

        def start(self):
            for copy, on in zip(self.copies, self.sends):
                only(on, copy.start)

        def relay(self):
            only(self.comes[0], self.copies[0].wait_recv)
            only(self.comes[0], self.swap.start)

        def arrive(self):
            for copy, on in zip([*self.copies[1:], self.swap], [*self.comes[1:], self.comes[0]]):
                only(on, copy.wait_recv)

        def finish(self):
            for copy, on in zip([*self.copies, self.swap], [*self.sends, self.comes[0]]):
                only(on, copy.wait_send)

    flat = [(pl.ds(i * half, half),) for i in range(2)]
    width = panel_ref.shape[1] // 2
    panel_rings = []
    for i in range(2):
        parts = [(*rows_of, pl.ds(i * width, width)) for rows_of in flat]
        panel_rings.append(
            Ring(panel_ref, panels, col, cols, "col", lambda c: c, parts, ring_send, ring_sem, 6 * i)
        )
    in_layer = dict(place=chip, size=inner, axis="row", peer=lambda x: layer * group + 2 * x + core)
    over_layers = dict(place=layer, size=outer, axis="row", peer=lambda z: z * group + 2 * chip + core)

    scan_sems = dict(send_sem=scan_send, recv_sem=scan_sem)
    chip_ring_m = SplitRing(chip_m, chips_m, base=2, cross=True, **in_layer, **scan_sems)
    layer_ring_m = LayerMaps(layer_m, layers_m, base=12, cross=False, **over_layers, **scan_sems)
    chip_ring_b = Direct(chip_b, chips_b, base=22, later=False, **in_layer, **scan_sems)
    layer_ring_b = Direct(layer_b, layers_b, base=26, later=True, **over_layers, **scan_sems)

    last = slabs * steps - 3
    row = lax.broadcasted_iota(jnp.int32, (2 * S, 2 * S), 0)
    colm = lax.broadcasted_iota(jnp.int32, (2 * S, 2 * S), 1)
    eye2 = (row == colm).astype(F32)

    def is_on(slot):
        return (slot >= 0) & (slot <= last)

    def begin(batch, filler):
        stages = prepare([v_all[at] for at, _ in batch], [is_on(slot) for _, slot in batch])
        share = -(-len(filler) // 9)
        filler = list(filler)
        while True:
            try:
                next(stages)
            except StopIteration as done:
                pairs, result = done.value
                break
            for piece in filler[:share]:
                piece()
            filler = filler[share:]
        for piece in filler:
            piece()
        for i in range(len(batch)):
            ready_v[i] = pairs[i]
            ready_r[i] = result[i]

    def end(i, at):
        x = less(ready_v[i], ready_r[i])
        for r in range(2):
            for c in range(2):
                here = pl.ds(r * S, S), pl.ds(c * S, S)
                part = x[r * S : (r + 1) * S, c * S : (c + 1) * S]
                high, low = split(eye2[:S, :S] + part if r == c else part)
                k_high[(at, *here)] = high
                k_low[(at, *here)] = low

    def ends(batch):
        return [functools.partial(end, i, at) for i, (at, _) in enumerate(batch)]

    first_slot = me * steps

    def batch_of(t):
        at, slot = 1 + 8 * t + 3 * (t // (steps // 8)), first_slot + lax.rem(t, steps // 8) * 8
        return [(at + i, slot + i) for i in range(8)]

    seam = [(0, first_slot - 1), (steps + 3, first_slot - 1)]
    seam += [(steps + 1, first_slot + steps), (steps + 2, first_slot + steps + 1)]

    o_one, o_two = offset_ref[0], offset_ref[1]
    reach = S + o_two - o_one
    jump = reach // S
    by = lax.rem(reach, S)
    eye = eye2[:S, :S]
    zero = jnp.zeros((S, S), F32)
    map_one[...] = eye
    map_two[...] = jnp.concatenate([zero, eye], axis=0)
    mid_map[0] = zero

    def map_step_one(k):
        out = mul(map_one[...], k_high[k + 1, :S], k_low[k + 1, :S])
        mid_map[k + 2] = out[:, :S]
        map_one[...] = out[:, S:]

    def map_step_two(k):
        fresh = window(mid_map[k + 2 + jump], mid_map[k + 3 + jump], by)
        at = k + steps + 4
        x = jnp.concatenate([map_two[...], jnp.concatenate([fresh, zero], axis=0)], axis=1)
        out = mul(x, k_high[at], k_low[at])
        z_all[k + 1] = out[:, :S]
        map_two[...] = out[:, S:]

    def wave(k, one, two, save_one, save_two):
        if k < steps + 2:
            one(k)
        if k > 1:
            two(k - 3)
        if k == steps - 2:
            save_one()
        if k == steps + 1:
            save_two()

    def save_map_one():
        own_m[0] = map_one[...]

    def save_map_two():
        own_m[1] = map_two[:S]
        own_m[2] = map_two[S:]

    def map_waves(ks):
        return [functools.partial(wave, k, map_step_one, map_step_two, save_map_one, save_map_two) for k in ks]

    def mixed(some, others):
        out = []
        while some or others:
            out += some[:1] + others[:1]
            some, others = some[1:], others[1:]
        return out

    def enter():
        pl.semaphore_wait(barrier, 2 + len(greeted))
        for copy in halos:
            copy.start()
        panel_rings[0].start()

    for copy in head_loads:
        copy.wait()
    for copy in loads[1:]:
        copy.start()
    begin(batch_of(0), [])
    enter()
    for copy in loads[1:4]:
        copy.wait()

    def tick(t, _):
        @pl.when(t == 3)
        def _():
            panel_rings[0].forward()
            panel_rings[1].start()

        begin(batch_of(t), ends(batch_of(t - 1)))
        return 0

    lax.fori_loop(1, steps // 4, tick, 0)
    for copy in halos:
        copy.wait()
    begin(seam, ends(batch_of(steps // 4 - 1)))
    loads[5].wait()
    turned[...] = mixing[...].T
    mix_high, mix_low = split(turned[pl.ds(pl.multiple_of(col * rows, rows), rows)])
    mix = jnp.concatenate([mix_high, mix_low], axis=0)
    home[0] = jnp.zeros((rows, S), F32)

    def merge(j, _):
        at = pl.ds(pl.multiple_of(j * S, S), S)
        part = jnp.concatenate([panels[c, :, at] for c in range(cols)], axis=0)
        both = dot(mix, wide(part))
        home[j + 1] = fold(both[:rows]) + fold(both[rows:])
        return 0

    margin = send(
        home.at[pl.ds(1, 4)], home.at[pl.ds(steps + 1, 4)], halo_send.at[3], halo_sem.at[3], {"row": before}
    )

    def merge_first():
        loads[4].wait()
        panel_rings[0].arrive()
        lax.fori_loop(0, steps // 2, merge, 0, unroll=4)

        @pl.when(me == slabs - 1)
        def _():
            home[pl.ds(steps + 1, 4)] = jnp.zeros((4, rows, S), F32)


    for piece in ends(seam) + map_waves(range(-1, 9)):
        piece()
    panel_rings[1].forward()
    for piece in map_waves(range(9, steps + 2)):
        piece()
    pair = send(own_m, pair_m, scan_send.at[0], scan_sem.at[0], {"row": partner})
    pair.start()
    map_waves([steps + 2])[0]()
    merge_first()

    def matrix(ref):
        high0, low0 = split(jnp.concatenate([ref[0], ref[1]], axis=1))
        high1, low1 = split(jnp.concatenate([zero, ref[2]], axis=1))
        return jnp.concatenate([high0, high1], axis=0), jnp.concatenate([low0, low1], axis=0)

    def whole(ref):
        return jnp.concatenate(
            [jnp.concatenate([ref[0], ref[1]], axis=1), jnp.concatenate([zero, ref[2]], axis=1)], axis=0
        )

    def keep(ref, x):
        ref[0] = x[:S, :S]
        ref[1] = x[:S, S:]
        ref[2] = x[S:, S:]

    on_first = core == 0

    def pair_maps():
        pair.wait()
        first = jnp.where(on_first, whole(own_m), whole(pair_m))
        second = jnp.where(on_first, whole(pair_m), whole(own_m))
        keep(chip_m, mul(first, *split(second)))
        chip_ring_m.start()

        @pl.when(me > 0)
        def _():
            margin.start()

        chips_m[chip] = chip_m[...]

    def fresh_one(k):
        return window(home[k + 1], home[k + 2], o_one)

    is_first = me == 0
    data_one[...] = jnp.where(is_first, fresh_one(-1), 0.0)
    mid_data[0] = jnp.zeros((rows, S), F32)

    def data_step_one(k):
        x = jnp.concatenate([data_one[...], fresh_one(k + 1)], axis=1)
        out = mul(x, k_high[k + 1], k_low[k + 1])
        mid_data[k + 2] = out[:, :S]
        data_one[...] = out[:, S:]

    def fresh_two(k):
        return window(mid_data[k + 1 + jump], mid_data[k + 2 + jump], by)

    def data_step_two(k):
        carried = data_two[...] if k >= 0 else jnp.where(is_first, fresh_two(-1), 0.0)
        x = jnp.concatenate([carried, fresh_two(k + 1)], axis=1)
        out = mul(x, k_high[k + steps + 4], k_low[k + steps + 4])
        aligned[k + 1] = out[:, :S]
        data_two[...] = out[:, S:]


    def save_data_one():
        own_b[:, :S] = data_one[...]

    def save_data_two():
        own_b[:, S:] = data_two[...]

    def merge_second():
        panel_rings[1].arrive()
        lax.fori_loop(steps // 2, steps, merge, 0, unroll=True)

    def take_margin():
        @pl.when(me < slabs - 1)
        def _():
            margin.wait_recv()

    pair_two = send(own_b, pair_b, scan_send.at[1], scan_sem.at[1], {"row": partner})
    also = {
        0: pair_maps, 5: merge_second, 12: chip_ring_m.forward, steps - 2: take_margin,
        steps: chip_ring_m.swap_near,
    }
    for k in range(-1, steps + 3):
        if k in also:
            also[k]()
        wave(k, data_step_one, data_step_two, save_data_one, save_data_two)
        if k == steps + 1:
            pair_two.start()


    pair_two.wait()
    first_m = jnp.where(on_first, whole(own_m), whole(pair_m))
    second_m = jnp.where(on_first, whole(pair_m), whole(own_m))
    first_b = jnp.where(on_first, own_b[...], pair_b[...])
    second_b = jnp.where(on_first, pair_b[...], own_b[...])
    chip_b[...] = mul(first_b, *split(second_m)) + second_b
    chip_ring_b.start()
    chips_b[chip] = chip_b[...]
    chip_ring_m.arrive()
    pieces = [whole(chips_m.at[j]) for j in range(inner)]
    halves = [split(x) for x in pieces]
    early = mul(pieces[0], *halves[1])
    late = mul(pieces[2], *halves[3])
    late_parts = split(late)
    keep(layer_m, mul(early, *late_parts))
    layer_ring_m.start()
    layers_m[layer] = layer_m[...]
    lead = jnp.where(chip == 0, eye2, jnp.where(chip == 1, pieces[0], early))
    lead = jnp.where(chip == 3, mul(early, *halves[2]), lead)
    lead_m = jnp.where(on_first, lead, mul(lead, *split(first_m)))
    chip_ring_b.relay()
    layer_ring_m.forward()
    chip_ring_b.arrive()
    early_b = mul(chips_b[0], *halves[1]) + chips_b[1]
    layer_b[...] = mul(early_b, *late_parts) + (mul(chips_b[2], *halves[3]) + chips_b[3])
    layer_ring_b.start()
    layers_b[layer] = layer_b[...]
    lead_b = jnp.where(chip == 0, 0.0, jnp.where(chip == 1, chips_b[0], early_b))
    lead_b = jnp.where(chip == 3, mul(early_b, *halves[2]) + chips_b[2], lead_b)
    lead_b = jnp.where(on_first, lead_b, mul(lead_b, *split(first_m)) + first_b)
    reach_out = S - o_two
    jump_out = reach_out // S
    by_out = lax.rem(reach_out, S)

    for j in range(steps):
        y_home[:, j * S : (j + 1) * S] = window(aligned[j + jump_out], aligned[j + jump_out + 1], by_out)
        z_high[j], z_low[j] = split(window(z_all[j + jump_out], z_all[j + jump_out + 1], by_out))
    layer_ring_m.swap_near()
    layer_ring_m.swap_far()
    layer_ring_b.relay()
    layer_ring_m.arrive()
    layer_ring_b.arrive()
    carry = jnp.where(layer > 0, layers_b[0], 0.0)
    for z in range(1, outer - 1):
        longer = mul(carry, *matrix(layers_m.at[z])) + layers_b[z]
        carry = jnp.where(z < layer, longer, carry)
    carry = mul(carry, *split(lead_m)) + lead_b
    for j in range(steps):
        here = slice(j * S, (j + 1) * S)
        out_ref[:, here] = y_home[:, here] + mul(carry, z_high[j], z_low[j])
    for ring in (*panel_rings, chip_ring_m, chip_ring_b, layer_ring_m, layer_ring_b):
        ring.finish()

    @pl.when(me > 0)
    def _():
        margin.wait_send()


def shards(panel, cauchy, refl_v, block_start):
    rows, width = panel.shape
    steps = refl_v.shape[1]
    cols, slabs = lax.axis_size("col"), lax.axis_size("row")
    inner = 4
    outer = slabs // (2 * inner)
    count = 2 * steps + 4
    scan_copies = 2 + 2 * 10 + 2 * 4

    def f(*shape):
        return pltpu.VMEM(shape, F32)

    def b(*shape):
        return pltpu.VMEM(shape, BF)

    dma = pltpu.SemaphoreType.DMA
    return pl.pallas_call(
        functools.partial(kernel, inner),
        in_specs=[SMEM, HBM, HBM, HBM],
        out_specs=VMEM,
        out_shape=pltpu.VMEM((rows, width), F32),
        scratch_shapes=[
            f(count, 2 * S, S), b(count, 2 * S, 2 * S), b(count, 2 * S, 2 * S),
            f(cols, rows, width), f(2 * S, 2 * S), f(2 * S, 2 * S), f(steps + 5, rows, S),
            f(steps + 5, S, S), f(steps + 5, rows, S),
            f(steps + 2, 2 * S, S), b(steps, 2 * S, S), b(steps, 2 * S, S), f(steps + 2, rows, S), f(rows, width),
            f(S, S), f(2 * S, S), f(rows, S), f(rows, S),
            f(3, S, S), f(3, S, S), f(inner, 3, S, S), f(3, S, S), f(outer, 3, S, S),
            f(rows, 2 * S), f(rows, 2 * S), f(rows, 2 * S), f(inner, rows, 2 * S),
            f(rows, 2 * S), f(outer, rows, 2 * S), f(3, S, S),
            b(8, 2 * S, 2 * S), f(8, S, S),
            dma((10,)), dma((12,)), dma((12,)), dma((4,)), dma((4,)),
            dma((scan_copies,)), dma((scan_copies,)),
        ],
        compiler_params=pltpu.CompilerParams(
            collective_id=0, has_side_effects=True, vmem_limit_bytes=60 * 2**20
        ),
        name="back_transform",
    )(block_start, panel, cauchy, refl_v)

def solution(mesh):
    placed = (P("col", "row"), P(), P(None, "row", None, None), P())
    return jax.shard_map(
        shards, mesh=mesh, in_specs=placed, out_specs=P("col", "row"), check_vma=False
    )
```

```python
import functools
import jax
import jax.numpy as jnp
from jax import lax
from jax.experimental import pallas as pl
from jax.experimental.pallas import tpu as pltpu
from jax.sharding import PartitionSpec as P

F32 = jnp.float32
BF = jnp.bfloat16
S = 128
MESH = pl.DeviceIdType.MESH
VMEM = pl.BlockSpec(memory_space=pltpu.VMEM)
SMEM = pl.BlockSpec(memory_space=pltpu.SMEM)
HBM = pl.BlockSpec(memory_space=pltpu.HBM)


def split(x):
    high = x.astype(BF)
    return high, (x - high.astype(F32)).astype(BF)


def dot(a, b):
    return jnp.dot(a, b, preferred_element_type=F32)


def dot_t(a, b):
    return lax.dot_general(a, b, (((1,), (1,)), ((), ())), preferred_element_type=F32)


def wide(x):
    return jnp.concatenate(split(x), axis=1)


def square(x):
    row = wide(x)
    return jnp.concatenate([row, row], axis=0)


def fold(x):
    return x[:, :S] + x[:, S:]


def mul(a, b_high, b_low):
    high, low = split(a)
    return dot(
        jnp.concatenate([high, low, high], axis=1), jnp.concatenate([b_high, b_high, b_low], axis=0)
    )


def lanes(rows, size):
    lane = lax.broadcasted_iota(jnp.int32, (rows, S), 1) // size
    return [(lane == b).astype(F32) for b in range(S // size)]


def spread(x, masks, at):
    high, low = split(x)
    zero = jnp.zeros(high.shape, BF)
    rows = []
    for b in range(len(masks)):
        if at[b] is None:
            rows.append(jnp.concatenate([zero, zero], axis=1))
        else:
            mask = masks[at[b]]
            rows.append(jnp.concatenate([high * mask, low * mask], axis=1))
    top = jnp.concatenate(rows, axis=0)
    return jnp.concatenate([top, top], axis=0)


def unit_inverses(nils):
    f4, f2 = lanes(32, 32), lanes(64, 64)
    b4, b2 = [m.astype(BF) for m in f4], [m.astype(BF) for m in f2]
    row = lax.broadcasted_iota(jnp.int32, (32, S), 0)
    lane = lax.broadcasted_iota(jnp.int32, (32, S), 1)
    eye = (row == lax.rem(lane, 32)).astype(F32)
    diag4, diag2 = [0, 1, 2, 3], [0, 1]

    def pick(n, size, masks, at):
        part = None
        for b, mask in zip(at, masks):
            piece = n[b * size : (b + 1) * size] * mask
            part = piece if part is None else part + piece
        return part

    small = [pick(n, 32, f4, diag4) for n in nils]
    result = [eye - c for c in small]
    power = [fold(dot(wide(c), spread(c, b4, diag4))) for c in small]
    yield
    for _ in range(3):
        both = [
            fold(dot(wide(jnp.concatenate([p, r], axis=0)), spread(p, b4, diag4)))
            for p, r in zip(power, result)
        ]
        result = [r + b[32:] for r, b in zip(result, both)]
        power = [b[:32] for b in both]
        yield
    result = [r + fold(dot(wide(r), spread(p, b4, diag4))) for p, r in zip(power, result)]
    yield

    under = [pick(n, 32, [f4[0], f4[2]], [1, 3]) for n in nils]
    inner = [fold(dot(wide(u), spread(r, b4, diag4))) for u, r in zip(under, result)]
    yield
    outer = [
        fold(dot(wide(r), spread(t, b4, [None, 0, None, 2]))) for r, t in zip(result, inner)
    ]
    result = [
        jnp.concatenate([r * (f4[0] + f4[2]), r * (f4[1] + f4[3]) - o], axis=0)
        for r, o in zip(result, outer)
    ]
    yield
    under = [n[64:] * f2[0] for n in nils]
    inner = [fold(dot(wide(u), spread(r, b2, diag2))) for u, r in zip(under, result)]
    yield
    outer = [fold(dot(wide(r), spread(t, b2, [None, 0]))) for r, t in zip(result, inner)]
    return [
        jnp.concatenate([r * f2[0], r * f2[1] - o], axis=0) for r, o in zip(result, outer)
    ]


def prepare(blocks, active):
    row = lax.broadcasted_iota(jnp.int32, (S, S), 0)
    col = lax.broadcasted_iota(jnp.int32, (S, S), 1)
    pairs = [wide(v) for v in blocks]
    quads = [dot(v.T.astype(BF), p) for v, p in zip(blocks, pairs)]
    yield
    grams = [fold(q) + q[:, S:].T for q in quads]
    scale = [
        jnp.where(on, -2.0 / jnp.sum(v * v, axis=0, keepdims=True), 0.0)
        for v, on in zip(blocks, active)
    ]
    nils = [jnp.where(row > col, g * -s, 0.0) for g, s in zip(grams, scale)]
    yield
    result = yield from unit_inverses(nils)
    result = [jnp.broadcast_to(s, (S, S)).T * r for s, r in zip(scale, result)]
    return pairs, result


def less(v_pair, result):
    high, low = split(fold(dot(v_pair, square(result))))
    v_high, v_low = v_pair[:, :S], v_pair[:, S:]
    both = jnp.concatenate([high, low], axis=1)
    return dot_t(both, jnp.concatenate([v_high, v_high], axis=1)) + dot_t(high, v_low)


def window(left, right, by):
    lane = lax.broadcasted_iota(jnp.int32, left.shape, 1)
    turn = lax.rem(S - by, S)
    return jnp.where(
        lane < S - by, pltpu.roll(left, turn, 1), pltpu.roll(right, turn, 1)
    )


def kernel(
    inner, offset_ref, panel_ref, cauchy_ref, v_ref, out_ref,
    v_all, k_high, k_low, panels, mixing, turned, home, mid_map, mid_data, z_all, z_high, z_low, aligned, y_home,
    map_one, map_two, data_one, data_two,
    pair_m, chip_m, chips_m, layer_m, layers_m, own_b, pair_b, chip_b, chips_b, layer_b, layers_b,
    own_m, ready_v, ready_r, load_sem, ring_send, ring_sem, halo_send, halo_sem, scan_send, scan_sem,
):
    me, slabs = lax.axis_index("row"), lax.axis_size("row")
    col, cols = lax.axis_index("col"), lax.axis_size("col")
    steps = v_ref.shape[1]
    rows = panel_ref.shape[0]
    half = rows // 2
    group = 2 * inner
    outer = slabs // group
    core = lax.rem(me, 2)
    chip = lax.rem(me // 2, inner)
    layer = me // group
    right, left = lax.rem(col + 1, cols), lax.rem(col + cols - 1, cols)
    after, before = lax.rem(me + 1, slabs), lax.rem(me + slabs - 1, slabs)
    partner = me + 1 - 2 * core
    near = [layer * group + lax.rem(chip + s, inner) * 2 + core for s in range(1, inner)]
    apart = [lax.rem(me + s * group, slabs) for s in range(1, outer)]

    loads = []
    for i in range(4):
        sweep, at = i // 2, (i % 2) * (steps // 2)
        loads.append(
            pltpu.make_async_copy(
                v_ref.at[sweep, pl.ds(at, steps // 2)],
                v_all.at[pl.ds(1 + sweep * (steps + 3) + at, steps // 2)],
                load_sem.at[i],
            )
        )
    loads.append(pltpu.make_async_copy(panel_ref, panels.at[col], load_sem.at[4]))
    loads.append(pltpu.make_async_copy(cauchy_ref, mixing, load_sem.at[5]))
    head_loads = []
    for i in range(4):
        head_loads.append(
            pltpu.make_async_copy(v_ref.at[0, pl.ds(2 * i, 2)], v_all.at[pl.ds(1 + 2 * i, 2)], load_sem.at[6 + i])
        )
        head_loads[-1].start()

    barrier = pltpu.get_barrier_semaphore()
    for peer in (right, left):
        pl.semaphore_signal(barrier, inc=1, device_id={"col": peer}, device_id_type=MESH)
    sides = [near[0], near[-1]]
    greeted = [after, before, partner] + near + apart + [peer + 1 - 2 * core for peer in sides]
    for peer in greeted:
        pl.semaphore_signal(barrier, inc=1, device_id={"row": peer}, device_id_type=MESH)

    def send(source, target, send_sem, recv_sem, device):
        return pltpu.make_async_remote_copy(
            src_ref=source, dst_ref=target, send_sem=send_sem, recv_sem=recv_sem,
            device_id=device, device_id_type=MESH,
        )

    halos = [
        send(v_ref.at[0, steps - 1], v_all.at[0], halo_send.at[0], halo_sem.at[0], {"row": after}),
        send(v_ref.at[1, steps - 1], v_all.at[steps + 3], halo_send.at[1], halo_sem.at[1], {"row": after}),
        send(v_ref.at[0, pl.ds(0, 2)], v_all.at[pl.ds(steps + 1, 2)], halo_send.at[2], halo_sem.at[2], {"row": before}),
    ]

    class Ring:
        def __init__(self, source, slots, place, size, axis, peer, parts, send_sem, recv_sem, base):
            ahead, behind = lax.rem(place + 1, size), lax.rem(place + size - 1, size)
            up, down = {axis: peer(ahead)}, {axis: peer(behind)}
            one, two = parts
            sems = iter(range(base, base + 6))

            def copy(slot, part, device, own):
                i = next(sems)
                target = slots.at[(slot, *part)]
                return send(source.at[part] if own else target, target, send_sem.at[i], recv_sem.at[i], device)

            self.first = [
                copy(place, one, up, True), copy(place, two, down, True),
                copy(place, two, up, True), copy(place, one, down, True),
            ]
            self.second = [copy(behind, one, up, False), copy(ahead, two, down, False)]

        def start(self):
            for copy in self.first:
                copy.start()

        def forward(self):
            for arrived, onward in zip(self.first, self.second):
                arrived.wait_recv()
                onward.start()

        def arrive(self):
            for copy in self.first[2:] + self.second:
                copy.wait_recv()

        def finish(self):
            for copy in self.first + self.second:
                copy.wait_send()

    class SplitRing(Ring):
        def __init__(self, source, slots, place, size, axis, peer, send_sem, recv_sem, base, cross):
            at, quarter = core * (S // 2), S // 4
            parts = [(slice(None), pl.ds(pl.multiple_of(at + i * quarter, quarter), quarter)) for i in range(2)]
            super().__init__(source, slots, place, size, axis, peer, parts, send_sem, recv_sem, base)
            rows_here = pl.ds(pl.multiple_of(at, S // 2), S // 2)
            across = 1 - 2 * core
            self.swaps, self.crossed = [], []
            for i, shift in enumerate((size - 1, 1)):
                ref = slots.at[lax.rem(place + shift, size), :, rows_here]
                self.swaps.append(
                    send(ref, ref, send_sem.at[base + 6 + i], recv_sem.at[base + 6 + i], {"row": partner})
                )
                if cross:
                    ref = slots.at[(lax.rem(place + shift, size), *parts[i])]
                    other = peer(lax.rem(place + size - shift, size)) + across
                    self.crossed.append(
                        send(ref, ref, send_sem.at[base + 8 + i], recv_sem.at[base + 8 + i], {axis: other})
                    )
            if not cross:
                ref = slots.at[lax.rem(place + 2, size), :, rows_here]
                self.far = send(ref, ref, send_sem.at[base + 8], recv_sem.at[base + 8], {"row": partner})
                self.swaps.append(self.far)

        def forward(self):
            for i in range(2):
                self.first[i].wait_recv()
                self.second[i].start()
                if self.crossed:
                    self.crossed[i].start()

        def swap_near(self):
            for copy, swap in zip(self.first[2:], self.swaps):
                copy.wait_recv()
                swap.start()

        def swap_far(self):
            for copy in self.second:
                copy.wait_recv()
            self.far.start()

        def arrive(self):
            for copy in self.swaps + (self.second + self.crossed if self.crossed else []):
                copy.wait_recv()

        def finish(self):
            for copy in self.first + self.second + self.swaps + self.crossed:
                copy.wait_send()

    def only(on, act):
        if on is None:
            act()
        elif on is not False:
            pl.when(on)(act)

    z1, z2 = layer == 1, layer == 2
    upper, top_layer, bottom = layer > 1, layer == outer - 1, layer == 0

    class LayerMaps(SplitRing):
        def start(self):
            self.first, self.sent = self.first[:3], [z1 | z2, z1, z1 | z2]
            for copy, on in zip(self.first, self.sent):
                only(on, copy.start)

        def forward(self):
            only(upper, self.first[0].wait_recv)
            only(z2, self.second[0].start)

        def forward_down(self):
            only(bottom, self.first[1].wait_recv)
            only(bottom, self.second[1].start)

        def swap_near(self):
            only(upper, self.first[2].wait_recv)
            only(upper, self.swaps[0].start)

        def swap_far(self):
            for copy in self.second:
                only(top_layer, copy.wait_recv)
            only(top_layer, self.far.start)

        def arrive(self):
            only(upper, self.swaps[0].wait_recv)
            only(top_layer, self.far.wait_recv)

        def finish(self):
            for copy, on in zip(self.first, self.sent):
                only(on, copy.wait_send)
            only(z2, self.second[0].wait_send)
            only(bottom, self.second[1].wait_send)
            only(upper, self.swaps[0].wait_send)
            only(top_layer, self.far.wait_send)

    class Direct:
        def __init__(self, source, slots, place, size, axis, peer, send_sem, recv_sem, base, later):
            self.sends = [place < size - 2, place < size - 1, place == 0] if later else [None] * 3
            self.comes = [place > 1, place > 0, place == size - 1] if later else [None] * 3
            mine = pl.ds(pl.multiple_of(core * half, half), half)
            to = [{axis: peer(lax.rem(place + shift, size))} for shift in (2, 1, size - 1)]
            refs = [(source.at[mine], slots.at[place, mine])] + [(source, slots.at[place])] * 2
            self.copies = [
                send(*ref, send_sem.at[base + i], recv_sem.at[base + i], device)
                for i, (ref, device) in enumerate(zip(refs, to))
            ]
            ref = slots.at[lax.rem(place + 2, size), mine]
            self.swap = send(ref, ref, send_sem.at[base + 3], recv_sem.at[base + 3], {"row": partner})

        def start(self):
            for copy, on in zip(self.copies, self.sends):
                only(on, copy.start)

        def relay(self):
            only(self.comes[0], self.copies[0].wait_recv)
            only(self.comes[0], self.swap.start)

        def arrive(self):
            for copy, on in zip([*self.copies[1:], self.swap], [*self.comes[1:], self.comes[0]]):
                only(on, copy.wait_recv)

        def finish(self):
            for copy, on in zip([*self.copies, self.swap], [*self.sends, self.comes[0]]):
                only(on, copy.wait_send)

    flat = [(pl.ds(i * half, half),) for i in range(2)]
    width = panel_ref.shape[1] // 2
    panel_rings = []
    for i in range(2):
        parts = [(*rows_of, pl.ds(i * width, width)) for rows_of in flat]
        panel_rings.append(
            Ring(panel_ref, panels, col, cols, "col", lambda c: c, parts, ring_send, ring_sem, 6 * i)
        )
    in_layer = dict(place=chip, size=inner, axis="row", peer=lambda x: layer * group + 2 * x + core)
    over_layers = dict(place=layer, size=outer, axis="row", peer=lambda z: z * group + 2 * chip + core)

    scan_sems = dict(send_sem=scan_send, recv_sem=scan_sem)
    chip_ring_m = SplitRing(chip_m, chips_m, base=2, cross=True, **in_layer, **scan_sems)
    layer_ring_m = LayerMaps(layer_m, layers_m, base=12, cross=False, **over_layers, **scan_sems)
    chip_ring_b = Direct(chip_b, chips_b, base=22, later=False, **in_layer, **scan_sems)
    layer_ring_b = Direct(layer_b, layers_b, base=26, later=True, **over_layers, **scan_sems)

    last = slabs * steps - 3
    row = lax.broadcasted_iota(jnp.int32, (2 * S, 2 * S), 0)
    colm = lax.broadcasted_iota(jnp.int32, (2 * S, 2 * S), 1)
    eye2 = (row == colm).astype(F32)

    def is_on(slot):
        return (slot >= 0) & (slot <= last)

    def begin(batch, filler):
        stages = prepare([v_all[at] for at, _ in batch], [is_on(slot) for _, slot in batch])
        share = -(-len(filler) // 9)
        filler = list(filler)
        while True:
            try:
                next(stages)
            except StopIteration as done:
                pairs, result = done.value
                break
            for piece in filler[:share]:
                piece()
            filler = filler[share:]
        for piece in filler:
            piece()
        for i in range(len(batch)):
            ready_v[i] = pairs[i]
            ready_r[i] = result[i]

    def end(i, at):
        x = less(ready_v[i], ready_r[i])
        for r in range(2):
            for c in range(2):
                here = pl.ds(r * S, S), pl.ds(c * S, S)
                part = x[r * S : (r + 1) * S, c * S : (c + 1) * S]
                high, low = split(eye2[:S, :S] + part if r == c else part)
                k_high[(at, *here)] = high
                k_low[(at, *here)] = low

    def ends(batch):
        return [functools.partial(end, i, at) for i, (at, _) in enumerate(batch)]

    first_slot = me * steps

    def batch_of(t):
        at, slot = 1 + 8 * t + 3 * (t // (steps // 8)), first_slot + lax.rem(t, steps // 8) * 8
        return [(at + i, slot + i) for i in range(8)]

    seam = [(0, first_slot - 1), (steps + 3, first_slot - 1)]
    seam += [(steps + 1, first_slot + steps), (steps + 2, first_slot + steps + 1)]

    o_one, o_two = offset_ref[0], offset_ref[1]
    reach = S + o_two - o_one
    jump = reach // S
    by = lax.rem(reach, S)
    eye = eye2[:S, :S]
    zero = jnp.zeros((S, S), F32)
    map_one[...] = eye
    map_two[...] = jnp.concatenate([zero, eye], axis=0)
    mid_map[0] = zero

    def map_step_one(k):
        out = mul(map_one[...], k_high[k + 1, :S], k_low[k + 1, :S])
        mid_map[k + 2] = out[:, :S]
        map_one[...] = out[:, S:]

    def map_step_two(k):
        fresh = window(mid_map[k + 2 + jump], mid_map[k + 3 + jump], by)
        at = k + steps + 4
        x = jnp.concatenate([map_two[...], jnp.concatenate([fresh, zero], axis=0)], axis=1)
        out = mul(x, k_high[at], k_low[at])
        z_all[k + 1] = out[:, :S]
        map_two[...] = out[:, S:]

    def wave(k, one, two, save_one, save_two):
        if k < steps + 2:
            one(k)
        if k > 1:
            two(k - 3)
        if k == steps - 2:
            save_one()
        if k == steps + 1:
            save_two()

    def save_map_one():
        own_m[0] = map_one[...]

    def save_map_two():
        own_m[1] = map_two[:S]
        own_m[2] = map_two[S:]

    def map_waves(ks):
        return [functools.partial(wave, k, map_step_one, map_step_two, save_map_one, save_map_two) for k in ks]

    def mixed(some, others):
        out = []
        while some or others:
            out += some[:1] + others[:1]
            some, others = some[1:], others[1:]
        return out

    def enter():
        pl.semaphore_wait(barrier, 2 + len(greeted))
        for copy in halos:
            copy.start()
        panel_rings[0].start()

    for copy in head_loads:
        copy.wait()
    for copy in loads[1:]:
        copy.start()
    begin(batch_of(0), [])
    enter()
    for copy in loads[1:4]:
        copy.wait()

    def tick(t, _):
        @pl.when(t == 3)
        def _():
            panel_rings[0].forward()
            panel_rings[1].start()

        begin(batch_of(t), ends(batch_of(t - 1)))
        return 0

    lax.fori_loop(1, steps // 4, tick, 0)
    for copy in halos:
        copy.wait()
    begin(seam, ends(batch_of(steps // 4 - 1)))
    loads[5].wait()
    turned[...] = mixing[...].T
    mix_high, mix_low = split(turned[pl.ds(pl.multiple_of(col * rows, rows), rows)])
    mix = jnp.concatenate([mix_high, mix_low], axis=0)
    home[0] = jnp.zeros((rows, S), F32)

    def merge(j, _):
        at = pl.ds(pl.multiple_of(j * S, S), S)
        part = jnp.concatenate([panels[c, :, at] for c in range(cols)], axis=0)
        both = dot(mix, wide(part))
        home[j + 1] = fold(both[:rows]) + fold(both[rows:])
        return 0

    margin = send(
        home.at[pl.ds(1, 4)], home.at[pl.ds(steps + 1, 4)], halo_send.at[3], halo_sem.at[3], {"row": before}
    )

    def merge_first():
        loads[4].wait()
        panel_rings[0].arrive()
        lax.fori_loop(0, steps // 2, merge, 0, unroll=4)

        @pl.when(me == slabs - 1)
        def _():
            home[pl.ds(steps + 1, 4)] = jnp.zeros((4, rows, S), F32)


    for piece in ends(seam) + map_waves(range(-1, 9)):
        piece()
    panel_rings[1].forward()
    for piece in map_waves(range(9, steps + 2)):
        piece()
    pair = send(own_m, pair_m, scan_send.at[0], scan_sem.at[0], {"row": partner})
    pair.start()
    map_waves([steps + 2])[0]()
    merge_first()

    def matrix(ref):
        high0, low0 = split(jnp.concatenate([ref[0], ref[1]], axis=1))
        high1, low1 = split(jnp.concatenate([zero, ref[2]], axis=1))
        return jnp.concatenate([high0, high1], axis=0), jnp.concatenate([low0, low1], axis=0)

    def whole(ref):
        return jnp.concatenate(
            [jnp.concatenate([ref[0], ref[1]], axis=1), jnp.concatenate([zero, ref[2]], axis=1)], axis=0
        )

    def keep(ref, x):
        ref[0] = x[:S, :S]
        ref[1] = x[:S, S:]
        ref[2] = x[S:, S:]

    on_first = core == 0

    def pair_maps():
        pair.wait()
        first = jnp.where(on_first, whole(own_m), whole(pair_m))
        second = jnp.where(on_first, whole(pair_m), whole(own_m))
        keep(chip_m, mul(first, *split(second)))
        chip_ring_m.start()

        @pl.when(me > 0)
        def _():
            margin.start()

        chips_m[chip] = chip_m[...]

    def fresh_one(k):
        return window(home[k + 1], home[k + 2], o_one)

    is_first = me == 0
    data_one[...] = jnp.where(is_first, fresh_one(-1), 0.0)
    mid_data[0] = jnp.zeros((rows, S), F32)

    def data_step_one(k):
        x = jnp.concatenate([data_one[...], fresh_one(k + 1)], axis=1)
        out = mul(x, k_high[k + 1], k_low[k + 1])
        mid_data[k + 2] = out[:, :S]
        data_one[...] = out[:, S:]

    def fresh_two(k):
        return window(mid_data[k + 1 + jump], mid_data[k + 2 + jump], by)

    def data_step_two(k):
        carried = data_two[...] if k >= 0 else jnp.where(is_first, fresh_two(-1), 0.0)
        x = jnp.concatenate([carried, fresh_two(k + 1)], axis=1)
        out = mul(x, k_high[k + steps + 4], k_low[k + steps + 4])
        aligned[k + 1] = out[:, :S]
        data_two[...] = out[:, S:]


    def save_data_one():
        own_b[:, :S] = data_one[...]

    def save_data_two():
        own_b[:, S:] = data_two[...]

    def merge_second():
        panel_rings[1].arrive()
        lax.fori_loop(steps // 2, steps, merge, 0, unroll=True)

    def take_margin():
        @pl.when(me < slabs - 1)
        def _():
            margin.wait_recv()

    pair_two = send(own_b, pair_b, scan_send.at[1], scan_sem.at[1], {"row": partner})
    also = {
        0: pair_maps, 5: merge_second, 12: chip_ring_m.forward, steps - 2: take_margin,
        steps: chip_ring_m.swap_near,
    }
    for k in range(-1, steps + 3):
        if k in also:
            also[k]()
        wave(k, data_step_one, data_step_two, save_data_one, save_data_two)
        if k == steps + 1:
            pair_two.start()


    pair_two.wait()
    first_m = jnp.where(on_first, whole(own_m), whole(pair_m))
    second_m = jnp.where(on_first, whole(pair_m), whole(own_m))
    first_b = jnp.where(on_first, own_b[...], pair_b[...])
    second_b = jnp.where(on_first, pair_b[...], own_b[...])
    chip_b[...] = mul(first_b, *split(second_m)) + second_b
    chip_ring_b.start()
    chips_b[chip] = chip_b[...]
    chip_ring_m.arrive()
    pieces = [whole(chips_m.at[j]) for j in range(inner)]
    halves = [split(x) for x in pieces]
    early = mul(pieces[0], *halves[1])
    late = mul(pieces[2], *halves[3])
    late_parts = split(late)
    keep(layer_m, mul(early, *late_parts))
    layer_ring_m.start()
    layers_m[layer] = layer_m[...]
    lead = jnp.where(chip == 0, eye2, jnp.where(chip == 1, pieces[0], early))
    lead = jnp.where(chip == 3, mul(early, *halves[2]), lead)
    lead_m = jnp.where(on_first, lead, mul(lead, *split(first_m)))
    chip_ring_b.relay()
    layer_ring_m.forward()
    chip_ring_b.arrive()
    early_b = mul(chips_b[0], *halves[1]) + chips_b[1]
    layer_b[...] = mul(early_b, *late_parts) + (mul(chips_b[2], *halves[3]) + chips_b[3])
    layer_ring_b.start()
    layer_ring_m.forward_down()
    layers_b[layer] = layer_b[...]
    lead_b = jnp.where(chip == 0, 0.0, jnp.where(chip == 1, chips_b[0], early_b))
    lead_b = jnp.where(chip == 3, mul(early_b, *halves[2]) + chips_b[2], lead_b)
    lead_b = jnp.where(on_first, lead_b, mul(lead_b, *split(first_m)) + first_b)
    reach_out = S - o_two
    jump_out = reach_out // S
    by_out = lax.rem(reach_out, S)

    for j in range(steps):
        y_home[:, j * S : (j + 1) * S] = window(aligned[j + jump_out], aligned[j + jump_out + 1], by_out)
        z_high[j], z_low[j] = split(window(z_all[j + jump_out], z_all[j + jump_out + 1], by_out))
    layer_ring_m.swap_near()
    layer_ring_m.swap_far()
    layer_ring_b.relay()
    layer_ring_m.arrive()
    layer_ring_b.arrive()
    carry = jnp.where(layer > 0, layers_b[0], 0.0)
    for z in range(1, outer - 1):
        longer = mul(carry, *matrix(layers_m.at[z])) + layers_b[z]
        carry = jnp.where(z < layer, longer, carry)
    carry = mul(carry, *split(lead_m)) + lead_b
    for j in range(steps):
        here = slice(j * S, (j + 1) * S)
        out_ref[:, here] = y_home[:, here] + mul(carry, z_high[j], z_low[j])
    for ring in (*panel_rings, chip_ring_m, chip_ring_b, layer_ring_m, layer_ring_b):
        ring.finish()

    @pl.when(me > 0)
    def _():
        margin.wait_send()


def shards(panel, cauchy, refl_v, block_start):
    rows, width = panel.shape
    steps = refl_v.shape[1]
    cols, slabs = lax.axis_size("col"), lax.axis_size("row")
    inner = 4
    outer = slabs // (2 * inner)
    count = 2 * steps + 4
    scan_copies = 2 + 2 * 10 + 2 * 4

    def f(*shape):
        return pltpu.VMEM(shape, F32)

    def b(*shape):
        return pltpu.VMEM(shape, BF)

    dma = pltpu.SemaphoreType.DMA
    return pl.pallas_call(
        functools.partial(kernel, inner),
        in_specs=[SMEM, HBM, HBM, HBM],
        out_specs=VMEM,
        out_shape=pltpu.VMEM((rows, width), F32),
        scratch_shapes=[
            f(count, 2 * S, S), b(count, 2 * S, 2 * S), b(count, 2 * S, 2 * S),
            f(cols, rows, width), f(2 * S, 2 * S), f(2 * S, 2 * S), f(steps + 5, rows, S),
            f(steps + 5, S, S), f(steps + 5, rows, S),
            f(steps + 2, 2 * S, S), b(steps, 2 * S, S), b(steps, 2 * S, S), f(steps + 2, rows, S), f(rows, width),
            f(S, S), f(2 * S, S), f(rows, S), f(rows, S),
            f(3, S, S), f(3, S, S), f(inner, 3, S, S), f(3, S, S), f(outer, 3, S, S),
            f(rows, 2 * S), f(rows, 2 * S), f(rows, 2 * S), f(inner, rows, 2 * S),
            f(rows, 2 * S), f(outer, rows, 2 * S), f(3, S, S),
            b(8, 2 * S, 2 * S), f(8, S, S),
            dma((10,)), dma((12,)), dma((12,)), dma((4,)), dma((4,)),
            dma((scan_copies,)), dma((scan_copies,)),
        ],
        compiler_params=pltpu.CompilerParams(
            collective_id=0, has_side_effects=True, vmem_limit_bytes=60 * 2**20
        ),
        name="back_transform",
    )(block_start, panel, cauchy, refl_v)

def solution(mesh):
    placed = (P("col", "row"), P(), P(None, "row", None, None), P())
    return jax.shard_map(
        shards, mesh=mesh, in_specs=placed, out_specs=P("col", "row"), check_vma=False
    )
```
